128 devices in a mesh: slab: 16 (over x, z), chan: 8 (over y, core).
Axes of the slice: x: 4, y: 4, z: 4, core: 2. Of those that a mesh axis runs over, the one named last changes fastest.
Arguments:
- stream_speed_field: bfloat16 [3, 8, 8, 8, 65536], P(None, None, None, None, ('slab', 'chan')), may hold values from -6 to 6
- liquid_to_solid_element: int32 [65536], P(('slab', 'chan')), may hold values from 0 to 65535, as said below
- previous_panel_warmth: float32 [8, 8, 8, 16, 4096], P(None, None, None, 'chan', 'slab'), may hold values from -6 to 6
- pointwise_energy_source: float32 [8, 8, 8, 16, 4096], P(None, None, None, 'chan', 'slab'), may hold values from -6 to 6
- coked_element_flags: int32 [16, 4096], P('chan', 'slab'), may hold values from 0 to 1, as said below
- coking_thickness_plies: int32 [16, 4096], P('chan', 'slab'), may hold values from 1 to 8
Outputs:
- stepped_stream_speed: bfloat16 [3, 8, 8, 8, 65536], P(None, None, None, None, ('slab', 'chan'))
- solved_panel_warmth: float32 [8, 8, 8, 16, 4096], P(None, None, None, 'chan', 'slab')
The draws below stay inside these ranges and needn't reach their ends.
Inputs may be any that keep to these rules, and one draw needn't show every extreme that they name: `liquid_to_solid_element`: A permutation of the element numbers. Element n belongs to thermal device n // 512 (devices numbered slab first, then chan) at local position n % 512. The fluid device f holds 256 elements of thermal device f and at most 128 of each of the thermal devices f + 1, f - 1 and f + 8 (modulo the number of devices), none of any other; these three counts are the same for every f, and one of them is 128. `coked_element_flags`: at most 192 flagged elements among one thermal device's elements, and exactly 192 on some device.
All inputs are finite; a program needn't handle non-finite values.
Results may differ from the reference program's by a relative error of at most 0.005.
Values may be sent and summed in bfloat16 or wider, within the bound.
A program may use at most 128 MiB of HBM per device.

```python
import jax
import jax.numpy as jnp
import numpy as np
from jax import lax

A_DEV = 256
L_DEV = 2
ITERS = 5
E_DEV = 512
HALF = 256
CAP = 128
DEP_CAP = 192
LENGTHWISE_TOTAL = 4096
CROSSWISE_TOTAL = 16
E_TOTAL = 65536
N_SLAB = 16
N_CHAN = 8


def shuffled(seed_key):
    return jax.random.permutation(seed_key, E_DEV).astype(jnp.int32)


def draw_liquid_to_solid_element(key, part):
    device_total = N_SLAB * N_CHAN
    split_value = jax.random.randint(jax.random.fold_in(key, 1), (), 1, CAP).astype(jnp.int32)
    rotation = jax.random.randint(jax.random.fold_in(key, 2), (), 0, 3)
    triple = jnp.stack([jnp.int32(CAP), split_value, jnp.int32(CAP) - split_value])
    triple = jnp.roll(triple, rotation)
    positions = jnp.arange(E_DEV, dtype=jnp.int32)
    offset_group = (positions >= HALF).astype(jnp.int32) + (positions >= HALF + triple[0]).astype(jnp.int32) + (positions >= HALF + triple[0] + triple[1]).astype(jnp.int32)
    shift_table = jnp.array([0, 1, device_total - 1, N_CHAN], jnp.int32)
    shifts = shift_table[offset_group]
    senders = jnp.arange(device_total, dtype=jnp.int32)[:, None]
    target_dev = (senders + shifts[None, :]) % device_total
    receive_order = jax.vmap(shuffled)(jax.random.split(jax.random.fold_in(key, 3), device_total))
    send_order = jax.vmap(shuffled)(jax.random.split(jax.random.fold_in(key, 4), device_total))
    values = target_dev * E_DEV + receive_order[target_dev, positions[None, :]]
    mapping = jnp.zeros((device_total, E_DEV), jnp.int32).at[senders, send_order].set(values)
    return mapping.reshape(-1)


def draw_coked_element_flags(key, part):
    device_total = N_SLAB * N_CHAN
    counts = jax.random.randint(jax.random.fold_in(key, 21), (device_total,), E_DEV // 16, 3 * E_DEV // 16)
    busiest = jax.random.randint(jax.random.fold_in(key, 22), (), 0, device_total)
    counts = jnp.where(jnp.arange(device_total) == busiest, DEP_CAP, counts)
    ranking = jax.vmap(shuffled)(jax.random.split(jax.random.fold_in(key, 23), device_total))
    flag_grid = (ranking < counts[:, None]).astype(jnp.int32)
    flag_grid = flag_grid.reshape(N_SLAB, N_CHAN, L_DEV, A_DEV).transpose(1, 2, 0, 3)
    return flag_grid.reshape(CROSSWISE_TOTAL, LENGTHWISE_TOTAL)


def set_ends(values, stream_key, least, top_value):
    longest = values.shape.index(max(values.shape))
    spots = []
    for shift in (0, 1):
        where = [jax.random.randint(jax.random.fold_in(stream_key, axis), (), 0, length) for axis, length in enumerate(values.shape)]
        where[longest] = (where[longest] + shift) % values.shape[longest]
        spots.append(tuple(where))
    return values.at[spots[0]].set(least).at[spots[1]].set(top_value)


def steps_of(own_key, dims, cuts, smallest, top_value):
    def one(axis_at, parts):
        draws = jax.random.uniform(jax.random.fold_in(jax.random.fold_in(own_key, 6), axis_at), (parts,), jnp.float32, smallest / len(cuts), top_value / len(cuts))
        return jnp.repeat(jnp.exp(draws), dims[axis_at] // parts).reshape((-1,) + (1,) * (len(dims) - axis_at - 1))

    loudness = one(*cuts[0])
    for cut in cuts[1:]:
        loudness = loudness * one(*cut)
    return loudness


def centred(own_key, dims, width, limit, pieces=(), kind=jnp.bfloat16):
    drawn = jax.random.normal(own_key, dims, jnp.float32) * width
    if len(pieces) > 0:
        drawn = steps_of(own_key, dims, pieces, -0.22, 0.18) * drawn
    return jnp.clip(drawn, min=-limit, max=limit).astype(kind)


def setup_inputs(seed: int = 0) -> dict:
    arg_keys = jax.random.split(jax.random.key(seed), 7)
    return {
        "stream_speed_field": centred(arg_keys[0], (3, 8, 8, 8, E_TOTAL), 1.0, 6.0, ((4, 128),)),
        "liquid_to_solid_element": draw_liquid_to_solid_element(jax.random.fold_in(arg_keys[6], 71), 0),
        "previous_panel_warmth": centred(arg_keys[2], (8, 8, 8, CROSSWISE_TOTAL, LENGTHWISE_TOTAL), 1.0, 6.0, ((3, 8), (4, 16)), jnp.float32),
        "pointwise_energy_source": centred(arg_keys[3], (8, 8, 8, CROSSWISE_TOTAL, LENGTHWISE_TOTAL), 1.0, 6.0, ((3, 8), (4, 16)), jnp.float32),
        "coked_element_flags": draw_coked_element_flags(jax.random.fold_in(arg_keys[6], 71), 0),
        "coking_thickness_plies": set_ends(jax.random.randint(arg_keys[5], (CROSSWISE_TOTAL, LENGTHWISE_TOTAL), 1, 9), jax.random.fold_in(arg_keys[5], 1), 1, 8).astype(jnp.int32),
    }


highest = lax.Precision.HIGHEST
coolant_throughput = 0.05
time_step = 0.01
viscosity = 0.02
cross_gain = 0.4
layer_damp = 0.25
forward_forms = ("ir,rst...->ist...", "js,rst...->rjt...", "kt,rst...->rsk...")
backward_forms = ("ir,ist...->rst...", "js,rjt...->rst...", "kt,rsk...->rst...")
fluid_forms = ("ir,crste->ciste", "js,crste->crjte", "kt,crste->crske")


def gll_tables():
    points = np.array([-1.0, -0.8717401485096066, -0.5917001814331423, -0.2092992179024789, 0.2092992179024789, 0.5917001814331423, 0.8717401485096066, 1.0])
    weights = np.array([1.0 / 28.0, 0.2107042271435061, 0.3411226924835044, 0.4124587946587038, 0.4124587946587038, 0.3411226924835044, 0.2107042271435061, 1.0 / 28.0])
    lower_poly = np.ones(8)
    upper_poly = points.copy()
    for degree in range(1, 7):
        next_poly = ((2 * degree + 1) * points * upper_poly - degree * lower_poly) / (degree + 1)
        lower_poly = upper_poly
        upper_poly = next_poly
    gaps_matrix = points[:, None] - points[None, :] + np.eye(8)
    derivative = upper_poly[:, None] / (upper_poly[None, :] * gaps_matrix)
    derivative = derivative * (1.0 - np.eye(8))
    derivative[0, 0] = -14.0
    derivative[7, 7] = 14.0
    return jnp.asarray(derivative, jnp.float32), jnp.asarray(weights, jnp.float32)


def forward(matrix, field, conjugate_update_vector):
    return jnp.einsum(forward_forms[conjugate_update_vector], matrix, field, precision=highest)


def backward(matrix, field, conjugate_update_vector):
    return jnp.einsum(backward_forms[conjugate_update_vector], matrix, field, precision=highest)


def fluid_update(velocity_block, matrix):
    velocity_now = velocity_block.astype(jnp.float32)
    gradients = [jnp.einsum(fluid_forms[conjugate_update_vector], matrix, velocity_now, precision=highest) for conjugate_update_vector in range(3)]
    convect = velocity_now[0:1] * gradients[0] + velocity_now[1:2] * gradients[1] + velocity_now[2:3] * gradients[2]
    laplace = jnp.einsum(fluid_forms[0], matrix, gradients[0], precision=highest)
    laplace = laplace + jnp.einsum(fluid_forms[1], matrix, gradients[1], precision=highest)
    laplace = laplace + jnp.einsum(fluid_forms[2], matrix, gradients[2], precision=highest)
    updated = velocity_now + time_step * (viscosity * laplace - convect)
    return updated.astype(jnp.bfloat16)


def conductivity_of(stepped_stream_speed):
    faster = stepped_stream_speed.astype(jnp.float32)
    return (1.0 + 0.5 * (faster[0] * faster[0] + faster[1] * faster[1] + faster[2] * faster[2])).astype(jnp.bfloat16)


def local_operator(field, weighted_kappa, cross_el, matrix, integration_factor):
    gradients = [forward(matrix, field, conjugate_update_vector) for conjugate_update_vector in range(3)]
    summed = coolant_throughput * integration_factor * field
    summed = summed + backward(matrix, weighted_kappa * gradients[0], 0)
    summed = summed + backward(matrix, weighted_kappa * gradients[1], 1)
    summed = summed + backward(matrix, weighted_kappa * gradients[2], 2)
    mixed = backward(matrix, weighted_kappa * gradients[1], 0) + backward(matrix, weighted_kappa * gradients[0], 1)
    return summed + cross_el * mixed


def collect_assembled_points(field):
    shared = field[7, :, :, :, :-1] + field[0, :, :, :, 1:]
    field = field.at[7, :, :, :, :-1].set(shared).at[0, :, :, :, 1:].set(shared)
    shared = field[:, 7, :, :-1, :] + field[:, 0, :, 1:, :]
    field = field.at[:, 7, :, :-1, :].set(shared).at[:, 0, :, 1:, :].set(shared)
    return field


def multiplicity(count_l, count_a, first_l, first_a, total_l, total_a):
    node_index = jnp.arange(8, dtype=jnp.int32)
    axial_pos = first_a + jnp.arange(count_a, dtype=jnp.int32)
    lateral_pos = first_l + jnp.arange(count_l, dtype=jnp.int32)
    along_axial = 1 + ((node_index[:, None] == 0) & (axial_pos[None, :] > 0)).astype(jnp.int32) + ((node_index[:, None] == 7) & (axial_pos[None, :] < total_a - 1)).astype(jnp.int32)
    along_lateral = 1 + ((node_index[:, None] == 0) & (lateral_pos[None, :] > 0)).astype(jnp.int32) + ((node_index[:, None] == 7) & (lateral_pos[None, :] < total_l - 1)).astype(jnp.int32)
    return (along_axial[:, None, None, None, :] * along_lateral[None, :, None, :, None]).astype(jnp.float32)


def reference(stream_speed_field, liquid_to_solid_element, previous_panel_warmth, pointwise_energy_source, coked_element_flags, coking_thickness_plies):
    matrix, node_gll = gll_tables()
    integration_factor = (node_gll[:, None, None] * node_gll[None, :, None] * node_gll[None, None, :])[:, :, :, None, None]
    device_total = N_SLAB * N_CHAN
    blocks = stream_speed_field.reshape(3, 8, 8, 8, device_total, E_DEV).transpose(4, 0, 1, 2, 3, 5)

    def per_block(velocity_block):
        next_block = fluid_update(velocity_block, matrix)
        return next_block, conductivity_of(next_block)

    next_blocks, cond_blocks = lax.map(per_block, blocks)
    stepped_stream_speed = next_blocks.transpose(1, 2, 3, 4, 0, 5).reshape(3, 8, 8, 8, E_TOTAL)
    cond_flat = cond_blocks.transpose(1, 2, 3, 0, 4).reshape(512, E_TOTAL)
    moved = jnp.zeros((512, E_TOTAL), jnp.bfloat16).at[:, liquid_to_solid_element].set(cond_flat)
    moved = moved.reshape(8, 8, 8, N_SLAB, N_CHAN, L_DEV, A_DEV).transpose(0, 1, 2, 4, 5, 3, 6).reshape(8, 8, 8, CROSSWISE_TOTAL, LENGTHWISE_TOTAL)
    layer_float = coking_thickness_plies.astype(jnp.float32)
    flag_float = coked_element_flags.astype(jnp.float32)
    damping = jnp.where(coked_element_flags == 1, 1.0 / (1.0 + layer_damp * layer_float), jnp.ones_like(layer_float))
    kappa = moved.astype(jnp.float32) * damping
    weighted_kappa = integration_factor * kappa
    cross_el = cross_gain * flag_float * layer_float / (layer_float + 1.0)
    inv_mult = 1.0 / multiplicity(CROSSWISE_TOTAL, LENGTHWISE_TOTAL, 0, 0, CROSSWISE_TOTAL, LENGTHWISE_TOTAL)

    def apply_operator(field):
        return collect_assembled_points(local_operator(field, weighted_kappa, cross_el, matrix, integration_factor))

    source_vector = collect_assembled_points(integration_factor * (coolant_throughput * previous_panel_warmth + pointwise_energy_source))
    solved_panel_warmth = jnp.zeros_like(source_vector)
    residual = source_vector
    conjugate_update_vector = source_vector
    norm_now = jnp.sum(residual * residual * inv_mult)
    for number in range(ITERS):
        applied = apply_operator(conjugate_update_vector)
        conjugate_alpha_factor = norm_now / jnp.sum(conjugate_update_vector * applied * inv_mult)
        solved_panel_warmth = solved_panel_warmth + conjugate_alpha_factor * conjugate_update_vector
        residual = residual - conjugate_alpha_factor * applied
        norm_next = jnp.sum(residual * residual * inv_mult)
        conjugate_update_vector = residual + (norm_next / norm_now) * conjugate_update_vector
        norm_now = norm_next
    return stepped_stream_speed, solved_panel_warmth
```

```python
import functools

import jax
import jax.numpy as jnp
import numpy as np
from jax import lax
from jax.experimental import pallas as pl
from jax.experimental.pallas import tpu as pltpu
from jax.sharding import PartitionSpec as P

F32 = jnp.float32
BF16 = jnp.bfloat16
MESH = pl.DeviceIdType.MESH
ITERS = 5
SCALE = 64.0
NT = (((1,), (1,)), ((), ()))
NN = (((1,), (0,)), ((), ()))


def gll():
    points = np.array(
        [
            -1.0,
            -0.8717401485096066,
            -0.5917001814331423,
            -0.2092992179024789,
            0.2092992179024789,
            0.5917001814331423,
            0.8717401485096066,
            1.0,
        ]
    )
    weights = np.array(
        [
            1.0 / 28.0,
            0.2107042271435061,
            0.3411226924835044,
            0.4124587946587038,
            0.4124587946587038,
            0.3411226924835044,
            0.2107042271435061,
            1.0 / 28.0,
        ]
    )
    low = np.ones(8)
    high = points.copy()
    for degree in range(1, 7):
        low, high = high, ((2 * degree + 1) * points * high - degree * low) / (degree + 1)
    gaps = points[:, None] - points[None, :] + np.eye(8)
    deriv = high[:, None] / (high[None, :] * gaps)
    deriv = deriv * (1.0 - np.eye(8))
    deriv[0, 0] = -14.0
    deriv[7, 7] = 14.0
    return deriv, weights


def two(matrix):
    high = np.asarray(matrix, np.float32).astype(BF16).astype(np.float64)
    return high, matrix - high


def operators():
    deriv, weights = gll()
    second = deriv @ deriv
    eye = np.eye
    kron = np.kron
    along_s = kron(eye(4), kron(deriv, eye(8)))
    along_t = kron(eye(32), deriv)
    along_r = kron(deriv, eye(32))
    ds_hi, ds_lo = two(along_s)
    dt_hi, dt_lo = two(along_t)
    dr_hi, dr_lo = two(along_r)
    fwd_st = np.block([[ds_hi, ds_lo, ds_hi], [dt_hi, dt_lo, dt_hi]])
    fwd_r = np.block([[dr_hi, dr_lo, dr_hi]])
    bwd_st = np.block([[ds_hi.T, dt_hi.T, ds_lo.T, dt_lo.T, ds_hi.T, dt_hi.T]])
    bwd_r = np.block([[dr_hi.T, dr_lo.T, dr_hi.T]])
    flu_st = np.block([[ds_hi, ds_lo], [dt_hi, dt_lo]])
    flu_r = np.block([[dr_hi, dr_lo]])
    lap_st = kron(eye(4), kron(second, eye(8))) + kron(eye(32), second)
    lap_r = kron(second, eye(32))
    volume = (weights[:, None, None] * weights[None, :, None] * weights[None, None, :]).reshape(512, 1)
    cast = lambda m: jnp.asarray(np.asarray(m, np.float32).astype(BF16))
    return {
        "fwd_st": cast(fwd_st),
        "fwd_r": cast(fwd_r),
        "bwd_st": cast(bwd_st),
        "bwd_r": cast(bwd_r),
        "flu_st": cast(flu_st),
        "flu_r": cast(flu_r),
        "lap_st": cast(lap_st),
        "lap_r": cast(lap_r),
        "volume": jnp.asarray(np.broadcast_to(volume, (512, 128)), F32),
    }


def dot(a, b, dims=NN):
    return lax.dot_general(a, b, dims, preferred_element_type=F32)


def iota(shape, dim):
    return lax.broadcasted_iota(jnp.int32, shape, dim)


def fluid_kernel(
    u_ref, index_ref, flu_st, flu_r, lap_st, lap_r, out_ref, pack_ref, grad, lap, cond
):
    step = pl.program_id(0)
    lanes = u_ref.shape[2]

    def component(c, square):
        field = u_ref[pl.ds(c * 64, 64)].astype(F32)
        flat = field.reshape(512, lanes)
        low = flat.astype(BF16)
        for h in range(2):
            rows = pl.ds(256 * h, 256)
            part = low[256 * h : 256 * h + 256]
            both = dot(flu_st[...], jnp.concatenate([part, part], 0))
            grad[1, rows] = both[:256]
            grad[2, rows] = both[256:]
            lap[rows] = dot(lap_st[...], part)
        by_r = flat.reshape(8, 64, lanes)
        for q in range(2):
            part = by_r[:, 32 * q : 32 * q + 32].reshape(256, lanes).astype(BF16)
            one = dot(flu_r[...], jnp.concatenate([part, part], 0)).reshape(8, 32, lanes)
            more = dot(lap_r[...], part).reshape(8, 32, lanes)
            for r in range(8):
                rows = pl.ds(64 * r + 32 * q, 32)
                grad[0, rows] = one[r]
                lap[rows] = lap[rows] + more[r]
        u0 = u_ref[0:64].astype(F32).reshape(512, lanes)
        u1 = u_ref[64:128].astype(F32).reshape(512, lanes)
        u2 = u_ref[128:192].astype(F32).reshape(512, lanes)
        convect = u0 * grad[0] + u1 * grad[1] + u2 * grad[2]
        new = (flat + 0.01 * (0.02 * lap[...] - convect)).astype(BF16)
        new32 = new.astype(F32)
        out_ref[pl.ds(c * 64, 64)] = new32.reshape(64, 8, lanes).astype(BF16)
        return square + new32 * new32

    square = jnp.zeros((512, lanes), F32)
    for c in range(3):
        square = component(c, square)
    cond[0:512, pl.ds(pl.multiple_of(step * lanes, lanes), lanes)] = (1.0 + 0.5 * square).astype(BF16)

    @pl.when(step == pl.num_programs(0) - 1)
    def _():
        total = lax.axis_size("slab") * lax.axis_size("chan")
        chans = lax.axis_size("chan")
        me = lax.axis_index("slab") * chans + lax.axis_index("chan")
        target = index_ref[...]
        device = target >> 9
        slot = target & 511
        distance = (device - me) & (total - 1)
        group = jnp.where(
            distance == 1,
            1,
            jnp.where(distance == total - 1, 2, jnp.where(distance == chans, 3, 0)),
        )
        member = iota((8, 512), 0) == group
        before = (iota((512, 512), 0) < iota((512, 512), 1)).astype(F32).astype(BF16)
        rank = dot(member.astype(F32).astype(BF16), before)
        start = jnp.where(
            iota((8, 512), 0) == 0, 0, 128 + 128 * iota((8, 512), 0)
        ).astype(F32)
        position = jnp.sum(jnp.where(member, rank + start, 0.0), axis=0, keepdims=True).astype(jnp.int32)
        code = jnp.where(
            iota((16, 512), 0) == 0,
            (slot >> 5) + 1,
            jnp.where(iota((16, 512), 0) == 1, slot & 31, 0),
        )
        cond[512:528] = code.astype(F32).astype(BF16)
        for k in range(5):
            chosen = (iota((128, 512), 0) + 128 * k == position).astype(F32).astype(BF16)
            pack_ref[k] = dot(cond[...], chosen, NT).astype(BF16)


def fluid(u, index, ops):
    blocks = 2
    lanes = 512 // blocks
    fixed = lambda shape: pl.BlockSpec(shape, lambda i: (0,) * len(shape))
    return pl.pallas_call(
        fluid_kernel,
        grid=(blocks,),
        in_specs=[
            pl.BlockSpec((192, 8, lanes), lambda i: (0, 0, i)),
            fixed((1, 512)),
            fixed((512, 512)),
            fixed((256, 512)),
            fixed((256, 256)),
            fixed((256, 256)),
        ],
        out_specs=[
            pl.BlockSpec((192, 8, lanes), lambda i: (0, 0, i)),
            fixed((5, 528, 128)),
        ],
        out_shape=[
            jax.ShapeDtypeStruct((192, 8, 512), BF16),
            jax.ShapeDtypeStruct((5, 528, 128), BF16),
        ],
        scratch_shapes=[
            pltpu.VMEM((3, 512, lanes), F32),
            pltpu.VMEM((512, lanes), F32),
            pltpu.VMEM((528, 512), BF16),
        ],
        name="fluid",
    )(u, index, ops["flu_st"], ops["flu_r"], ops["lap_st"], ops["lap_r"])


def krylov_weights(m):
    n = ITERS
    zero = jnp.zeros_like(m[0])
    older, newer = [zero] * (2 * n), list(m)
    diag = [newer[1] / newer[0]]
    off = [zero]
    for k in range(1, n):
        fresh = [zero] * (2 * n)
        for l in range(k, 2 * n - k):
            fresh[l] = newer[l + 1] - diag[k - 1] * newer[l] - off[k - 1] * older[l]
        diag.append(fresh[k + 1] / fresh[k] - newer[k] / newer[k - 1])
        off.append(fresh[k] / newer[k - 1])
        older, newer = newer, fresh
    alpha = [1.0 / diag[0]]
    beta = []
    for k in range(1, n):
        beta.append(off[k] * alpha[k - 1] * alpha[k - 1])
        alpha.append(1.0 / (diag[k] - beta[k - 1] / alpha[k - 1]))
    one = jnp.ones_like(zero)
    res, way, sol = [one], [one], [zero] * n
    for k in range(n):
        for i in range(k + 1):
            sol[i] = sol[i] + alpha[k] * way[i]
        if k < n - 1:
            res = res + [zero]
            for i in range(k + 1):
                res[i + 1] = res[i + 1] - alpha[k] * way[i]
            way = [res[i] + (beta[k] * way[i] if i <= k else 0.0) for i in range(k + 2)]
    return sol


HALO = ((1, 0), (-1, 0), (0, 1), (0, -1), (1, 1), (1, -1), (-1, 1), (-1, -1))


def panel_kernel(
    n_slab,
    n_chan,
    pack_ref,
    prev_ref,
    source_ref,
    flag_ref,
    ply_ref,
    fwd_st,
    fwd_r,
    bwd_st,
    bwd_r,
    volume_ref,
    out_ref,
    basis,
    kap,
    inv_mult,
    grad,
    flux,
    acc,
    got_pack,
    edge_out,
    edge_in,
    side_out,
    side_in,
    chan_sum,
    slab_sum,
    pack_send,
    pack_recv,
    halo_send,
    halo_recv,
    chan_send,
    chan_recv,
    slab_send,
    slab_recv,
):
    slab = lax.axis_index("slab")
    chan = lax.axis_index("chan")
    device = slab * n_chan + chan
    devices = n_slab * n_chan

    def near(ds, dc):
        return (lax.rem(slab + ds + n_slab, n_slab), lax.rem(chan + dc + n_chan, n_chan))

    barrier = pltpu.get_barrier_semaphore()
    greet = [near(*d) for d in HALO]
    greet += [(slab, lax.rem(chan + j, n_chan)) for j in range(2, n_chan - 1)]
    greet += [(lax.rem(slab + j, n_slab), chan) for j in range(2, n_slab - 1)]
    for peer in greet:
        pl.semaphore_signal(barrier, inc=1, device_id=peer, device_id_type=MESH)

    for l in range(2):
        for h in range(2):
            lane = pl.ds(256 * l + 128 * h, 128)
            rows = pl.ds(2 * h + l, 512, stride=4)
            value = volume_ref[...] * (0.05 * prev_ref[rows, :] + source_ref[rows, :])
            basis[0, :, :, :, lane] = value.reshape(8, 8, 8, 128)
    node = iota((512, 128), 0)
    at_r = node >> 6
    at_s = (node >> 3) & 7
    for l in range(2):
        for h in range(2):
            lane = pl.ds(256 * l + 128 * h, 128)
            axial = slab * 256 + 128 * h + iota((512, 128), 1)
            m_r = jnp.where(((at_r == 0) & (axial > 0)) | ((at_r == 7) & (axial < n_slab * 256 - 1)), 0.5, 1.0)
            lateral = chan * 2 + l
            m_s = jnp.where(((at_s == 0) & (lateral > 0)) | ((at_s == 7) & (lateral < n_chan * 2 - 1)), 0.5, 1.0)
            inv_mult[:, lane] = m_r * m_s
    flag = jnp.concatenate([flag_ref[0:1], flag_ref[1:2]], 1)
    ply = jnp.concatenate([ply_ref[0:1], ply_ref[1:2]], 1).astype(F32)
    damping = jnp.where(flag == 1, 1.0 / (1.0 + 0.25 * ply), 1.0)
    cross = 0.4 * flag.astype(F32) * ply / (ply + 1.0)

    pl.semaphore_wait(barrier, len(greet))

    def device_at(step):
        number = lax.rem(device + step + devices, devices)
        return (number // n_chan, lax.rem(number, n_chan))

    moves = []
    for k, step in enumerate((1, -1, n_chan)):
        copy = pltpu.make_async_remote_copy(
            src_ref=pack_ref.at[2 + k],
            dst_ref=got_pack.at[k],
            send_sem=pack_send.at[k],
            recv_sem=pack_recv.at[k],
            device_id=device_at(step),
            device_id_type=MESH,
        )
        copy.start()
        moves.append(copy)

    lane8 = iota((8, 128), 1)
    has_left = slab > 0
    has_right = slab < n_slab - 1
    has_under = chan > 0
    has_over = chan < n_chan - 1

    def halo_copies(i):
        copies = []
        for d, (ds, dc) in enumerate(HALO):
            if ds == 0:
                k = 0 if dc == 1 else 1
                src, dst = side_out.at[i, k], side_in.at[i, k]
            else:
                src, dst = edge_out.at[i, 0 if ds == 1 else 1], edge_in.at[i, d]
            copies.append(
                pltpu.make_async_remote_copy(
                    src_ref=src,
                    dst_ref=dst,
                    send_sem=halo_send.at[i, d],
                    recv_sem=halo_recv.at[i, d],
                    device_id=near(ds, dc),
                    device_id_type=MESH,
                )
            )
        return copies

    def assemble_start(i):
        up = jnp.zeros((8, 128), F32)
        down = jnp.zeros((8, 128), F32)
        for l in range(2):
            for s in range(8):
                to = s + 8 * l
                here = lane8 == to
                last = basis[i, 7, s, :, 256 * l + 128 : 256 * l + 256]
                up = jnp.where(here, pltpu.roll(last, (to - 127) % 128, 1), up)
                first = basis[i, 0, s, :, 256 * l : 256 * l + 128]
                down = jnp.where(here, pltpu.roll(first, to, 1), down)
        edge_out[i, 0] = up
        edge_out[i, 1] = down
        copies = halo_copies(i)
        for d, (ds, dc) in enumerate(HALO):
            if ds != 0:
                copies[d].start()
        lane_a = iota((64, 256), 1)
        for l in range(2):
            lane = pl.ds(256 * l, 256)
            high = basis[i, 7, :, :, lane].reshape(64, 256)
            low = basis[i, 0, :, :, lane].reshape(64, 256)
            basis[i, 7, :, :, lane] = (
                high + jnp.where(lane_a == 255, 0.0, pltpu.roll(low, 255, 1))
            ).reshape(8, 8, 256)
            basis[i, 0, :, :, lane] = (
                low + jnp.where(lane_a == 0, 0.0, pltpu.roll(high, 1, 1))
            ).reshape(8, 8, 256)
        side_out[i, 0] = basis[i, :, 7, :, 256:512]
        side_out[i, 1] = basis[i, :, 0, :, 0:256]
        for d, (ds, dc) in enumerate(HALO):
            if ds == 0:
                copies[d].start()
        both = basis[i, :, 7, :, 0:256] + basis[i, :, 0, :, 256:512]
        basis[i, :, 7, :, 0:256] = both
        basis[i, :, 0, :, 256:512] = both

    def assemble_end(i):
        copies = halo_copies(i)
        for copy in copies:
            copy.wait()
        from_left = edge_in[i, 0]
        from_right = edge_in[i, 1]
        first = lane8 == 0
        last = lane8 == 127
        for l in range(2):
            for s in range(8):
                at = s + 8 * l
                lane0 = pl.ds(256 * l, 128)
                lane1 = pl.ds(256 * l + 128, 128)
                basis[i, 0, s, :, lane0] += jnp.where(
                    first & has_left, pltpu.roll(from_left, (128 - at) % 128, 1), 0.0
                )
                basis[i, 7, s, :, lane1] += jnp.where(
                    last & has_right, pltpu.roll(from_right, (127 - at) % 128, 1), 0.0
                )
        for k, (has, dc, at, s, l) in enumerate(
            ((has_under, 1, 15, 0, 0), (has_over, -1, 0, 7, 1))
        ):
            lane0 = pl.ds(256 * l, 128)
            lane1 = pl.ds(256 * l + 128, 128)
            face = side_in[i, k]
            basis[i, :, s, :, 256 * l : 256 * l + 256] += jnp.where(has, face, 0.0)
            left = edge_in[i, HALO.index((1, dc))]
            right = edge_in[i, HALO.index((-1, dc))]
            basis[i, 0, s, :, lane0] += jnp.where(
                first & has_left & has, pltpu.roll(left, (128 - at) % 128, 1), 0.0
            )
            basis[i, 7, s, :, lane1] += jnp.where(
                last & has_right & has, pltpu.roll(right, (127 - at) % 128, 1), 0.0
            )

    assemble_start(0)

    def place(slots, block):
        code = block[512:528].astype(F32)
        slot = ((code[0:1] - 1.0) * 32.0 + code[1:2]).astype(jnp.int32)
        chosen = (iota((512, 128), 0) == slot).astype(F32).astype(BF16)
        value = dot(block[0:512], chosen, NT)
        return value if slots is None else slots + value

    moved = place(place(None, pack_ref[0]), pack_ref[1])
    for k in range(3):
        moves[k].wait()
        moved = place(moved, got_pack[k])
    for h in range(4):
        lane = pl.ds(128 * h, 128)
        kap[:, lane] = (
            volume_ref[...] * (1.0 / SCALE) * moved[:, 128 * h : 128 * h + 128] * damping[:, 128 * h : 128 * h + 128]
        )

    assemble_end(0)

    def cut(x):
        high = x.astype(BF16)
        return high, (x - high.astype(F32)).astype(BF16)

    def gradient(i, lane):
        for h in range(2):
            field = basis[i, 4 * h : 4 * h + 4, :, :, lane].reshape(256, 256)
            high, low = cut(field)
            both = dot(fwd_st[...], jnp.concatenate([high, high, low], 0))
            grad[1, pl.ds(256 * h, 256)] = both[:256]
            grad[2, pl.ds(256 * h, 256)] = both[256:]
        for q in range(2):
            field = basis[i, :, 4 * q : 4 * q + 4, :, lane].reshape(256, 256)
            high, low = cut(field)
            one = dot(fwd_r[...], jnp.concatenate([high, high, low], 0)).reshape(8, 32, 256)
            for r in range(8):
                grad[0, pl.ds(64 * r + 32 * q, 32)] = one[r]

    def fold(x):
        total = jnp.sum(x.reshape(64, 8, 256), axis=0)
        return total[:, :128] + total[:, 128:]

    acc[...] = jnp.zeros_like(acc)

    def norm(i, block):
        lane = pl.ds(256 * block, 256)
        field = basis[i, :, :, :, lane].reshape(512, 256)
        acc[2 * i] += fold(field * field * inv_mult[:, lane])

    def volume2():
        v = volume_ref[...] * (0.05 / SCALE)
        return jnp.concatenate([v, v], 1)

    def power(i):
        for block in range(2):
            lane = pl.ds(256 * block, 256)
            gradient(i, lane)
            mix = cross[:, 256 * block : 256 * block + 256]
            k = kap[:, lane]
            k1 = k * grad[0]
            k2 = k * grad[1]
            flux[0] = k1 + mix * k2
            flux[1] = k2 + mix * k1
            flux[2] = k * grad[2]
            for h in range(2):
                rows = pl.ds(256 * h, 256)
                h2, l2 = cut(flux[1, rows])
                h3, l3 = cut(flux[2, rows])
                grad[0, rows] = dot(bwd_st[...], jnp.concatenate([h2, h3, h2, h3, l2, l3], 0))
            for q in range(2):
                part = jnp.concatenate([flux[0, pl.ds(64 * r + 32 * q, 32)] for r in range(8)], 0)
                high, low = cut(part)
                one = dot(bwd_r[...], jnp.concatenate([high, high, low], 0)).reshape(8, 32, 256)
                for r in range(8):
                    rows = pl.ds(64 * r + 32 * q, 32)
                    grad[0, rows] = grad[0, rows] + one[r]
            field = basis[i, :, :, :, lane].reshape(512, 256)
            value = grad[0] + volume2() * field
            basis[i + 1, :, :, :, lane] = value.reshape(8, 8, 8, 256)
            acc[2 * i + 1] += fold(value * field)

    def body(i, carry):
        power(i)
        assemble_start(i + 1)
        for block in range(2):
            norm(i, block)
        assemble_end(i + 1)
        return carry

    lax.fori_loop(0, ITERS - 1, body, 0)

    final = ITERS - 1
    for block in range(2):
        lane = pl.ds(256 * block, 256)
        norm(final, block)
        gradient(final, lane)
        mix = cross[:, 256 * block : 256 * block + 256]
        g1, g2, g3 = grad[0], grad[1], grad[2]
        field = basis[final, :, :, :, lane].reshape(512, 256)
        energy = kap[:, lane] * (g1 * g1 + g2 * g2 + g3 * g3 + 2.0 * mix * (g1 * g2))
        acc[2 * final + 1] += fold(energy + volume2() * (field * field))

    rows = jnp.concatenate([jnp.sum(acc[k], axis=0, keepdims=True) for k in range(16)], 0)
    mine = jnp.sum(rows, axis=1, keepdims=True)
    message = jnp.sum(jnp.where(iota((16, 128), 0) == iota((16, 128), 1), mine, 0.0), axis=0, keepdims=True)
    chan_sum[chan] = message
    copies = []
    for j in range(1, n_chan):
        copies.append(
            pltpu.make_async_remote_copy(
                src_ref=chan_sum.at[chan],
                dst_ref=chan_sum.at[chan],
                send_sem=chan_send.at[j],
                recv_sem=chan_recv.at[j],
                device_id=(slab, lax.rem(chan + j, n_chan)),
                device_id_type=MESH,
            )
        )
    for copy in copies:
        copy.start()
    for copy in copies:
        copy.wait()
    message = chan_sum[0]
    for j in range(1, n_chan):
        message = message + chan_sum[j]
    slab_sum[slab] = message
    copies = []
    for j in range(1, n_slab):
        copies.append(
            pltpu.make_async_remote_copy(
                src_ref=slab_sum.at[slab],
                dst_ref=slab_sum.at[slab],
                send_sem=slab_send.at[j],
                recv_sem=slab_recv.at[j],
                device_id=(lax.rem(slab + j, n_slab), chan),
                device_id_type=MESH,
            )
        )
    for copy in copies:
        copy.start()
    for copy in copies:
        copy.wait()
    message = slab_sum[0]
    for j in range(1, n_slab):
        message = message + slab_sum[j]
    lane1 = iota((1, 128), 1)
    moment = [
        jnp.sum(jnp.where(lane1 == k, message, 0.0), axis=1, keepdims=True) for k in range(2 * ITERS)
    ]
    weight = [w * (1.0 / SCALE) for w in krylov_weights(moment)]
    for l in range(2):
        for h in range(2):
            lane = pl.ds(256 * l + 128 * h, 128)
            total = weight[0] * basis[0, :, :, :, lane].reshape(512, 128)
            for i in range(1, ITERS):
                total = total + weight[i] * basis[i, :, :, :, lane].reshape(512, 128)
            out_ref[pl.ds(2 * h + l, 512, stride=4), :] = total


def panel(pack, prev, source, flags, plies, ops):
    n_slab, n_chan = lax.axis_size("slab"), lax.axis_size("chan")
    vmem = pl.BlockSpec(memory_space=pltpu.VMEM)
    dma = pltpu.SemaphoreType.DMA
    return pl.pallas_call(
        functools.partial(panel_kernel, n_slab, n_chan),
        in_specs=[vmem] * 10,
        out_specs=vmem,
        out_shape=jax.ShapeDtypeStruct((2048, 128), F32),
        scratch_shapes=[
            pltpu.VMEM((ITERS, 8, 8, 8, 512), F32),
            pltpu.VMEM((512, 512), F32),
            pltpu.VMEM((512, 512), F32),
            pltpu.VMEM((3, 512, 256), F32),
            pltpu.VMEM((3, 512, 256), F32),
            pltpu.VMEM((16, 8, 128), F32),
            pltpu.VMEM((3, 528, 128), BF16),
            pltpu.VMEM((ITERS, 2, 8, 128), F32),
            pltpu.VMEM((ITERS, 8, 8, 128), F32),
            pltpu.VMEM((ITERS, 2, 8, 8, 256), F32),
            pltpu.VMEM((ITERS, 2, 8, 8, 256), F32),
            pltpu.VMEM((n_chan, 1, 128), F32),
            pltpu.VMEM((n_slab, 1, 128), F32),
            dma((3,)),
            dma((3,)),
            dma((ITERS, 8)),
            dma((ITERS, 8)),
            dma((n_chan,)),
            dma((n_chan,)),
            dma((n_slab,)),
            dma((n_slab,)),
        ],
        compiler_params=pltpu.CompilerParams(collective_id=0, has_side_effects=True),
        name="panel",
    )(
        pack,
        prev,
        source,
        flags,
        plies,
        ops["fwd_st"],
        ops["fwd_r"],
        ops["bwd_st"],
        ops["bwd_r"],
        ops["volume"],
    )


def lanes_first(x):
    return x.reshape(512, 2, 2, 128).transpose(0, 2, 1, 3).reshape(2048, 128)


def on_device(u, index, prev, source, flags, plies):
    ops = operators()
    stepped, pack = fluid(u.reshape(192, 8, 512), index.reshape(1, 512), ops)
    warmth = panel(pack, lanes_first(prev), lanes_first(source), flags, plies, ops)
    warmth = warmth.reshape(512, 2, 2, 128).transpose(0, 2, 1, 3).reshape(8, 8, 8, 2, 256)
    return stepped.reshape(3, 8, 8, 8, 512), warmth


def solution(mesh):
    in_specs = (
        P(None, None, None, None, ("slab", "chan")),
        P(("slab", "chan")),
        P(None, None, None, "chan", "slab"),
        P(None, None, None, "chan", "slab"),
        P("chan", "slab"),
        P("chan", "slab"),
    )
    out_specs = (P(None, None, None, None, ("slab", "chan")), P(None, None, None, "chan", "slab"))
    return jax.shard_map(
        on_device, mesh=mesh, in_specs=in_specs, out_specs=out_specs, check_vma=False
    )
```

```python
import functools

import jax
import jax.numpy as jnp
import numpy as np
from jax import lax
from jax.experimental import pallas as pl
from jax.experimental.pallas import tpu as pltpu
from jax.sharding import PartitionSpec as P

F32 = jnp.float32
BF16 = jnp.bfloat16
MESH = pl.DeviceIdType.MESH
ITERS = 5
SCALE = 64.0
NT = (((1,), (1,)), ((), ()))
NN = (((1,), (0,)), ((), ()))


def gll():
    points = np.array(
        [
            -1.0,
            -0.8717401485096066,
            -0.5917001814331423,
            -0.2092992179024789,
            0.2092992179024789,
            0.5917001814331423,
            0.8717401485096066,
            1.0,
        ]
    )
    weights = np.array(
        [
            1.0 / 28.0,
            0.2107042271435061,
            0.3411226924835044,
            0.4124587946587038,
            0.4124587946587038,
            0.3411226924835044,
            0.2107042271435061,
            1.0 / 28.0,
        ]
    )
    low = np.ones(8)
    high = points.copy()
    for degree in range(1, 7):
        low, high = high, ((2 * degree + 1) * points * high - degree * low) / (degree + 1)
    gaps = points[:, None] - points[None, :] + np.eye(8)
    deriv = high[:, None] / (high[None, :] * gaps)
    deriv = deriv * (1.0 - np.eye(8))
    deriv[0, 0] = -14.0
    deriv[7, 7] = 14.0
    return deriv, weights


def two(matrix):
    high = np.asarray(matrix, np.float32).astype(BF16).astype(np.float64)
    return high, matrix - high


def operators():
    deriv, weights = gll()
    second = deriv @ deriv
    eye = np.eye
    kron = np.kron
    along_s = kron(eye(4), kron(deriv, eye(8)))
    along_t = kron(eye(32), deriv)
    along_r = kron(deriv, eye(32))
    ds_hi, ds_lo = two(along_s)
    dt_hi, dt_lo = two(along_t)
    forward = np.block([[ds_hi, ds_lo], [dt_hi, dt_lo]])
    backward = np.block([[ds_hi.T, dt_hi.T, ds_lo.T, dt_lo.T]])
    lap_st = kron(eye(4), kron(second, eye(8))) + kron(eye(32), second)
    both_r = np.block([[along_r], [kron(second, eye(32))]])
    volume = (weights[:, None, None] * weights[None, :, None] * weights[None, None, :]).reshape(512, 1)
    cast = lambda m: jnp.asarray(np.asarray(m, np.float32).astype(BF16))
    return {
        "forward": cast(forward),
        "backward": cast(backward),
        "lap_st": cast(lap_st),
        "both_r": cast(both_r),
        "volume": jnp.asarray(np.broadcast_to(volume, (512, 128)), F32),
    }


def dot(a, b, dims=NN):
    return lax.dot_general(a, b, dims, preferred_element_type=F32)


def iota(shape, dim):
    return lax.broadcasted_iota(jnp.int32, shape, dim)


def fluid_kernel(u_ref, index_ref, grad_st, lap_st, both_r, out_ref, pack_ref, grad, lap, cond):
    step = pl.program_id(0)
    lanes = u_ref.shape[2]

    def component(c, square):
        field = u_ref[pl.ds(c * 64, 64)].astype(F32)
        flat = field.reshape(512, lanes)
        low = flat.astype(BF16)
        for h in range(2):
            rows = pl.ds(256 * h, 256)
            part = low[256 * h : 256 * h + 256]
            both = dot(grad_st[...], part)
            grad[1, rows] = both[:256]
            grad[2, rows] = both[256:]
            lap[rows] = dot(lap_st[...], part)
        by_r = flat.reshape(8, 64, lanes)
        for q in range(2):
            part = by_r[:, 32 * q : 32 * q + 32].reshape(256, lanes).astype(BF16)
            both = dot(both_r[...], part).reshape(16, 32, lanes)
            for r in range(8):
                rows = pl.ds(64 * r + 32 * q, 32)
                grad[0, rows] = both[r]
                lap[rows] = lap[rows] + both[8 + r]
        u0 = u_ref[0:64].astype(F32).reshape(512, lanes)
        u1 = u_ref[64:128].astype(F32).reshape(512, lanes)
        u2 = u_ref[128:192].astype(F32).reshape(512, lanes)
        convect = u0 * grad[0] + u1 * grad[1] + u2 * grad[2]
        new = (flat + 0.01 * (0.02 * lap[...] - convect)).astype(BF16)
        new32 = new.astype(F32)
        out_ref[pl.ds(c * 64, 64)] = new32.reshape(64, 8, lanes).astype(BF16)
        return square + new32 * new32

    square = jnp.zeros((512, lanes), F32)
    for c in range(3):
        square = component(c, square)
    cond[0:512, pl.ds(pl.multiple_of(step * lanes, lanes), lanes)] = (1.0 + 0.5 * square).astype(BF16)

    @pl.when(step == pl.num_programs(0) - 1)
    def _():
        total = lax.axis_size("slab") * lax.axis_size("chan")
        chans = lax.axis_size("chan")
        me = lax.axis_index("slab") * chans + lax.axis_index("chan")
        target = index_ref[...]
        device = target >> 9
        slot = target & 511
        distance = (device - me) & (total - 1)
        group = jnp.where(
            distance == 1,
            1,
            jnp.where(distance == total - 1, 2, jnp.where(distance == chans, 3, 0)),
        )
        member = iota((8, 512), 0) == group
        before = (iota((512, 512), 0) < iota((512, 512), 1)).astype(F32).astype(BF16)
        rank = dot(member.astype(F32).astype(BF16), before)
        start = jnp.where(
            iota((8, 512), 0) == 0, 0, 128 + 128 * iota((8, 512), 0)
        ).astype(F32)
        position = jnp.sum(jnp.where(member, rank + start, 0.0), axis=0, keepdims=True).astype(jnp.int32)
        code = jnp.where(
            iota((16, 512), 0) == 0,
            (slot >> 5) + 1,
            jnp.where(iota((16, 512), 0) == 1, slot & 31, 0),
        )
        cond[512:528] = code.astype(F32).astype(BF16)
        for k in range(5):
            chosen = (iota((128, 512), 0) + 128 * k == position).astype(F32).astype(BF16)
            pack_ref[k] = dot(cond[...], chosen, NT).astype(BF16)


def fluid(u, index, ops):
    blocks = 2
    lanes = 512 // blocks
    fixed = lambda shape: pl.BlockSpec(shape, lambda i: (0,) * len(shape))
    return pl.pallas_call(
        fluid_kernel,
        grid=(blocks,),
        in_specs=[
            pl.BlockSpec((192, 8, lanes), lambda i: (0, 0, i)),
            fixed((1, 512)),
            fixed((512, 256)),
            fixed((256, 256)),
            fixed((512, 256)),
        ],
        out_specs=[
            pl.BlockSpec((192, 8, lanes), lambda i: (0, 0, i)),
            fixed((5, 528, 128)),
        ],
        out_shape=[
            jax.ShapeDtypeStruct((192, 8, 512), BF16),
            jax.ShapeDtypeStruct((5, 528, 128), BF16),
        ],
        scratch_shapes=[
            pltpu.VMEM((3, 512, lanes), F32),
            pltpu.VMEM((512, lanes), F32),
            pltpu.VMEM((528, 512), BF16),
        ],
        name="fluid",
    )(u, index, ops["forward"], ops["lap_st"], ops["both_r"])


def krylov_weights(m):
    n = ITERS
    zero = jnp.zeros_like(m[0])
    older, newer = [zero] * (2 * n), list(m)
    diag = [newer[1] / newer[0]]
    off = [zero]
    for k in range(1, n):
        fresh = [zero] * (2 * n)
        for l in range(k, 2 * n - k):
            fresh[l] = newer[l + 1] - diag[k - 1] * newer[l] - off[k - 1] * older[l]
        diag.append(fresh[k + 1] / fresh[k] - newer[k] / newer[k - 1])
        off.append(fresh[k] / newer[k - 1])
        older, newer = newer, fresh
    alpha = [1.0 / diag[0]]
    beta = []
    for k in range(1, n):
        beta.append(off[k] * alpha[k - 1] * alpha[k - 1])
        alpha.append(1.0 / (diag[k] - beta[k - 1] / alpha[k - 1]))
    one = jnp.ones_like(zero)
    res, way, sol = [one], [one], [zero] * n
    for k in range(n):
        for i in range(k + 1):
            sol[i] = sol[i] + alpha[k] * way[i]
        if k < n - 1:
            res = res + [zero]
            for i in range(k + 1):
                res[i + 1] = res[i + 1] - alpha[k] * way[i]
            way = [res[i] + (beta[k] * way[i] if i <= k else 0.0) for i in range(k + 2)]
    return sol


HALO = ((1, 0), (-1, 0), (0, 1), (0, -1), (1, 1), (1, -1), (-1, 1), (-1, -1))


def panel_kernel(
    n_slab,
    n_chan,
    pack_ref,
    prev_hbm,
    source_hbm,
    flag_hbm,
    ply_hbm,
    forward_ref,
    backward_ref,
    volume_hbm,
    out_ref,
    basis,
    kap,
    inv_mult,
    grad,
    flux,
    acc,
    got_pack,
    edge_out,
    edge_in,
    side_out,
    side_in,
    chan_sum,
    slab_sum,
    prev_ref,
    source_ref,
    volume_ref,
    flag_ref,
    ply_ref,
    own_pack,
    fwd_st,
    bwd_st,
    load_sem,
    pack_send,
    pack_recv,
    halo_send,
    halo_recv,
    chan_send,
    chan_recv,
    slab_send,
    slab_recv,
):
    slab = lax.axis_index("slab")
    chan = lax.axis_index("chan")
    device = slab * n_chan + chan
    devices = n_slab * n_chan

    def near(ds, dc):
        return (lax.rem(slab + ds + n_slab, n_slab), lax.rem(chan + dc + n_chan, n_chan))

    barrier = pltpu.get_barrier_semaphore()
    greet = [near(*d) for d in HALO]
    greet += [(slab, lax.rem(chan + j, n_chan)) for j in range(2, n_chan - 1)]
    greet += [(lax.rem(slab + j, n_slab), chan) for j in range(2, n_slab - 1)]
    for peer in greet:
        pl.semaphore_signal(barrier, inc=1, device_id=peer, device_id_type=MESH)

    loads = [
        pltpu.make_async_copy(src, dst, load_sem.at[k])
        for k, (src, dst) in enumerate(
            (
                (prev_hbm, prev_ref),
                (source_hbm, source_ref),
                (volume_hbm, volume_ref),
                (flag_hbm, flag_ref),
                (ply_hbm, ply_ref),
                (pack_ref.at[pl.ds(0, 2)], own_pack),
                (forward_ref, fwd_st.at[:, pl.ds(0, 512)]),
                (forward_ref.at[:, pl.ds(0, 256)], fwd_st.at[:, pl.ds(512, 256)]),
                (backward_ref, bwd_st.at[:, pl.ds(0, 1024)]),
                (backward_ref.at[:, pl.ds(0, 512)], bwd_st.at[:, pl.ds(1024, 512)]),
            )
        )
    ]
    for load in loads:
        load.start()
    for load in loads[:5]:
        load.wait()

    for l in range(2):
        for h in range(2):
            lane = pl.ds(256 * l + 128 * h, 128)
            rows = pl.ds(2 * h + l, 512, stride=4)
            value = volume_ref[...] * (0.05 * prev_ref[rows, :] + source_ref[rows, :])
            basis[0, :, :, :, lane] = value.reshape(8, 8, 8, 128)
    node = iota((512, 128), 0)
    at_r = node >> 6
    at_s = (node >> 3) & 7
    for l in range(2):
        for h in range(2):
            lane = pl.ds(256 * l + 128 * h, 128)
            axial = slab * 256 + 128 * h + iota((512, 128), 1)
            m_r = jnp.where(((at_r == 0) & (axial > 0)) | ((at_r == 7) & (axial < n_slab * 256 - 1)), 0.5, 1.0)
            lateral = chan * 2 + l
            m_s = jnp.where(((at_s == 0) & (lateral > 0)) | ((at_s == 7) & (lateral < n_chan * 2 - 1)), 0.5, 1.0)
            inv_mult[:, lane] = m_r * m_s
    flag = jnp.concatenate([flag_ref[0:1], flag_ref[1:2]], 1)
    ply = jnp.concatenate([ply_ref[0:1], ply_ref[1:2]], 1).astype(F32)
    damping = jnp.where(flag == 1, 1.0 / (1.0 + 0.25 * ply), 1.0)
    cross = 0.4 * flag.astype(F32) * ply / (ply + 1.0)

    lane8 = iota((8, 128), 1)
    has_left = slab > 0
    has_right = slab < n_slab - 1
    has_under = chan > 0
    has_over = chan < n_chan - 1

    has_next = {(1, 0): has_right, (-1, 0): has_left, (0, 1): has_over, (0, -1): has_under}

    def both_of(ds, dc):
        if ds == 0 or dc == 0:
            return has_next[ds, dc]
        return has_next[ds, 0] & has_next[0, dc]

    def halo_copies(i):
        copies = []
        for d, (ds, dc) in enumerate(HALO):
            if ds == 0:
                k = 0 if dc == 1 else 1
                src, dst = side_out.at[i, k], side_in.at[i, k]
            else:
                src, dst = edge_out.at[i, 0 if ds == 1 else 1], edge_in.at[i, d]
            copies.append(
                pltpu.make_async_remote_copy(
                    src_ref=src,
                    dst_ref=dst,
                    send_sem=halo_send.at[i, d],
                    recv_sem=halo_recv.at[i, d],
                    device_id=near(ds, dc),
                    device_id_type=MESH,
                )
            )
        return copies

    def assemble_start(i):
        up = jnp.zeros((8, 128), F32)
        down = jnp.zeros((8, 128), F32)
        for l in range(2):
            for s in range(8):
                to = s + 8 * l
                here = lane8 == to
                last = basis[i, 7, s, :, 256 * l + 128 : 256 * l + 256]
                up = jnp.where(here, pltpu.roll(last, (to - 127) % 128, 1), up)
                first = basis[i, 0, s, :, 256 * l : 256 * l + 128]
                down = jnp.where(here, pltpu.roll(first, to, 1), down)
        edge_out[i, 0] = up
        edge_out[i, 1] = down
        copies = halo_copies(i)
        for d, (ds, dc) in enumerate(HALO):
            if ds != 0:
                pl.when(both_of(ds, dc))(copies[d].start)
        lane_a = iota((64, 256), 1)
        for l in range(2):
            lane = pl.ds(256 * l, 256)
            high = basis[i, 7, :, :, lane].reshape(64, 256)
            low = basis[i, 0, :, :, lane].reshape(64, 256)
            basis[i, 7, :, :, lane] = (
                high + jnp.where(lane_a == 255, 0.0, pltpu.roll(low, 255, 1))
            ).reshape(8, 8, 256)
            basis[i, 0, :, :, lane] = (
                low + jnp.where(lane_a == 0, 0.0, pltpu.roll(high, 1, 1))
            ).reshape(8, 8, 256)
        side_out[i, 0] = basis[i, :, 7, :, 256:512]
        side_out[i, 1] = basis[i, :, 0, :, 0:256]
        for d, (ds, dc) in enumerate(HALO):
            if ds == 0:
                pl.when(both_of(ds, dc))(copies[d].start)
        both = basis[i, :, 7, :, 0:256] + basis[i, :, 0, :, 256:512]
        basis[i, :, 7, :, 0:256] = both
        basis[i, :, 0, :, 256:512] = both

    def assemble_end(i):
        copies = halo_copies(i)
        for d, (ds, dc) in enumerate(HALO):
            pl.when(both_of(ds, dc))(copies[d].wait_send)
            pl.when(both_of(-ds, -dc))(copies[d].wait_recv)
        from_left = edge_in[i, 0]
        from_right = edge_in[i, 1]
        first = lane8 == 0
        last = lane8 == 127
        for l in range(2):
            for s in range(8):
                at = s + 8 * l
                lane0 = pl.ds(256 * l, 128)
                lane1 = pl.ds(256 * l + 128, 128)
                basis[i, 0, s, :, lane0] += jnp.where(
                    first & has_left, pltpu.roll(from_left, (128 - at) % 128, 1), 0.0
                )
                basis[i, 7, s, :, lane1] += jnp.where(
                    last & has_right, pltpu.roll(from_right, (127 - at) % 128, 1), 0.0
                )
        for k, (has, dc, at, s, l) in enumerate(
            ((has_under, 1, 15, 0, 0), (has_over, -1, 0, 7, 1))
        ):
            lane0 = pl.ds(256 * l, 128)
            lane1 = pl.ds(256 * l + 128, 128)
            face = side_in[i, k]
            basis[i, :, s, :, 256 * l : 256 * l + 256] += jnp.where(has, face, 0.0)
            left = edge_in[i, HALO.index((1, dc))]
            right = edge_in[i, HALO.index((-1, dc))]
            basis[i, 0, s, :, lane0] += jnp.where(
                first & has_left & has, pltpu.roll(left, (128 - at) % 128, 1), 0.0
            )
            basis[i, 7, s, :, lane1] += jnp.where(
                last & has_right & has, pltpu.roll(right, (127 - at) % 128, 1), 0.0
            )

    pl.semaphore_wait(barrier, len(greet))
    assemble_start(0)

    def device_at(step):
        number = lax.rem(device + step + devices, devices)
        return (number // n_chan, lax.rem(number, n_chan))

    moves = []
    for k, step in enumerate((1, -1, n_chan)):
        copy = pltpu.make_async_remote_copy(
            src_ref=pack_ref.at[2 + k],
            dst_ref=got_pack.at[k],
            send_sem=pack_send.at[k],
            recv_sem=pack_recv.at[k],
            device_id=device_at(step),
            device_id_type=MESH,
        )
        copy.start()
        moves.append(copy)

    def place(slots, block):
        code = block[512:528].astype(F32)
        slot = ((code[0:1] - 1.0) * 32.0 + code[1:2]).astype(jnp.int32)
        chosen = (iota((512, 128), 0) == slot).astype(F32).astype(BF16)
        value = dot(block[0:512], chosen, NT)
        return value if slots is None else slots + value

    loads[5].wait()
    kap[...] = place(place(None, own_pack[0]), own_pack[1])

    def cut(x):
        high = x.astype(BF16)
        return high, (x - high.astype(F32)).astype(BF16)

    def along_r(matrix, v):
        even = [v[k] + v[7 - k] for k in range(4)]
        odd = [v[k] - v[7 - k] for k in range(4)]
        first, last = [], []
        for i in range(4):
            same = [0.5 * float(matrix[i, k] + matrix[i, 7 - k]) for k in range(4)]
            flip = [0.5 * float(matrix[i, k] - matrix[i, 7 - k]) for k in range(4)]
            p = (same[0] * even[0] + same[1] * even[1]) + (same[2] * even[2] + same[3] * even[3])
            q = (flip[0] * odd[0] + flip[1] * odd[1]) + (flip[2] * odd[2] + flip[3] * odd[3])
            first.append(p + q)
            last.append(q - p)
        return first + last[::-1]

    deriv = gll()[0]

    def gradient(i):
        for block in range(2):
            lane = pl.ds(256 * block, 256)
            for h in range(2):
                field = basis[i, 4 * h : 4 * h + 4, :, :, lane].reshape(256, 256)
                high, low = cut(field)
                both = dot(fwd_st[...], jnp.concatenate([high, high, low], 0))
                grad[1, pl.ds(256 * h, 256), lane] = both[:256]
                grad[2, pl.ds(256 * h, 256), lane] = both[256:]
            for s in range(8):
                for tile in range(2):
                    part = pl.ds(256 * block + 128 * tile, 128)
                    out = along_r(deriv, [basis[i, r, s, :, part] for r in range(8)])
                    for r in range(8):
                        grad[0, pl.ds(64 * r + 8 * s, 8), part] = out[r]

    assemble_end(0)
    for load in loads[6:]:
        load.wait()
    gradient(0)

    for k in range(3):
        moves[k].wait()
        kap[...] = place(kap[...], got_pack[k])
    for h in range(4):
        lane = pl.ds(128 * h, 128)
        kap[:, lane] = volume_ref[...] * (1.0 / SCALE) * kap[:, lane] * damping[:, 128 * h : 128 * h + 128]

    def fold(x):
        total = jnp.sum(x.reshape(x.shape[0] // 8, 8, 256), axis=0)
        return total[:, :128] + total[:, 128:]

    acc[...] = jnp.zeros_like(acc)

    def norm(i, block):
        lane = pl.ds(256 * block, 256)
        field = basis[i, :, :, :, lane].reshape(512, 256)
        acc[2 * i] += fold(field * field * inv_mult[:, lane])

    def power(i):
        for block in range(2):
            lane = pl.ds(256 * block, 256)
            mix = cross[:, 256 * block : 256 * block + 256]
            k = kap[:, lane]
            k1 = k * grad[0, :, lane]
            k2 = k * grad[1, :, lane]
            flux[0] = k1 + mix * k2
            flux[1] = k2 + mix * k1
            flux[2] = k * grad[2, :, lane]
            for s in range(8):
                for tile in range(2):
                    part = pl.ds(128 * tile, 128)
                    out = along_r(deriv.T, [flux[0, pl.ds(64 * r + 8 * s, 8), part] for r in range(8)])
                    for r in range(8):
                        flux[0, pl.ds(64 * r + 8 * s, 8), part] = out[r]
            for h in range(2):
                rows = pl.ds(256 * h, 256)
                h2, l2 = cut(flux[1, rows])
                h3, l3 = cut(flux[2, rows])
                value = dot(bwd_st[...], jnp.concatenate([h2, h3, h2, h3, l2, l3], 0))
                field = basis[i, 4 * h : 4 * h + 4, :, :, lane].reshape(256, 256)
                v = volume_ref[rows] * (0.05 / SCALE)
                value = value + flux[0, rows] + jnp.concatenate([v, v], 1) * field
                basis[i + 1, 4 * h : 4 * h + 4, :, :, lane] = value.reshape(4, 8, 8, 256)
                acc[2 * i + 1] += fold(value * field)

    def body(i, carry):
        power(i)
        assemble_start(i + 1)
        for block in range(2):
            norm(i, block)
        assemble_end(i + 1)
        gradient(i + 1)
        return carry

    lax.fori_loop(0, ITERS - 1, body, 0)

    final = ITERS - 1
    for block in range(2):
        lane = pl.ds(256 * block, 256)
        norm(final, block)
        mix = 2.0 * cross[:, 256 * block : 256 * block + 256]
        for h in range(4):
            rows = pl.ds(128 * h, 128)
            g1, g2, g3 = grad[0, rows, lane], grad[1, rows, lane], grad[2, rows, lane]
            field = basis[final, 2 * h : 2 * h + 2, :, :, lane].reshape(128, 256)
            v = volume_ref[rows] * (0.05 / SCALE)
            energy = kap[rows, lane] * (g1 * (g1 + mix * g2) + g2 * g2 + g3 * g3)
            acc[2 * final + 1] += fold(energy + jnp.concatenate([v, v], 1) * (field * field))

    rows = jnp.concatenate([jnp.sum(acc[k], axis=0, keepdims=True) for k in range(16)], 0)
    mine = jnp.sum(rows, axis=1, keepdims=True)
    message = jnp.sum(jnp.where(iota((16, 128), 0) == iota((16, 128), 1), mine, 0.0), axis=0, keepdims=True)
    chan_sum[chan] = message
    copies = []
    for j in range(1, n_chan):
        copies.append(
            pltpu.make_async_remote_copy(
                src_ref=chan_sum.at[chan],
                dst_ref=chan_sum.at[chan],
                send_sem=chan_send.at[j],
                recv_sem=chan_recv.at[j],
                device_id=(slab, lax.rem(chan + j, n_chan)),
                device_id_type=MESH,
            )
        )
    for copy in copies:
        copy.start()
    for copy in copies:
        copy.wait()
    message = chan_sum[0]
    for j in range(1, n_chan):
        message = message + chan_sum[j]
    slab_sum[slab] = message
    copies = []
    for j in range(1, n_slab):
        copies.append(
            pltpu.make_async_remote_copy(
                src_ref=slab_sum.at[slab],
                dst_ref=slab_sum.at[slab],
                send_sem=slab_send.at[j],
                recv_sem=slab_recv.at[j],
                device_id=(lax.rem(slab + j, n_slab), chan),
                device_id_type=MESH,
            )
        )
    for copy in copies:
        copy.start()
    for copy in copies:
        copy.wait()
    message = slab_sum[0]
    for j in range(1, n_slab):
        message = message + slab_sum[j]
    lane1 = iota((1, 128), 1)
    moment = [
        jnp.sum(jnp.where(lane1 == k, message, 0.0), axis=1, keepdims=True) for k in range(2 * ITERS)
    ]
    weight = [w * (1.0 / SCALE) for w in krylov_weights(moment)]
    full = [jnp.broadcast_to(w, (8, 128)) for w in weight]
    for r in range(8):
        for s in range(8):
            for l in range(2):
                for h in range(2):
                    lane = pl.ds(256 * l + 128 * h, 128)
                    total = full[0] * basis[0, r, s, :, lane]
                    for i in range(1, ITERS):
                        total = total + full[i] * basis[i, r, s, :, lane]
                    out_ref[pl.ds(256 * r + 32 * s + 2 * h + l, 8, stride=4), :] = total


def panel(pack, prev, source, flags, plies, ops):
    n_slab, n_chan = lax.axis_size("slab"), lax.axis_size("chan")
    vmem = pl.BlockSpec(memory_space=pltpu.VMEM)
    anywhere = pl.BlockSpec(memory_space=pl.ANY)
    dma = pltpu.SemaphoreType.DMA
    return pl.pallas_call(
        functools.partial(panel_kernel, n_slab, n_chan),
        in_specs=[anywhere] * 8,
        out_specs=vmem,
        out_shape=jax.ShapeDtypeStruct((2048, 128), F32),
        scratch_shapes=[
            pltpu.VMEM((ITERS, 8, 8, 8, 512), F32),
            pltpu.VMEM((512, 512), F32),
            pltpu.VMEM((512, 512), F32),
            pltpu.VMEM((3, 512, 512), F32),
            pltpu.VMEM((3, 512, 256), F32),
            pltpu.VMEM((16, 8, 128), F32),
            pltpu.VMEM((3, 528, 128), BF16),
            pltpu.VMEM((ITERS, 2, 8, 128), F32),
            pltpu.VMEM((ITERS, 8, 8, 128), F32),
            pltpu.VMEM((ITERS, 2, 8, 8, 256), F32),
            pltpu.VMEM((ITERS, 2, 8, 8, 256), F32),
            pltpu.VMEM((n_chan, 1, 128), F32),
            pltpu.VMEM((n_slab, 1, 128), F32),
            pltpu.VMEM((2048, 128), F32),
            pltpu.VMEM((2048, 128), F32),
            pltpu.VMEM((512, 128), F32),
            pltpu.VMEM((2, 256), jnp.int32),
            pltpu.VMEM((2, 256), jnp.int32),
            pltpu.VMEM((2, 528, 128), BF16),
            pltpu.VMEM((512, 768), BF16),
            pltpu.VMEM((256, 1536), BF16),
            dma((10,)),
            dma((3,)),
            dma((3,)),
            dma((ITERS, 8)),
            dma((ITERS, 8)),
            dma((n_chan,)),
            dma((n_chan,)),
            dma((n_slab,)),
            dma((n_slab,)),
        ],
        compiler_params=pltpu.CompilerParams(collective_id=0, has_side_effects=True),
        name="panel",
    )(
        pack,
        prev,
        source,
        flags,
        plies,
        ops["forward"],
        ops["backward"],
        ops["volume"],
    )


def lanes_first(x):
    return x.reshape(512, 2, 2, 128).transpose(0, 2, 1, 3).reshape(2048, 128)


def on_device(u, index, prev, source, flags, plies):
    ops = operators()
    stepped, pack = fluid(u.reshape(192, 8, 512), index.reshape(1, 512), ops)
    warmth = panel(pack, lanes_first(prev), lanes_first(source), flags, plies, ops)
    warmth = warmth.reshape(512, 2, 2, 128).transpose(0, 2, 1, 3).reshape(8, 8, 8, 2, 256)
    return stepped.reshape(3, 8, 8, 8, 512), warmth


def solution(mesh):
    in_specs = (
        P(None, None, None, None, ("slab", "chan")),
        P(("slab", "chan")),
        P(None, None, None, "chan", "slab"),
        P(None, None, None, "chan", "slab"),
        P("chan", "slab"),
        P("chan", "slab"),
    )
    out_specs = (P(None, None, None, None, ("slab", "chan")), P(None, None, None, "chan", "slab"))
    return jax.shard_map(
        on_device, mesh=mesh, in_specs=in_specs, out_specs=out_specs, check_vma=False
    )
```

```python
import functools

import jax
import jax.numpy as jnp
import numpy as np
from jax import lax
from jax.experimental import pallas as pl
from jax.experimental.pallas import tpu as pltpu
from jax.sharding import PartitionSpec as P

F32 = jnp.float32
BF16 = jnp.bfloat16
MESH = pl.DeviceIdType.MESH
ITERS = 5
SCALE = 64.0
NT = (((1,), (1,)), ((), ()))
NN = (((1,), (0,)), ((), ()))


def gll():
    points = np.array(
        [
            -1.0,
            -0.8717401485096066,
            -0.5917001814331423,
            -0.2092992179024789,
            0.2092992179024789,
            0.5917001814331423,
            0.8717401485096066,
            1.0,
        ]
    )
    weights = np.array(
        [
            1.0 / 28.0,
            0.2107042271435061,
            0.3411226924835044,
            0.4124587946587038,
            0.4124587946587038,
            0.3411226924835044,
            0.2107042271435061,
            1.0 / 28.0,
        ]
    )
    low = np.ones(8)
    high = points.copy()
    for degree in range(1, 7):
        low, high = high, ((2 * degree + 1) * points * high - degree * low) / (degree + 1)
    gaps = points[:, None] - points[None, :] + np.eye(8)
    deriv = high[:, None] / (high[None, :] * gaps)
    deriv = deriv * (1.0 - np.eye(8))
    deriv[0, 0] = -14.0
    deriv[7, 7] = 14.0
    return deriv, weights


def two(matrix):
    high = np.asarray(matrix, np.float32).astype(BF16).astype(np.float64)
    return high, matrix - high


def operators():
    deriv, weights = gll()
    second = deriv @ deriv
    eye = np.eye
    kron = np.kron
    along_s = kron(eye(4), kron(deriv, eye(8)))
    along_t = kron(eye(32), deriv)
    along_r = kron(deriv, eye(32))
    ds_hi, ds_lo = two(along_s)
    dt_hi, dt_lo = two(along_t)
    forward = np.block([[ds_hi, ds_lo], [dt_hi, dt_lo]])
    backward = np.block([[ds_hi.T, dt_hi.T, ds_lo.T, dt_lo.T]])
    lap_st = 0.0002 * (kron(eye(4), kron(second, eye(8))) + kron(eye(32), second))
    both_r = np.block([[along_r], [0.0002 * kron(second, eye(32))]])
    volume = (weights[:, None, None] * weights[None, :, None] * weights[None, None, :]).reshape(512, 1)
    cast = lambda m: jnp.asarray(np.asarray(m, np.float32).astype(BF16))
    return {
        "forward": cast(forward),
        "backward": cast(backward),
        "lap_st": cast(lap_st),
        "both_r": cast(both_r),
        "volume": jnp.asarray(np.broadcast_to(volume, (512, 128)), F32),
    }


def dot(a, b, dims=NN):
    return lax.dot_general(a, b, dims, preferred_element_type=F32)


def iota(shape, dim):
    return lax.broadcasted_iota(jnp.int32, shape, dim)


def krylov_weights(m):
    n = ITERS
    zero = jnp.zeros_like(m[0])
    older, newer = [zero] * (2 * n), list(m)
    diag = [newer[1] / newer[0]]
    off = [zero]
    for k in range(1, n):
        fresh = [zero] * (2 * n)
        for l in range(k, 2 * n - k):
            fresh[l] = newer[l + 1] - diag[k - 1] * newer[l] - off[k - 1] * older[l]
        diag.append(fresh[k + 1] / fresh[k] - newer[k] / newer[k - 1])
        off.append(fresh[k] / newer[k - 1])
        older, newer = newer, fresh
    alpha = [1.0 / diag[0]]
    beta = []
    for k in range(1, n):
        beta.append(off[k] * alpha[k - 1] * alpha[k - 1])
        alpha.append(1.0 / (diag[k] - beta[k - 1] / alpha[k - 1]))
    one = jnp.ones_like(zero)
    res, way, sol = [one], [one], [zero] * n
    for k in range(n):
        for i in range(k + 1):
            sol[i] = sol[i] + alpha[k] * way[i]
        if k < n - 1:
            res = res + [zero]
            for i in range(k + 1):
                res[i + 1] = res[i + 1] - alpha[k] * way[i]
            way = [res[i] + (beta[k] * way[i] if i <= k else 0.0) for i in range(k + 2)]
    return sol


EDGES = ((1, 0), (-1, 0), (1, 1), (1, -1), (-1, 1), (-1, -1))
HALO = EDGES + ((0, 1), (0, -1))


def along(matrix, v):
    even = [v[k] + v[7 - k] for k in range(4)]
    odd = [v[k] - v[7 - k] for k in range(4)]
    first, last = [], []
    for i in range(4):
        same = [0.5 * float(matrix[i, k] + matrix[i, 7 - k]) for k in range(4)]
        flip = [0.5 * float(matrix[i, k] - matrix[i, 7 - k]) for k in range(4)]
        p = (same[0] * even[0] + same[1] * even[1]) + (same[2] * even[2] + same[3] * even[3])
        q = (flip[0] * odd[0] + flip[1] * odd[1]) + (flip[2] * odd[2] + flip[3] * odd[3])
        first.append(p + q)
        last.append(q - p)
    return first + last[::-1]


def cut(x):
    high = x.astype(BF16)
    return high, (x - high.astype(F32)).astype(BF16)


def ends_middle(low, high):
    half = iota(low.shape, 1) < 64
    return jnp.where(half, low, high), jnp.where(half, high, low)


def kernel(
    n_slab,
    n_chan,
    u_hbm,
    index_hbm,
    prev_hbm,
    source_hbm,
    flag_hbm,
    ply_hbm,
    forward_hbm,
    backward_hbm,
    lap_hbm,
    both_hbm,
    volume_hbm,
    new_ref,
    out_ref,
    u_ref,
    index_ref,
    prev_ref,
    source_ref,
    flag_ref,
    ply_ref,
    fwd_st,
    bwd_st,
    lap_st,
    both_r,
    volume_ref,
    speed_grad,
    lap,
    cond,
    own_pack,
    put_pack,
    got_pack,
    basis,
    kap,
    mix_ref,
    inv_mult,
    grad,
    ysum,
    flux,
    acc,
    edge_out,
    edge_in,
    side_out,
    side_in,
    chan_sum,
    slab_sum,
    load_sem,
    pack_send,
    pack_recv,
    halo_send,
    halo_recv,
    chan_send,
    chan_recv,
    slab_send,
    slab_recv,
):
    slab = lax.axis_index("slab")
    chan = lax.axis_index("chan")
    device = slab * n_chan + chan
    devices = n_slab * n_chan

    def near(ds, dc):
        return (lax.rem(slab + ds + n_slab, n_slab), lax.rem(chan + dc + n_chan, n_chan))

    left, right = pl.ds(0, 256), pl.ds(256, 256)
    loads = [
        pltpu.make_async_copy(src, dst, load_sem.at[k])
        for k, (src, dst) in enumerate(
            (
                (prev_hbm, prev_ref),
                (source_hbm, source_ref),
                (volume_hbm, volume_ref),
                (flag_hbm, flag_ref),
                (ply_hbm, ply_ref),
                (u_hbm.at[:, :, left], u_ref.at[:, :, left]),
                (lap_hbm, lap_st),
                (both_hbm, both_r),
                (forward_hbm, fwd_st.at[:, pl.ds(0, 512)]),
                (u_hbm.at[:, :, right], u_ref.at[:, :, right]),
                (forward_hbm.at[:, pl.ds(0, 256)], fwd_st.at[:, pl.ds(512, 256)]),
                (backward_hbm, bwd_st.at[:, pl.ds(0, 1024)]),
                (backward_hbm.at[:, pl.ds(0, 512)], bwd_st.at[:, pl.ds(1024, 512)]),
                (index_hbm, index_ref),
            )
        )
    ]
    loads[13].start()
    for load in loads[:13]:
        load.start()

    barrier = pltpu.get_barrier_semaphore()
    greet = [near(*d) for d in HALO]
    greet += [(slab, lax.rem(chan + j, n_chan)) for j in range(2, n_chan - 1)]
    greet += [(lax.rem(slab + j, n_slab), chan) for j in range(2, n_slab - 1)]
    for peer in greet:
        pl.semaphore_signal(barrier, inc=1, device_id=peer, device_id_type=MESH)

    loads[13].wait()
    target = index_ref[...]
    slot = target & 511
    distance = ((target >> 9) - device) & (devices - 1)
    group = jnp.where(
        distance == 1,
        1,
        jnp.where(distance == devices - 1, 2, jnp.where(distance == n_chan, 3, 0)),
    )
    member = iota((8, 512), 0) == group
    before = (iota((512, 512), 0) < iota((512, 512), 1)).astype(F32).astype(BF16)
    rank = dot(member.astype(F32).astype(BF16), before)
    begin = jnp.where(iota((8, 512), 0) == 0, 0, 128 + 128 * iota((8, 512), 0)).astype(F32)
    position = jnp.sum(jnp.where(member, rank + begin, 0.0), axis=0, keepdims=True).astype(jnp.int32)
    code = jnp.where(
        iota((16, 512), 0) == 0,
        (slot >> 5) + 1,
        jnp.where(iota((16, 512), 0) == 1, slot & 31, 0),
    )
    cond[512:528] = code.astype(F32).astype(BF16)

    for load in loads[:5]:
        load.wait()
    for l in range(2):
        halves = []
        for h in range(2):
            rows = pl.ds(2 * h + l, 512, stride=4)
            halves.append(volume_ref[...] * (0.05 * prev_ref[rows, :] + source_ref[rows, :]))
        for m, value in enumerate(ends_middle(*halves)):
            basis[0, :, :, :, pl.ds(256 * m + 128 * l, 128)] = value.reshape(8, 8, 8, 128)
    damping = []
    mixing = []
    for l in range(2):
        flag = flag_ref[pl.ds(l, 1)]
        ply = ply_ref[pl.ds(l, 1)].astype(F32)
        damp = jnp.where(flag == 1, 1.0 / (1.0 + 0.25 * ply), 1.0) * (1.0 / SCALE)
        mix = 0.4 * flag.astype(F32) * ply / (ply + 1.0)
        wide = [jnp.broadcast_to(x, (8, 256)) for x in (damp, mix)]
        damping.append(ends_middle(wide[0][:, :128], wide[0][:, 128:]))
        mixing.append(ends_middle(wide[1][:, :128], wide[1][:, 128:]))
    damping = [damping[l][m][0:1] for m in range(2) for l in range(2)]
    mixing = [mixing[l][m] for m in range(2) for l in range(2)]
    for tile in range(4):
        mix_ref[:, pl.ds(128 * tile, 128)] = mixing[tile]

    def fluid(block):
        lane = pl.ds(256 * block, 256)
        for c in range(3):
            flat = u_ref[pl.ds(64 * c, 64), :, lane].astype(F32).reshape(512, 256)
            low = flat.astype(BF16)
            for h in range(2):
                rows = pl.ds(256 * h, 256)
                part = low[256 * h : 256 * h + 256]
                both = dot(fwd_st[:, 0:256], part)
                speed_grad[c, 1, rows, lane] = both[:256]
                speed_grad[c, 2, rows, lane] = both[256:]
                lap[c, rows, lane] = dot(lap_st[...], part)
            by_r = flat.reshape(8, 64, 256)
            for q in range(2):
                part = by_r[:, 32 * q : 32 * q + 32].reshape(256, 256).astype(BF16)
                both = dot(both_r[...], part).reshape(16, 32, 256)
                for r in range(8):
                    rows = pl.ds(64 * r + 32 * q, 32)
                    speed_grad[c, 0, rows, lane] = both[r]
                    lap[c, rows, lane] += both[8 + r]
            for n in range(32):
                for tile in range(2):
                    part = pl.ds(256 * block + 128 * tile, 128)
                    rows = pl.ds(16 * n, 16)
                    u = [u_ref[pl.ds(64 * k + 2 * n, 2), :, part].astype(F32).reshape(16, 128) for k in range(3)]
                    turn = (
                        u[0] * speed_grad[c, 0, rows, part]
                        + u[1] * speed_grad[c, 1, rows, part]
                        + u[2] * speed_grad[c, 2, rows, part]
                    )
                    new = ((u[c] + lap[c, rows, part]) - 0.01 * turn).astype(BF16).astype(F32)
                    new_ref[pl.ds(64 * c + 2 * n, 2), :, part] = new.reshape(2, 8, 128).astype(BF16)
                    square = new * new if c == 0 else ysum[rows, part] + new * new
                    if c < 2:
                        ysum[rows, part] = square
                    else:
                        cond[rows, part] = (1.0 + 0.5 * square).astype(BF16)

    for load in loads[5:9]:
        load.wait()
    fluid(0)

    lane8 = iota((8, 128), 1)
    has_left = slab > 0
    has_right = slab < n_slab - 1
    has_under = chan > 0
    has_over = chan < n_chan - 1
    has_next = {(1, 0): has_right, (-1, 0): has_left, (0, 1): has_over, (0, -1): has_under}

    def both_of(ds, dc):
        if ds == 0 or dc == 0:
            return has_next[ds, dc]
        return has_next[ds, 0] & has_next[0, dc]

    SIDES = ((0, 1, 0), (0, -1, 0), (0, 1, 1), (0, -1, 1))

    def halo_copies(i, want_edges, want_sides):
        turn = i % 2 if isinstance(i, int) else lax.rem(i, 2)

        def remote(src, dst, number, ds, dc):
            return pltpu.make_async_remote_copy(
                src_ref=src,
                dst_ref=dst,
                send_sem=halo_send.at[turn, number],
                recv_sem=halo_recv.at[turn, number],
                device_id=near(ds, dc),
                device_id_type=MESH,
            )

        edges = [
            (ds, dc, remote(edge_out.at[turn, 0 if ds == 1 else 1], edge_in.at[turn, d], d, ds, dc))
            for d, (ds, dc) in enumerate(EDGES)
            if want_edges
        ]
        sides = []
        for d, (ds, dc, m) in enumerate(SIDES):
            if m not in want_sides:
                continue
            k = 0 if dc == 1 else 1
            sides.append((ds, dc, remote(side_out.at[turn, k, m], side_in.at[turn, k, m], 6 + d, ds, dc)))
        return turn, edges, sides

    def send(copies):
        for ds, dc, copy in copies:
            pl.when(both_of(ds, dc))(copy.start)

    def arrive(copies):
        for ds, dc, copy in copies:
            pl.when(both_of(ds, dc))(copy.wait_send)
            pl.when(both_of(-ds, -dc))(copy.wait_recv)

    def lanes(m, l):
        return pl.ds(256 * m + 128 * l, 128)

    def between(i, m, turn):
        side_out[turn, 0, m] = basis[i, :, 7, :, lanes(m, 1)]
        side_out[turn, 1, m] = basis[i, :, 0, :, lanes(m, 0)]
        both = basis[i, :, 7, :, lanes(m, 0)] + basis[i, :, 0, :, lanes(m, 1)]
        basis[i, :, 7, :, lanes(m, 0)] = both
        basis[i, :, 0, :, lanes(m, 1)] = both

    def start_ends(i):
        turn, edges, sides = halo_copies(i, True, (0,))
        between(i, 0, turn)
        up = jnp.zeros((8, 128), F32)
        down = jnp.zeros((8, 128), F32)
        for l in range(2):
            for s in range(8):
                to = s + 8 * l
                here = lane8 == to
                up = jnp.where(here, pltpu.roll(basis[i, 7, s, :, lanes(0, l)], (to - 127) % 128, 1), up)
                down = jnp.where(here, pltpu.roll(basis[i, 0, s, :, lanes(0, l)], to, 1), down)
        edge_out[turn, 0] = up
        edge_out[turn, 1] = down
        send(edges)
        send(sides)

    def start_middle(i):
        turn, edges, sides = halo_copies(i, False, (1,))
        between(i, 1, turn)
        send(sides)

    def finish_sides(i):
        turn, edges, sides = halo_copies(i, False, (0, 1))
        arrive(sides)
        for k, (has, s, l) in enumerate(((has_under, 0, 0), (has_over, 7, 1))):
            for m in range(2):
                basis[i, :, s, :, lanes(m, l)] += jnp.where(has, side_in[turn, k, m], 0.0)
        j = iota((64, 128), 1)
        for l in range(2):
            high = [basis[i, 7, :, :, lanes(m, l)].reshape(64, 128) for m in range(2)]
            low = [basis[i, 0, :, :, lanes(m, l)].reshape(64, 128) for m in range(2)]
            ahead = [pltpu.roll(x, 127, 1) for x in low]
            behind = [pltpu.roll(x, 1, 1) for x in high]
            for m in range(2):
                more = jnp.where(j == 63, ahead[1 - m], ahead[m])
                less = jnp.where(j == 64, behind[1 - m], behind[m])
                if m == 0:
                    more = jnp.where(j == 127, 0.0, more)
                    less = jnp.where(j == 0, 0.0, less)
                basis[i, 7, :, :, lanes(m, l)] = (high[m] + more).reshape(8, 8, 128)
                basis[i, 0, :, :, lanes(m, l)] = (low[m] + less).reshape(8, 8, 128)

    def finish_edges(i):
        turn, edges, sides = halo_copies(i, True, ())
        arrive(edges)
        first = lane8 == 0
        last = lane8 == 127

        def add(l, s, at, slot_left, slot_right, has):
            left_ok = has_left if has is None else has_left & has
            right_ok = has_right if has is None else has_right & has
            basis[i, 0, s, :, lanes(0, l)] += jnp.where(
                first & left_ok, pltpu.roll(edge_in[turn, slot_left], (128 - at) % 128, 1), 0.0
            )
            basis[i, 7, s, :, lanes(0, l)] += jnp.where(
                last & right_ok, pltpu.roll(edge_in[turn, slot_right], (127 - at) % 128, 1), 0.0
            )

        for l in range(2):
            for s in range(8):
                add(l, s, s + 8 * l, EDGES.index((1, 0)), EDGES.index((-1, 0)), None)
        add(0, 0, 15, EDGES.index((1, 1)), EDGES.index((-1, 1)), has_under)
        add(1, 7, 0, EDGES.index((1, -1)), EDGES.index((-1, -1)), has_over)

    loads[9].wait()
    fluid(1)
    pl.semaphore_wait(barrier, len(greet))
    start_ends(0)
    start_middle(0)

    def packed(start, count):
        chosen = (iota((count, 512), 0) + start == position).astype(F32).astype(BF16)
        return dot(cond[...], chosen, NT).astype(BF16)

    def device_at(step):
        number = lax.rem(device + step + devices, devices)
        return (number // n_chan, lax.rem(number, n_chan))

    moves = [
        pltpu.make_async_remote_copy(
            src_ref=put_pack.at[k],
            dst_ref=got_pack.at[k],
            send_sem=pack_send.at[k],
            recv_sem=pack_recv.at[k],
            device_id=device_at(step),
            device_id_type=MESH,
        )
        for k, step in enumerate((n_chan, 1, -1))
    ]
    late = packed(512, 128)
    put_pack[0] = late
    moves[0].start()
    soon = packed(256, 256)
    put_pack[1] = soon[:, :128]
    put_pack[2] = soon[:, 128:]
    moves[1].start()
    moves[2].start()
    own_pack[...] = packed(0, 256)

    def place(block):
        code = block[512:528].astype(F32)
        slot = ((code[0:1] - 1.0) * 32.0 + code[1:2]).astype(jnp.int32)
        lane = iota((512, block.shape[1]), 0)
        here = lane & 127
        axial = here + jnp.where((lane < 256) == (here < 64), 0, 128)
        chosen = (((lane >> 7) & 1) * 256 + axial == slot).astype(F32).astype(BF16)
        return dot(block[0:512], chosen, NT)

    kap[...] = place(own_pack[...])
    node = iota((512, 128), 0)
    at_r = node >> 6
    at_s = (node >> 3) & 7
    for m in range(2):
        for l in range(2):
            here = iota((512, 128), 1)
            axial = slab * 256 + here + jnp.where(here < 64, 128 * m, 128 - 128 * m)
            m_r = jnp.where(((at_r == 0) & (axial > 0)) | ((at_r == 7) & (axial < n_slab * 256 - 1)), 0.5, 1.0)
            lateral = chan * 2 + l
            m_s = jnp.where(((at_s == 0) & (lateral > 0)) | ((at_s == 7) & (lateral < n_chan * 2 - 1)), 0.5, 1.0)
            inv_mult[:, lanes(m, l)] = m_r * m_s

    deriv = gll()[0]

    spare = lax.div(slab, n_slab)

    def gradient(i, block):
        lane = pl.ds(256 * block, 256)
        pairs = [cut(basis[i, 4 * h : 4 * h + 4, :, :, lane].reshape(256, 256)) for h in range(2)]

        def turn(h):
            high, low = pairs[h]
            both = dot(fwd_st[...], jnp.concatenate([high, high, low], 0))
            grad[1, pl.ds(256 * h, 256), lane] = both[:256]
            grad[2, pl.ds(256 * h, 256), lane] = both[256:]
            return both

        basis[ITERS + spare, 0, 0, :, 0:128] = turn(0)[0:8, 0:128]
        for s in range(8):
            for tile in range(2):
                part = pl.ds(256 * block + 128 * tile, 128)
                out = along(deriv, [basis[i, r, s, :, part] for r in range(8)])
                for r in range(8):
                    grad[0, pl.ds(64 * r + 8 * s, 8), part] = out[r]
        turn(1)

    def fold(x):
        total = jnp.sum(x.reshape(x.shape[0] // 8, 8, 256), axis=0)
        return total[:, :128] + total[:, 128:]

    def norm(i):
        totals = [None] * 4
        for n in range(64):
            for tile in range(4):
                part = pl.ds(128 * tile, 128)
                v = basis[i, n // 8, n % 8, :, part]
                term = v * v * inv_mult[pl.ds(8 * n, 8), part]
                totals[tile] = term if n == 0 else totals[tile] + term
        acc[2 * i] = (totals[0] + totals[1]) + (totals[2] + totals[3])

    def power(i, block):
        lane = pl.ds(256 * block, 256)
        mix = mix_ref[0:1, lane]

        def stage(h):
            rows = pl.ds(256 * h, 256)
            k = kap[rows, lane]
            k1 = k * grad[0, rows, lane]
            k2 = k * grad[1, rows, lane]
            flux[0, rows] = k1 + mix * k2
            h2, l2 = cut(k2 + mix * k1)
            h3, l3 = cut(k * grad[2, rows, lane])
            return jnp.concatenate([h2, h3, h2, h3, l2, l3], 0)

        staged = [stage(h) for h in range(2)]
        for h in range(2):
            value = dot(bwd_st[...], staged[h])
            ysum[pl.ds(256 * h, 256), lane] = value
            if h == 0:
                flux[1 + spare, 0:8, 0:128] = value[0:8, 0:128]
                for s in range(8):
                    for tile in range(2):
                        part = pl.ds(128 * tile, 128)
                        out = along(deriv.T, [flux[0, pl.ds(64 * r + 8 * s, 8), part] for r in range(8)])
                        for r in range(8):
                            flux[0, pl.ds(64 * r + 8 * s, 8), part] = out[r]
        total = None
        for h in range(2):
            rows = pl.ds(256 * h, 256)
            field = basis[i, 4 * h : 4 * h + 4, :, :, lane].reshape(256, 256)
            v = volume_ref[rows] * (0.05 / SCALE)
            value = ysum[rows, lane] + flux[0, rows] + jnp.concatenate([v, v], 1) * field
            basis[i + 1, 4 * h : 4 * h + 4, :, :, lane] = value.reshape(4, 8, 8, 256)
            part = fold(value * field)
            total = part if total is None else total + part
        return total

    for load in loads[10:13]:
        load.wait()
    finish_sides(0)
    gradient(0, 1)
    finish_edges(0)
    gradient(0, 0)
    moves[1].wait()
    moves[2].wait()
    kap[...] += place(jnp.concatenate([got_pack[1], got_pack[2]], 1))
    moves[0].wait()
    last_part = place(got_pack[0])
    for tile in range(4):
        lane = pl.ds(128 * tile, 128)
        kap[:, lane] = (
            volume_ref[...]
            * (kap[:, lane] + last_part[:, 128 * tile : 128 * tile + 128])
            * damping[tile]
        )

    def body(i, carry):
        ends = power(i, 0)
        start_ends(i + 1)
        acc[2 * i + 1] = ends + power(i, 1)
        start_middle(i + 1)
        norm(i)
        finish_sides(i + 1)
        gradient(i + 1, 1)
        finish_edges(i + 1)
        gradient(i + 1, 0)
        return carry

    lax.fori_loop(0, ITERS - 1, body, 0)

    final = ITERS - 1
    norm(final)
    totals = [None] * 4
    twice = [2.0 * mix_ref[:, pl.ds(128 * tile, 128)] for tile in range(4)]
    for n in range(64):
        eight = pl.ds(8 * n, 8)
        v5 = volume_ref[eight, :] * (0.05 / SCALE)
        for tile in range(4):
            part = pl.ds(128 * tile, 128)
            g1, g2, g3 = grad[0, eight, part], grad[1, eight, part], grad[2, eight, part]
            v = basis[final, n // 8, n % 8, :, part]
            term = kap[eight, part] * (g1 * (g1 + twice[tile] * g2) + (g2 * g2 + g3 * g3)) + v5 * (v * v)
            totals[tile] = term if n == 0 else totals[tile] + term
    acc[2 * final + 1] = (totals[0] + totals[1]) + (totals[2] + totals[3])

    rows = [jnp.sum(acc[k], axis=0, keepdims=True) for k in range(2 * ITERS)]
    rows = jnp.concatenate(rows + [jnp.zeros((6, 128), F32)], 0)
    mine = jnp.sum(rows, axis=1, keepdims=True)
    message = jnp.sum(jnp.where(iota((16, 128), 0) == iota((16, 128), 1), mine, 0.0), axis=0, keepdims=True)

    def everyone(message, sums, me, count, sends, recvs, peer):
        sums[me] = message
        copies = [
            pltpu.make_async_remote_copy(
                src_ref=sums.at[me],
                dst_ref=sums.at[me],
                send_sem=sends.at[j],
                recv_sem=recvs.at[j],
                device_id=peer(lax.rem(me + j, count)),
                device_id_type=MESH,
            )
            for j in range(1, count)
        ]
        for copy in copies:
            copy.start()
        for copy in copies:
            copy.wait()
        total = sums[0]
        for j in range(1, count):
            total = total + sums[j]
        return total

    message = everyone(message, chan_sum, chan, n_chan, chan_send, chan_recv, lambda c: (slab, c))
    message = everyone(message, slab_sum, slab, n_slab, slab_send, slab_recv, lambda s: (s, chan))
    lane1 = iota((1, 128), 1)
    moment = [
        jnp.sum(jnp.where(lane1 == k, message, 0.0), axis=1, keepdims=True) for k in range(2 * ITERS)
    ]
    weight = [w * (1.0 / SCALE) for w in krylov_weights(moment)]
    full = [jnp.broadcast_to(w, (8, 128)) for w in weight]
    for r in range(8):
        for s in range(8):
            for l in range(2):
                pieces = []
                for m in range(2):
                    total = full[0] * basis[0, r, s, :, lanes(m, l)]
                    for i in range(1, ITERS):
                        total = total + full[i] * basis[i, r, s, :, lanes(m, l)]
                    pieces.append(total)
                for h, total in enumerate(ends_middle(*pieces)):
                    out_ref[pl.ds(256 * r + 32 * s + 2 * h + l, 8, stride=4), :] = total


def flush_kernel(new_ref, out_ref, new_hbm, out_hbm, sem):
    first = pltpu.make_async_copy(new_ref, new_hbm, sem.at[0])
    second = pltpu.make_async_copy(out_ref, out_hbm, sem.at[1])
    first.start()
    second.start()
    first.wait()
    second.wait()


def step(u, index, prev, source, flags, plies, ops):
    n_slab, n_chan = lax.axis_size("slab"), lax.axis_size("chan")
    anywhere = pl.BlockSpec(memory_space=pl.ANY)
    vmem = pl.BlockSpec(memory_space=pltpu.VMEM)
    dma = pltpu.SemaphoreType.DMA
    new, warmth = pl.pallas_call(
        functools.partial(kernel, n_slab, n_chan),
        in_specs=[anywhere] * 11,
        out_specs=[vmem, vmem],
        out_shape=[
            pltpu.MemorySpace.VMEM((192, 8, 512), BF16),
            pltpu.MemorySpace.VMEM((2048, 128), F32),
        ],
        scratch_shapes=[
            pltpu.VMEM((192, 8, 512), BF16),
            pltpu.VMEM((1, 512), jnp.int32),
            pltpu.VMEM((2048, 128), F32),
            pltpu.VMEM((2048, 128), F32),
            pltpu.VMEM((2, 256), jnp.int32),
            pltpu.VMEM((2, 256), jnp.int32),
            pltpu.VMEM((512, 768), BF16),
            pltpu.VMEM((256, 1536), BF16),
            pltpu.VMEM((256, 256), BF16),
            pltpu.VMEM((512, 256), BF16),
            pltpu.VMEM((512, 128), F32),
            pltpu.VMEM((3, 3, 512, 512), F32),
            pltpu.VMEM((3, 512, 512), F32),
            pltpu.VMEM((528, 512), BF16),
            pltpu.VMEM((528, 256), BF16),
            pltpu.VMEM((3, 528, 128), BF16),
            pltpu.VMEM((3, 528, 128), BF16),
            pltpu.VMEM((ITERS + 1, 8, 8, 8, 512), F32),
            pltpu.VMEM((512, 512), F32),
            pltpu.VMEM((8, 512), F32),
            pltpu.VMEM((512, 512), F32),
            pltpu.VMEM((3, 512, 512), F32),
            pltpu.VMEM((512, 512), F32),
            pltpu.VMEM((2, 512, 256), F32),
            pltpu.VMEM((2 * ITERS, 8, 128), F32),
            pltpu.VMEM((2, 2, 8, 128), F32),
            pltpu.VMEM((2, 6, 8, 128), F32),
            pltpu.VMEM((2, 2, 2, 8, 8, 128), F32),
            pltpu.VMEM((2, 2, 2, 8, 8, 128), F32),
            pltpu.VMEM((n_chan, 1, 128), F32),
            pltpu.VMEM((n_slab, 1, 128), F32),
            dma((14,)),
            dma((3,)),
            dma((3,)),
            dma((2, 10)),
            dma((2, 10)),
            dma((n_chan,)),
            dma((n_chan,)),
            dma((n_slab,)),
            dma((n_slab,)),
        ],
        compiler_params=pltpu.CompilerParams(
            collective_id=0, has_side_effects=True
        ),
        name="step",
    )(
        u,
        index,
        prev,
        source,
        flags,
        plies,
        ops["forward"],
        ops["backward"],
        ops["lap_st"],
        ops["both_r"],
        ops["volume"],
    )
    new, warmth = pl.pallas_call(
        flush_kernel,
        in_specs=[vmem, vmem],
        out_specs=[anywhere, anywhere],
        out_shape=[
            jax.ShapeDtypeStruct((192, 8, 512), BF16),
            jax.ShapeDtypeStruct((2048, 128), F32),
        ],
        scratch_shapes=[dma((2,))],
        name="flush",
    )(
        pltpu.with_memory_space_constraint(new, pltpu.VMEM),
        pltpu.with_memory_space_constraint(warmth, pltpu.VMEM),
    )
    return new, warmth


def lanes_first(x):
    return x.reshape(512, 2, 2, 128).transpose(0, 2, 1, 3).reshape(2048, 128)


def on_device(u, index, prev, source, flags, plies):
    ops = operators()
    stepped, warmth = step(
        u.reshape(192, 8, 512),
        index.reshape(1, 512),
        lanes_first(prev),
        lanes_first(source),
        flags,
        plies,
        ops,
    )
    warmth = warmth.reshape(512, 2, 2, 128).transpose(0, 2, 1, 3).reshape(8, 8, 8, 2, 256)
    return stepped.reshape(3, 8, 8, 8, 512), warmth


def solution(mesh):
    in_specs = (
        P(None, None, None, None, ("slab", "chan")),
        P(("slab", "chan")),
        P(None, None, None, "chan", "slab"),
        P(None, None, None, "chan", "slab"),
        P("chan", "slab"),
        P("chan", "slab"),
    )
    out_specs = (P(None, None, None, None, ("slab", "chan")), P(None, None, None, "chan", "slab"))
    return jax.shard_map(
        on_device, mesh=mesh, in_specs=in_specs, out_specs=out_specs, check_vma=False
    )
```

```python
import functools

import jax
import jax.numpy as jnp
import numpy as np
from jax import lax
from jax.experimental import pallas as pl
from jax.experimental.pallas import tpu as pltpu
from jax.sharding import PartitionSpec as P

F32 = jnp.float32
BF16 = jnp.bfloat16
MESH = pl.DeviceIdType.MESH
ITERS = 5
SCALE = 64.0
NT = (((1,), (1,)), ((), ()))
NN = (((1,), (0,)), ((), ()))


def gll():
    points = np.array(
        [
            -1.0,
            -0.8717401485096066,
            -0.5917001814331423,
            -0.2092992179024789,
            0.2092992179024789,
            0.5917001814331423,
            0.8717401485096066,
            1.0,
        ]
    )
    weights = np.array(
        [
            1.0 / 28.0,
            0.2107042271435061,
            0.3411226924835044,
            0.4124587946587038,
            0.4124587946587038,
            0.3411226924835044,
            0.2107042271435061,
            1.0 / 28.0,
        ]
    )
    low = np.ones(8)
    high = points.copy()
    for degree in range(1, 7):
        low, high = high, ((2 * degree + 1) * points * high - degree * low) / (degree + 1)
    gaps = points[:, None] - points[None, :] + np.eye(8)
    deriv = high[:, None] / (high[None, :] * gaps)
    deriv = deriv * (1.0 - np.eye(8))
    deriv[0, 0] = -14.0
    deriv[7, 7] = 14.0
    return deriv, weights


def two(matrix):
    high = np.asarray(matrix, np.float32).astype(BF16).astype(np.float64)
    return high, matrix - high


def operators():
    deriv, weights = gll()
    second = deriv @ deriv
    eye = np.eye
    kron = np.kron
    along_s = kron(eye(4), kron(deriv, eye(8)))
    along_t = kron(eye(32), deriv)
    along_r = kron(deriv, eye(32))
    ds_hi, ds_lo = two(along_s)
    dt_hi, dt_lo = two(along_t)
    forward = np.block([[ds_hi, ds_lo], [dt_hi, dt_lo]])
    backward = np.block([[ds_hi.T, dt_hi.T, ds_lo.T, dt_lo.T]])
    lap_st = 0.0002 * (kron(eye(4), kron(second, eye(8))) + kron(eye(32), second))
    both_r = np.block([[along_r], [0.0002 * kron(second, eye(32))]])
    volume = (weights[:, None, None] * weights[None, :, None] * weights[None, None, :]).reshape(512, 1)
    cast = lambda m: jnp.asarray(np.asarray(m, np.float32).astype(BF16))
    return {
        "forward": cast(forward),
        "backward": cast(backward),
        "lap_st": cast(lap_st),
        "both_r": cast(both_r),
        "volume": jnp.asarray(np.broadcast_to(volume, (512, 128)), F32),
    }


def dot(a, b, dims=NN):
    return lax.dot_general(a, b, dims, preferred_element_type=F32)


def iota(shape, dim):
    return lax.broadcasted_iota(jnp.int32, shape, dim)


def krylov_weights(m):
    n = ITERS
    zero = jnp.zeros_like(m[0])
    older, newer = [zero] * (2 * n), list(m)
    diag = [newer[1] / newer[0]]
    off = [zero]
    for k in range(1, n):
        fresh = [zero] * (2 * n)
        for l in range(k, 2 * n - k):
            fresh[l] = newer[l + 1] - diag[k - 1] * newer[l] - off[k - 1] * older[l]
        diag.append(fresh[k + 1] / fresh[k] - newer[k] / newer[k - 1])
        off.append(fresh[k] / newer[k - 1])
        older, newer = newer, fresh
    alpha = [1.0 / diag[0]]
    beta = []
    for k in range(1, n):
        beta.append(off[k] * alpha[k - 1] * alpha[k - 1])
        alpha.append(1.0 / (diag[k] - beta[k - 1] / alpha[k - 1]))
    one = jnp.ones_like(zero)
    res, way, sol = [one], [one], [zero] * n
    for k in range(n):
        for i in range(k + 1):
            sol[i] = sol[i] + alpha[k] * way[i]
        if k < n - 1:
            res = res + [zero]
            for i in range(k + 1):
                res[i + 1] = res[i + 1] - alpha[k] * way[i]
            way = [res[i] + (beta[k] * way[i] if i <= k else 0.0) for i in range(k + 2)]
    return sol


EDGES = ((1, 0), (-1, 0), (1, 1), (1, -1), (-1, 1), (-1, -1))
HALO = EDGES + ((0, 1), (0, -1))


def along(matrix, v):
    even = [v[k] + v[7 - k] for k in range(4)]
    odd = [v[k] - v[7 - k] for k in range(4)]
    first, last = [], []
    for i in range(4):
        same = [0.5 * float(matrix[i, k] + matrix[i, 7 - k]) for k in range(4)]
        flip = [0.5 * float(matrix[i, k] - matrix[i, 7 - k]) for k in range(4)]
        p = (same[0] * even[0] + same[1] * even[1]) + (same[2] * even[2] + same[3] * even[3])
        q = (flip[0] * odd[0] + flip[1] * odd[1]) + (flip[2] * odd[2] + flip[3] * odd[3])
        first.append(p + q)
        last.append(q - p)
    return first + last[::-1]


def cut(x):
    high = x.astype(BF16)
    return high, (x - high.astype(F32)).astype(BF16)


def ends_middle(low, high):
    half = iota(low.shape, 1) < 64
    return jnp.where(half, low, high), jnp.where(half, high, low)


def kernel(
    n_slab,
    n_chan,
    u_hbm,
    index_hbm,
    prev_hbm,
    source_hbm,
    flag_hbm,
    ply_hbm,
    forward_hbm,
    backward_hbm,
    lap_hbm,
    both_hbm,
    volume_hbm,
    new_ref,
    out_ref,
    u_ref,
    index_ref,
    prev_ref,
    source_ref,
    flag_ref,
    ply_ref,
    fwd_st,
    bwd_st,
    lap_st,
    both_r,
    volume_ref,
    speed_grad,
    lap,
    cond,
    own_pack,
    put_pack,
    got_pack,
    basis,
    kap,
    mix_ref,
    inv_mult,
    grad,
    ysum,
    flux,
    acc,
    edge_out,
    edge_in,
    side_out,
    side_in,
    chan_sum,
    slab_sum,
    load_sem,
    pack_send,
    pack_recv,
    halo_send,
    halo_recv,
    chan_send,
    chan_recv,
    slab_send,
    slab_recv,
):
    slab = lax.axis_index("slab")
    chan = lax.axis_index("chan")
    device = slab * n_chan + chan
    devices = n_slab * n_chan

    def near(ds, dc):
        return (lax.rem(slab + ds + n_slab, n_slab), lax.rem(chan + dc + n_chan, n_chan))

    left, right = pl.ds(0, 256), pl.ds(256, 256)
    loads = [
        pltpu.make_async_copy(src, dst, load_sem.at[k])
        for k, (src, dst) in enumerate(
            (
                (prev_hbm, prev_ref),
                (source_hbm, source_ref),
                (volume_hbm, volume_ref),
                (flag_hbm, flag_ref),
                (ply_hbm, ply_ref),
                (u_hbm.at[:, :, left], u_ref.at[:, :, left]),
                (lap_hbm, lap_st),
                (both_hbm, both_r),
                (forward_hbm, fwd_st.at[:, pl.ds(0, 512)]),
                (u_hbm.at[:, :, right], u_ref.at[:, :, right]),
                (forward_hbm.at[:, pl.ds(0, 256)], fwd_st.at[:, pl.ds(512, 256)]),
                (backward_hbm, bwd_st.at[:, pl.ds(0, 1024)]),
                (backward_hbm.at[:, pl.ds(0, 512)], bwd_st.at[:, pl.ds(1024, 512)]),
                (index_hbm, index_ref),
            )
        )
    ]
    loads[13].start()
    for load in loads[:13]:
        load.start()

    barrier = pltpu.get_barrier_semaphore()
    greet = [near(*d) for d in HALO]
    greet += [(slab, lax.rem(chan + j, n_chan)) for j in range(2, n_chan - 1)]
    greet += [(lax.rem(slab + j, n_slab), chan) for j in range(2, n_slab - 1)]
    for peer in greet:
        pl.semaphore_signal(barrier, inc=1, device_id=peer, device_id_type=MESH)

    loads[13].wait()
    target = index_ref[...]
    slot = target & 511
    distance = ((target >> 9) - device) & (devices - 1)
    group = jnp.where(
        distance == 1,
        1,
        jnp.where(distance == devices - 1, 2, jnp.where(distance == n_chan, 3, 0)),
    )
    member = iota((8, 512), 0) == group
    before = (iota((512, 512), 0) < iota((512, 512), 1)).astype(F32).astype(BF16)
    rank = dot(member.astype(F32).astype(BF16), before)
    begin = jnp.where(iota((8, 512), 0) == 0, 0, 128 + 128 * iota((8, 512), 0)).astype(F32)
    position = jnp.sum(jnp.where(member, rank + begin, 0.0), axis=0, keepdims=True).astype(jnp.int32)
    code = jnp.where(
        iota((16, 512), 0) == 0,
        (slot >> 5) + 1,
        jnp.where(iota((16, 512), 0) == 1, slot & 31, 0),
    )
    cond[512:528] = code.astype(F32).astype(BF16)

    for load in loads[:5]:
        load.wait()
    for l in range(2):
        halves = []
        for h in range(2):
            rows = pl.ds(2 * h + l, 512, stride=4)
            halves.append(volume_ref[...] * (0.05 * prev_ref[rows, :] + source_ref[rows, :]))
        for m, value in enumerate(ends_middle(*halves)):
            basis[0, :, :, :, pl.ds(256 * m + 128 * l, 128)] = value.reshape(8, 8, 8, 128)
    damping = []
    mixing = []
    for l in range(2):
        flag = flag_ref[pl.ds(l, 1)]
        ply = ply_ref[pl.ds(l, 1)].astype(F32)
        damp = jnp.where(flag == 1, 1.0 / (1.0 + 0.25 * ply), 1.0) * (1.0 / SCALE)
        mix = 0.4 * flag.astype(F32) * ply / (ply + 1.0)
        wide = [jnp.broadcast_to(x, (8, 256)) for x in (damp, mix)]
        damping.append(ends_middle(wide[0][:, :128], wide[0][:, 128:]))
        mixing.append(ends_middle(wide[1][:, :128], wide[1][:, 128:]))
    damping = [damping[l][m][0:1] for m in range(2) for l in range(2)]
    mixing = [mixing[l][m] for m in range(2) for l in range(2)]
    for tile in range(4):
        mix_ref[:, pl.ds(128 * tile, 128)] = mixing[tile]

    def fluid(block):
        lane = pl.ds(256 * block, 256)
        for c in range(3):
            flat = u_ref[pl.ds(64 * c, 64), :, lane].astype(F32).reshape(512, 256)
            low = flat.astype(BF16)
            for h in range(2):
                rows = pl.ds(256 * h, 256)
                part = low[256 * h : 256 * h + 256]
                both = dot(fwd_st[:, 0:256], part)
                speed_grad[c, 1, rows, lane] = both[:256]
                speed_grad[c, 2, rows, lane] = both[256:]
                lap[c, rows, lane] = dot(lap_st[...], part)
            by_r = flat.reshape(8, 64, 256)
            for q in range(2):
                part = by_r[:, 32 * q : 32 * q + 32].reshape(256, 256).astype(BF16)
                both = dot(both_r[...], part).reshape(16, 32, 256)
                for r in range(8):
                    rows = pl.ds(64 * r + 32 * q, 32)
                    speed_grad[c, 0, rows, lane] = both[r]
                    lap[c, rows, lane] += both[8 + r]
            for n in range(32):
                for tile in range(2):
                    part = pl.ds(256 * block + 128 * tile, 128)
                    rows = pl.ds(16 * n, 16)
                    u = [u_ref[pl.ds(64 * k + 2 * n, 2), :, part].astype(F32).reshape(16, 128) for k in range(3)]
                    turn = (
                        u[0] * speed_grad[c, 0, rows, part]
                        + u[1] * speed_grad[c, 1, rows, part]
                        + u[2] * speed_grad[c, 2, rows, part]
                    )
                    new = ((u[c] + lap[c, rows, part]) - 0.01 * turn).astype(BF16).astype(F32)
                    new_ref[pl.ds(64 * c + 2 * n, 2), :, part] = new.reshape(2, 8, 128).astype(BF16)
                    square = new * new if c == 0 else ysum[rows, part] + new * new
                    if c < 2:
                        ysum[rows, part] = square
                    else:
                        cond[rows, part] = (1.0 + 0.5 * square).astype(BF16)

    for load in loads[5:10]:
        load.wait()
    fluid(0)

    lane8 = iota((8, 128), 1)
    has_left = slab > 0
    has_right = slab < n_slab - 1
    has_under = chan > 0
    has_over = chan < n_chan - 1
    has_next = {(1, 0): has_right, (-1, 0): has_left, (0, 1): has_over, (0, -1): has_under}

    def both_of(ds, dc):
        if ds == 0 or dc == 0:
            return has_next[ds, dc]
        return has_next[ds, 0] & has_next[0, dc]

    SIDES = ((0, 1, 0), (0, -1, 0), (0, 1, 1), (0, -1, 1))

    def halo_copies(i, want_edges, want_sides):
        turn = i % 2 if isinstance(i, int) else lax.rem(i, 2)

        def remote(src, dst, number, ds, dc):
            return pltpu.make_async_remote_copy(
                src_ref=src,
                dst_ref=dst,
                send_sem=halo_send.at[turn, number],
                recv_sem=halo_recv.at[turn, number],
                device_id=near(ds, dc),
                device_id_type=MESH,
            )

        edges = [
            (ds, dc, remote(edge_out.at[turn, 0 if ds == 1 else 1], edge_in.at[turn, d], d, ds, dc))
            for d, (ds, dc) in enumerate(EDGES)
            if want_edges
        ]
        sides = []
        for d, (ds, dc, m) in enumerate(SIDES):
            if m not in want_sides:
                continue
            k = 0 if dc == 1 else 1
            sides.append((ds, dc, remote(side_out.at[turn, k, m], side_in.at[turn, k, m], 6 + d, ds, dc)))
        return turn, edges, sides

    def send(copies):
        for ds, dc, copy in copies:
            pl.when(both_of(ds, dc))(copy.start)

    def arrive(copies):
        for ds, dc, copy in copies:
            pl.when(both_of(ds, dc))(copy.wait_send)
            pl.when(both_of(-ds, -dc))(copy.wait_recv)

    def lanes(m, l):
        return pl.ds(256 * m + 128 * l, 128)

    def between(i, m, turn):
        side_out[turn, 0, m] = basis[i, :, 7, :, lanes(m, 1)]
        side_out[turn, 1, m] = basis[i, :, 0, :, lanes(m, 0)]
        both = basis[i, :, 7, :, lanes(m, 0)] + basis[i, :, 0, :, lanes(m, 1)]
        basis[i, :, 7, :, lanes(m, 0)] = both
        basis[i, :, 0, :, lanes(m, 1)] = both

    def start_ends(i):
        turn, edges, sides = halo_copies(i, True, (0,))
        between(i, 0, turn)
        up = jnp.zeros((8, 128), F32)
        down = jnp.zeros((8, 128), F32)
        for l in range(2):
            for s in range(8):
                to = s + 8 * l
                here = lane8 == to
                up = jnp.where(here, pltpu.roll(basis[i, 7, s, :, lanes(0, l)], (to - 127) % 128, 1), up)
                down = jnp.where(here, pltpu.roll(basis[i, 0, s, :, lanes(0, l)], to, 1), down)
        edge_out[turn, 0] = up
        edge_out[turn, 1] = down
        send(edges)
        send(sides)

    def start_middle(i):
        turn, edges, sides = halo_copies(i, False, (1,))
        between(i, 1, turn)
        send(sides)

    def finish_sides(i):
        turn, edges, sides = halo_copies(i, False, (0, 1))
        arrive(sides)
        for k, (has, s, l) in enumerate(((has_under, 0, 0), (has_over, 7, 1))):
            for m in range(2):
                basis[i, :, s, :, lanes(m, l)] += jnp.where(has, side_in[turn, k, m], 0.0)
        j = iota((64, 128), 1)
        for l in range(2):
            high = [basis[i, 7, :, :, lanes(m, l)].reshape(64, 128) for m in range(2)]
            low = [basis[i, 0, :, :, lanes(m, l)].reshape(64, 128) for m in range(2)]
            ahead = [pltpu.roll(x, 127, 1) for x in low]
            behind = [pltpu.roll(x, 1, 1) for x in high]
            for m in range(2):
                more = jnp.where(j == 63, ahead[1 - m], ahead[m])
                less = jnp.where(j == 64, behind[1 - m], behind[m])
                if m == 0:
                    more = jnp.where(j == 127, 0.0, more)
                    less = jnp.where(j == 0, 0.0, less)
                basis[i, 7, :, :, lanes(m, l)] = (high[m] + more).reshape(8, 8, 128)
                basis[i, 0, :, :, lanes(m, l)] = (low[m] + less).reshape(8, 8, 128)

    deriv = gll()[0]

    def finish_edges(i):
        turn, edges, sides = halo_copies(i, True, ())
        arrive(edges)
        first = lane8 == 0
        last = lane8 == 127

        def lines(at, slot_left, slot_right, has):
            left_ok = has_left if has is None else has_left & has
            right_ok = has_right if has is None else has_right & has
            return (
                jnp.where(first & left_ok, pltpu.roll(edge_in[turn, slot_left], (128 - at) % 128, 1), 0.0),
                jnp.where(last & right_ok, pltpu.roll(edge_in[turn, slot_right], (127 - at) % 128, 1), 0.0),
            )

        corner = {
            (0, 0): lines(15, EDGES.index((1, 1)), EDGES.index((-1, 1)), has_under),
            (1, 7): lines(0, EDGES.index((1, -1)), EDGES.index((-1, -1)), has_over),
        }
        slope = [jnp.where(last, float(deriv[r, 7]), float(deriv[r, 0])) for r in range(8)]
        for l in range(2):
            starts, ends = [], []
            for s in range(8):
                low, high = lines(s + 8 * l, EDGES.index((1, 0)), EDGES.index((-1, 0)), None)
                if (l, s) in corner:
                    low, high = low + corner[l, s][0], high + corner[l, s][1]
                starts.append(low)
                ends.append(high)
                basis[i, 0, s, :, lanes(0, l)] += low
                basis[i, 7, s, :, lanes(0, l)] += high
                both = low + high
                for r in range(8):
                    grad[0, pl.ds(64 * r + 8 * s, 8), lanes(0, l)] += slope[r] * both
            for r, face in ((0, along(deriv, starts)), (7, along(deriv, ends))):
                for s in range(8):
                    grad[1, pl.ds(64 * r + 8 * s, 8), lanes(0, l)] += face[s]
        faces = jnp.concatenate(
            [basis[i, r, :, :, 0:256].reshape(64, 256) for r in (0, 7)], 1
        )
        high, low = cut(faces)
        main, rest = fwd_st[256:320, 0:64], fwd_st[256:320, 256:320]
        value = dot(main, high) + (dot(rest, high) + dot(main, low))
        grad[2, 0:64, 0:256] = value[:, :256]
        grad[2, 448:512, 0:256] = value[:, 256:]

    fluid(1)
    pl.semaphore_wait(barrier, len(greet))
    start_ends(0)
    start_middle(0)

    def packed(start, count):
        chosen = (iota((count, 512), 0) + start == position).astype(F32).astype(BF16)
        return dot(cond[...], chosen, NT).astype(BF16)

    def device_at(step):
        number = lax.rem(device + step + devices, devices)
        return (number // n_chan, lax.rem(number, n_chan))

    moves = [
        pltpu.make_async_remote_copy(
            src_ref=put_pack.at[k],
            dst_ref=got_pack.at[k],
            send_sem=pack_send.at[k],
            recv_sem=pack_recv.at[k],
            device_id=device_at(step),
            device_id_type=MESH,
        )
        for k, step in enumerate((n_chan, 1, -1))
    ]
    late = packed(512, 128)
    put_pack[0] = late
    moves[0].start()
    soon = packed(256, 256)
    put_pack[1] = soon[:, :128]
    put_pack[2] = soon[:, 128:]
    moves[1].start()
    moves[2].start()
    own_pack[...] = packed(0, 256)

    def place(block):
        code = block[512:528].astype(F32)
        slot = ((code[0:1] - 1.0) * 32.0 + code[1:2]).astype(jnp.int32)
        lane = iota((512, block.shape[1]), 0)
        here = lane & 127
        axial = here + jnp.where((lane < 256) == (here < 64), 0, 128)
        chosen = (((lane >> 7) & 1) * 256 + axial == slot).astype(F32).astype(BF16)
        return dot(block[0:512], chosen, NT)

    kap[...] = place(own_pack[...])
    node = iota((512, 128), 0)
    at_r = node >> 6
    at_s = (node >> 3) & 7
    for m in range(2):
        for l in range(2):
            here = iota((512, 128), 1)
            axial = slab * 256 + here + jnp.where(here < 64, 128 * m, 128 - 128 * m)
            m_r = jnp.where(((at_r == 0) & (axial > 0)) | ((at_r == 7) & (axial < n_slab * 256 - 1)), 0.5, 1.0)
            lateral = chan * 2 + l
            m_s = jnp.where(((at_s == 0) & (lateral > 0)) | ((at_s == 7) & (lateral < n_chan * 2 - 1)), 0.5, 1.0)
            inv_mult[:, lanes(m, l)] = m_r * m_s


    spare = lax.div(slab, n_slab)

    def gradient(i, block):
        lane = pl.ds(256 * block, 256)
        pairs = [cut(basis[i, 4 * h : 4 * h + 4, :, :, lane].reshape(256, 256)) for h in range(2)]

        def turn(h):
            high, low = pairs[h]
            both = dot(fwd_st[...], jnp.concatenate([high, high, low], 0))
            grad[1, pl.ds(256 * h, 256), lane] = both[:256]
            grad[2, pl.ds(256 * h, 256), lane] = both[256:]
            return both

        basis[ITERS + spare, 0, 0, :, 0:128] = turn(0)[0:8, 0:128]
        for s in range(8):
            for tile in range(2):
                part = pl.ds(256 * block + 128 * tile, 128)
                out = along(deriv, [basis[i, r, s, :, part] for r in range(8)])
                for r in range(8):
                    grad[0, pl.ds(64 * r + 8 * s, 8), part] = out[r]
        turn(1)

    def fold(x):
        total = jnp.sum(x.reshape(x.shape[0] // 8, 8, 256), axis=0)
        return total[:, :128] + total[:, 128:]

    def norm(i):
        totals = [None] * 4
        for n in range(64):
            for tile in range(4):
                part = pl.ds(128 * tile, 128)
                v = basis[i, n // 8, n % 8, :, part]
                term = v * v * inv_mult[pl.ds(8 * n, 8), part]
                totals[tile] = term if n == 0 else totals[tile] + term
        acc[2 * i] = (totals[0] + totals[1]) + (totals[2] + totals[3])

    def power(i, block):
        lane = pl.ds(256 * block, 256)
        mix = mix_ref[0:1, lane]

        def stage(h):
            rows = pl.ds(256 * h, 256)
            k = kap[rows, lane]
            k1 = k * grad[0, rows, lane]
            k2 = k * grad[1, rows, lane]
            flux[0, rows] = k1 + mix * k2
            h2, l2 = cut(k2 + mix * k1)
            h3, l3 = cut(k * grad[2, rows, lane])
            return jnp.concatenate([h2, h3, h2, h3, l2, l3], 0)

        staged = [stage(h) for h in range(2)]
        for h in range(2):
            value = dot(bwd_st[...], staged[h])
            ysum[pl.ds(256 * h, 256), lane] = value
            if h == 0:
                flux[1 + spare, 0:8, 0:128] = value[0:8, 0:128]
                for s in range(8):
                    for tile in range(2):
                        part = pl.ds(128 * tile, 128)
                        out = along(deriv.T, [flux[0, pl.ds(64 * r + 8 * s, 8), part] for r in range(8)])
                        for r in range(8):
                            flux[0, pl.ds(64 * r + 8 * s, 8), part] = out[r]
        total = None
        for h in range(2):
            rows = pl.ds(256 * h, 256)
            field = basis[i, 4 * h : 4 * h + 4, :, :, lane].reshape(256, 256)
            v = volume_ref[rows] * (0.05 / SCALE)
            value = ysum[rows, lane] + flux[0, rows] + jnp.concatenate([v, v], 1) * field
            basis[i + 1, 4 * h : 4 * h + 4, :, :, lane] = value.reshape(4, 8, 8, 256)
            part = fold(value * field)
            total = part if total is None else total + part
        return total

    for load in loads[10:13]:
        load.wait()
    finish_sides(0)
    gradient(0, 1)
    gradient(0, 0)
    finish_edges(0)
    moves[1].wait()
    moves[2].wait()
    kap[...] += place(jnp.concatenate([got_pack[1], got_pack[2]], 1))
    moves[0].wait()
    last_part = place(got_pack[0])
    for tile in range(4):
        lane = pl.ds(128 * tile, 128)
        kap[:, lane] = (
            volume_ref[...]
            * (kap[:, lane] + last_part[:, 128 * tile : 128 * tile + 128])
            * damping[tile]
        )

    def body(i, carry):
        ends = power(i, 0)
        start_ends(i + 1)
        acc[2 * i + 1] = ends + power(i, 1)
        start_middle(i + 1)
        norm(i)
        finish_sides(i + 1)
        gradient(i + 1, 1)
        gradient(i + 1, 0)
        finish_edges(i + 1)
        return carry

    lax.fori_loop(0, ITERS - 1, body, 0)

    final = ITERS - 1
    norm(final)
    totals = [None] * 4
    twice = [2.0 * mix_ref[:, pl.ds(128 * tile, 128)] for tile in range(4)]
    for n in range(64):
        eight = pl.ds(8 * n, 8)
        v5 = volume_ref[eight, :] * (0.05 / SCALE)
        for tile in range(4):
            part = pl.ds(128 * tile, 128)
            g1, g2, g3 = grad[0, eight, part], grad[1, eight, part], grad[2, eight, part]
            v = basis[final, n // 8, n % 8, :, part]
            term = kap[eight, part] * (g1 * (g1 + twice[tile] * g2) + (g2 * g2 + g3 * g3)) + v5 * (v * v)
            totals[tile] = term if n == 0 else totals[tile] + term
    acc[2 * final + 1] = (totals[0] + totals[1]) + (totals[2] + totals[3])

    rows = [jnp.sum(acc[k], axis=0, keepdims=True) for k in range(2 * ITERS)]
    rows = jnp.concatenate(rows + [jnp.zeros((6, 128), F32)], 0)
    mine = jnp.sum(rows, axis=1, keepdims=True)
    message = jnp.sum(jnp.where(iota((16, 128), 0) == iota((16, 128), 1), mine, 0.0), axis=0, keepdims=True)

    def everyone(message, sums, me, count, sends, recvs, peer):
        sums[me] = message
        copies = [
            pltpu.make_async_remote_copy(
                src_ref=sums.at[me],
                dst_ref=sums.at[me],
                send_sem=sends.at[j],
                recv_sem=recvs.at[j],
                device_id=peer(lax.rem(me + j, count)),
                device_id_type=MESH,
            )
            for j in range(1, count)
        ]
        for copy in copies:
            copy.start()
        for copy in copies:
            copy.wait()
        total = sums[0]
        for j in range(1, count):
            total = total + sums[j]
        return total

    message = everyone(message, chan_sum, chan, n_chan, chan_send, chan_recv, lambda c: (slab, c))
    message = everyone(message, slab_sum, slab, n_slab, slab_send, slab_recv, lambda s: (s, chan))
    lane1 = iota((1, 128), 1)
    moment = [
        jnp.sum(jnp.where(lane1 == k, message, 0.0), axis=1, keepdims=True) for k in range(2 * ITERS)
    ]
    weight = [w * (1.0 / SCALE) for w in krylov_weights(moment)]
    full = [jnp.broadcast_to(w, (8, 128)) for w in weight]
    for r in range(8):
        for s in range(8):
            for l in range(2):
                pieces = []
                for m in range(2):
                    total = full[0] * basis[0, r, s, :, lanes(m, l)]
                    for i in range(1, ITERS):
                        total = total + full[i] * basis[i, r, s, :, lanes(m, l)]
                    pieces.append(total)
                for h, total in enumerate(ends_middle(*pieces)):
                    out_ref[pl.ds(256 * r + 32 * s + 2 * h + l, 8, stride=4), :] = total


def flush_kernel(new_ref, out_ref, new_hbm, out_hbm, sem):
    first = pltpu.make_async_copy(new_ref, new_hbm, sem.at[0])
    second = pltpu.make_async_copy(out_ref, out_hbm, sem.at[1])
    first.start()
    second.start()
    first.wait()
    second.wait()


def step(u, index, prev, source, flags, plies, ops):
    n_slab, n_chan = lax.axis_size("slab"), lax.axis_size("chan")
    anywhere = pl.BlockSpec(memory_space=pl.ANY)
    vmem = pl.BlockSpec(memory_space=pltpu.VMEM)
    dma = pltpu.SemaphoreType.DMA
    new, warmth = pl.pallas_call(
        functools.partial(kernel, n_slab, n_chan),
        in_specs=[anywhere] * 11,
        out_specs=[vmem, vmem],
        out_shape=[
            pltpu.MemorySpace.VMEM((192, 8, 512), BF16),
            pltpu.MemorySpace.VMEM((2048, 128), F32),
        ],
        scratch_shapes=[
            pltpu.VMEM((192, 8, 512), BF16),
            pltpu.VMEM((1, 512), jnp.int32),
            pltpu.VMEM((2048, 128), F32),
            pltpu.VMEM((2048, 128), F32),
            pltpu.VMEM((2, 256), jnp.int32),
            pltpu.VMEM((2, 256), jnp.int32),
            pltpu.VMEM((512, 768), BF16),
            pltpu.VMEM((256, 1536), BF16),
            pltpu.VMEM((256, 256), BF16),
            pltpu.VMEM((512, 256), BF16),
            pltpu.VMEM((512, 128), F32),
            pltpu.VMEM((3, 3, 512, 512), F32),
            pltpu.VMEM((3, 512, 512), F32),
            pltpu.VMEM((528, 512), BF16),
            pltpu.VMEM((528, 256), BF16),
            pltpu.VMEM((3, 528, 128), BF16),
            pltpu.VMEM((3, 528, 128), BF16),
            pltpu.VMEM((ITERS + 1, 8, 8, 8, 512), F32),
            pltpu.VMEM((512, 512), F32),
            pltpu.VMEM((8, 512), F32),
            pltpu.VMEM((512, 512), F32),
            pltpu.VMEM((3, 512, 512), F32),
            pltpu.VMEM((512, 512), F32),
            pltpu.VMEM((2, 512, 256), F32),
            pltpu.VMEM((2 * ITERS, 8, 128), F32),
            pltpu.VMEM((2, 2, 8, 128), F32),
            pltpu.VMEM((2, 6, 8, 128), F32),
            pltpu.VMEM((2, 2, 2, 8, 8, 128), F32),
            pltpu.VMEM((2, 2, 2, 8, 8, 128), F32),
            pltpu.VMEM((n_chan, 1, 128), F32),
            pltpu.VMEM((n_slab, 1, 128), F32),
            dma((14,)),
            dma((3,)),
            dma((3,)),
            dma((2, 10)),
            dma((2, 10)),
            dma((n_chan,)),
            dma((n_chan,)),
            dma((n_slab,)),
            dma((n_slab,)),
        ],
        compiler_params=pltpu.CompilerParams(
            collective_id=0, has_side_effects=True
        ),
        name="step",
    )(
        u,
        index,
        prev,
        source,
        flags,
        plies,
        ops["forward"],
        ops["backward"],
        ops["lap_st"],
        ops["both_r"],
        ops["volume"],
    )
    new, warmth = pl.pallas_call(
        flush_kernel,
        in_specs=[vmem, vmem],
        out_specs=[anywhere, anywhere],
        out_shape=[
            jax.ShapeDtypeStruct((192, 8, 512), BF16),
            jax.ShapeDtypeStruct((2048, 128), F32),
        ],
        scratch_shapes=[dma((2,))],
        name="flush",
    )(
        pltpu.with_memory_space_constraint(new, pltpu.VMEM),
        pltpu.with_memory_space_constraint(warmth, pltpu.VMEM),
    )
    return new, warmth


def lanes_first(x):
    return x.reshape(512, 2, 2, 128).transpose(0, 2, 1, 3).reshape(2048, 128)


def on_device(u, index, prev, source, flags, plies):
    ops = operators()
    stepped, warmth = step(
        u.reshape(192, 8, 512),
        index.reshape(1, 512),
        lanes_first(prev),
        lanes_first(source),
        flags,
        plies,
        ops,
    )
    warmth = warmth.reshape(512, 2, 2, 128).transpose(0, 2, 1, 3).reshape(8, 8, 8, 2, 256)
    return stepped.reshape(3, 8, 8, 8, 512), warmth


def solution(mesh):
    in_specs = (
        P(None, None, None, None, ("slab", "chan")),
        P(("slab", "chan")),
        P(None, None, None, "chan", "slab"),
        P(None, None, None, "chan", "slab"),
        P("chan", "slab"),
        P("chan", "slab"),
    )
    out_specs = (P(None, None, None, None, ("slab", "chan")), P(None, None, None, "chan", "slab"))
    return jax.shard_map(
        on_device, mesh=mesh, in_specs=in_specs, out_specs=out_specs, check_vma=False
    )
```

```python
import functools

import jax
import jax.numpy as jnp
import numpy as np
from jax import lax
from jax.experimental import pallas as pl
from jax.experimental.pallas import tpu as pltpu
from jax.sharding import PartitionSpec as P

F32 = jnp.float32
BF16 = jnp.bfloat16
MESH = pl.DeviceIdType.MESH
ITERS = 5
SCALE = 64.0
NT = (((1,), (1,)), ((), ()))
NN = (((1,), (0,)), ((), ()))


def gll():
    points = np.array(
        [
            -1.0,
            -0.8717401485096066,
            -0.5917001814331423,
            -0.2092992179024789,
            0.2092992179024789,
            0.5917001814331423,
            0.8717401485096066,
            1.0,
        ]
    )
    weights = np.array(
        [
            1.0 / 28.0,
            0.2107042271435061,
            0.3411226924835044,
            0.4124587946587038,
            0.4124587946587038,
            0.3411226924835044,
            0.2107042271435061,
            1.0 / 28.0,
        ]
    )
    low = np.ones(8)
    high = points.copy()
    for degree in range(1, 7):
        low, high = high, ((2 * degree + 1) * points * high - degree * low) / (degree + 1)
    gaps = points[:, None] - points[None, :] + np.eye(8)
    deriv = high[:, None] / (high[None, :] * gaps)
    deriv = deriv * (1.0 - np.eye(8))
    deriv[0, 0] = -14.0
    deriv[7, 7] = 14.0
    return deriv, weights


def two(matrix):
    high = np.asarray(matrix, np.float32).astype(BF16).astype(np.float64)
    return high, matrix - high


def operators():
    deriv, weights = gll()
    second = deriv @ deriv
    eye = np.eye
    kron = np.kron
    along_s = kron(eye(4), kron(deriv, eye(8)))
    along_t = kron(eye(32), deriv)
    along_r = kron(deriv, eye(32))
    ds_hi, ds_lo = two(along_s)
    dt_hi, dt_lo = two(along_t)
    forward = np.block([[ds_hi, ds_lo], [dt_hi, dt_lo]])
    backward = np.block([[ds_hi.T, dt_hi.T, ds_lo.T, dt_lo.T]])
    lap_st = 0.0002 * (kron(eye(4), kron(second, eye(8))) + kron(eye(32), second))
    both_r = np.block([[along_r], [0.0002 * kron(second, eye(32))]])
    volume = (weights[:, None, None] * weights[None, :, None] * weights[None, None, :]).reshape(512, 1)
    cast = lambda m: jnp.asarray(np.asarray(m, np.float32).astype(BF16))
    return {
        "forward": cast(forward),
        "backward": cast(backward),
        "lap_st": cast(lap_st),
        "both_r": cast(both_r),
        "volume": jnp.asarray(np.broadcast_to(volume, (512, 128)), F32),
    }


def dot(a, b, dims=NN):
    return lax.dot_general(a, b, dims, preferred_element_type=F32)


def iota(shape, dim):
    return lax.broadcasted_iota(jnp.int32, shape, dim)


def krylov_weights(m):
    n = ITERS
    zero = jnp.zeros_like(m[0])
    older, newer = [zero] * (2 * n), list(m)
    diag = [newer[1] / newer[0]]
    off = [zero]
    for k in range(1, n):
        fresh = [zero] * (2 * n)
        for l in range(k, 2 * n - k):
            fresh[l] = newer[l + 1] - diag[k - 1] * newer[l] - off[k - 1] * older[l]
        diag.append(fresh[k + 1] / fresh[k] - newer[k] / newer[k - 1])
        off.append(fresh[k] / newer[k - 1])
        older, newer = newer, fresh
    alpha = [1.0 / diag[0]]
    beta = []
    for k in range(1, n):
        beta.append(off[k] * alpha[k - 1] * alpha[k - 1])
        alpha.append(1.0 / (diag[k] - beta[k - 1] / alpha[k - 1]))
    one = jnp.ones_like(zero)
    res, way, sol = [one], [one], [zero] * n
    for k in range(n):
        for i in range(k + 1):
            sol[i] = sol[i] + alpha[k] * way[i]
        if k < n - 1:
            res = res + [zero]
            for i in range(k + 1):
                res[i + 1] = res[i + 1] - alpha[k] * way[i]
            way = [res[i] + (beta[k] * way[i] if i <= k else 0.0) for i in range(k + 2)]
    return sol


EDGES = ((1, 0), (-1, 0), (1, 1), (1, -1), (-1, 1), (-1, -1))
HALO = EDGES + ((0, 1), (0, -1))


def along(matrix, v):
    even = [v[k] + v[7 - k] for k in range(4)]
    odd = [v[k] - v[7 - k] for k in range(4)]
    first, last = [], []
    for i in range(4):
        same = [0.5 * float(matrix[i, k] + matrix[i, 7 - k]) for k in range(4)]
        flip = [0.5 * float(matrix[i, k] - matrix[i, 7 - k]) for k in range(4)]
        p = (same[0] * even[0] + same[1] * even[1]) + (same[2] * even[2] + same[3] * even[3])
        q = (flip[0] * odd[0] + flip[1] * odd[1]) + (flip[2] * odd[2] + flip[3] * odd[3])
        first.append(p + q)
        last.append(q - p)
    return first + last[::-1]


def cut(x):
    high = x.astype(BF16)
    return high, (x - high.astype(F32)).astype(BF16)


def ends_middle(low, high):
    half = iota(low.shape, 1) < 64
    return jnp.where(half, low, high), jnp.where(half, high, low)


def kernel(
    n_slab,
    n_chan,
    u_hbm,
    index_hbm,
    prev_hbm,
    source_hbm,
    flag_hbm,
    ply_hbm,
    forward_hbm,
    backward_hbm,
    lap_hbm,
    both_hbm,
    volume_hbm,
    new_ref,
    out_ref,
    u_ref,
    index_ref,
    prev_ref,
    source_ref,
    flag_ref,
    ply_ref,
    fwd_st,
    bwd_st,
    lap_st,
    both_r,
    volume_ref,
    speed_grad,
    lap,
    cond,
    own_pack,
    put_pack,
    got_pack,
    basis,
    kap,
    mix_ref,
    inv_mult,
    grad,
    ysum,
    flux,
    acc,
    edge_out,
    edge_in,
    side_out,
    side_in,
    chan_sum,
    slab_sum,
    load_sem,
    pack_send,
    pack_recv,
    halo_send,
    halo_recv,
    chan_send,
    chan_recv,
    slab_send,
    slab_recv,
):
    slab = lax.axis_index("slab")
    chan = lax.axis_index("chan")
    device = slab * n_chan + chan
    devices = n_slab * n_chan

    def near(ds, dc):
        return (lax.rem(slab + ds + n_slab, n_slab), lax.rem(chan + dc + n_chan, n_chan))

    left, right = pl.ds(0, 256), pl.ds(256, 256)
    loads = [
        pltpu.make_async_copy(src, dst, load_sem.at[k])
        for k, (src, dst) in enumerate(
            (
                (prev_hbm, prev_ref),
                (source_hbm, source_ref),
                (volume_hbm, volume_ref),
                (flag_hbm, flag_ref),
                (ply_hbm, ply_ref),
                (u_hbm.at[:, :, left], u_ref.at[:, :, left]),
                (lap_hbm, lap_st),
                (both_hbm, both_r),
                (forward_hbm, fwd_st.at[:, pl.ds(0, 512)]),
                (u_hbm.at[:, :, right], u_ref.at[:, :, right]),
                (forward_hbm.at[:, pl.ds(0, 256)], fwd_st.at[:, pl.ds(512, 256)]),
                (backward_hbm, bwd_st.at[:, pl.ds(0, 1024)]),
                (backward_hbm.at[:, pl.ds(0, 512)], bwd_st.at[:, pl.ds(1024, 512)]),
                (index_hbm, index_ref),
            )
        )
    ]
    loads[13].start()
    for load in loads[:13]:
        load.start()

    barrier = pltpu.get_barrier_semaphore()
    greet = [near(*d) for d in HALO]
    greet += [(slab, lax.rem(chan + j, n_chan)) for j in range(2, n_chan - 1)]
    greet += [(lax.rem(slab + j, n_slab), chan) for j in range(2, n_slab - 1)]
    for peer in greet:
        pl.semaphore_signal(barrier, inc=1, device_id=peer, device_id_type=MESH)

    loads[13].wait()
    target = index_ref[...]
    slot = target & 511
    distance = ((target >> 9) - device) & (devices - 1)
    group = jnp.where(
        distance == 1,
        1,
        jnp.where(distance == devices - 1, 2, jnp.where(distance == n_chan, 3, 0)),
    )
    member = iota((8, 512), 0) == group
    before = (iota((512, 512), 0) < iota((512, 512), 1)).astype(F32).astype(BF16)
    rank = dot(member.astype(F32).astype(BF16), before)
    begin = jnp.where(iota((8, 512), 0) == 0, 0, 128 + 128 * iota((8, 512), 0)).astype(F32)
    position = jnp.sum(jnp.where(member, rank + begin, 0.0), axis=0, keepdims=True).astype(jnp.int32)
    code = jnp.where(
        iota((16, 512), 0) == 0,
        (slot >> 5) + 1,
        jnp.where(iota((16, 512), 0) == 1, slot & 31, 0),
    )
    cond[512:528] = code.astype(F32).astype(BF16)

    for load in loads[:5]:
        load.wait()
    for l in range(2):
        halves = []
        for h in range(2):
            rows = pl.ds(2 * h + l, 512, stride=4)
            halves.append(volume_ref[...] * (0.05 * prev_ref[rows, :] + source_ref[rows, :]))
        for m, value in enumerate(ends_middle(*halves)):
            basis[0, :, :, :, pl.ds(256 * m + 128 * l, 128)] = value.reshape(8, 8, 8, 128)
    damping = []
    mixing = []
    for l in range(2):
        flag = flag_ref[pl.ds(l, 1)]
        ply = ply_ref[pl.ds(l, 1)].astype(F32)
        damp = jnp.where(flag == 1, 1.0 / (1.0 + 0.25 * ply), 1.0) * (1.0 / SCALE)
        mix = 0.4 * flag.astype(F32) * ply / (ply + 1.0)
        wide = [jnp.broadcast_to(x, (8, 256)) for x in (damp, mix)]
        damping.append(ends_middle(wide[0][:, :128], wide[0][:, 128:]))
        mixing.append(ends_middle(wide[1][:, :128], wide[1][:, 128:]))
    damping = [damping[l][m][0:1] for m in range(2) for l in range(2)]
    mixing = [mixing[l][m] for m in range(2) for l in range(2)]
    for tile in range(4):
        mix_ref[:, pl.ds(128 * tile, 128)] = mixing[tile]

    def fluid(block):
        lane = pl.ds(256 * block, 256)
        for c in range(3):
            flat = u_ref[pl.ds(64 * c, 64), :, lane].astype(F32).reshape(512, 256)
            low = flat.astype(BF16)
            for h in range(2):
                rows = pl.ds(256 * h, 256)
                part = low[256 * h : 256 * h + 256]
                both = dot(fwd_st[:, 0:256], part)
                speed_grad[c, 1, rows, lane] = both[:256]
                speed_grad[c, 2, rows, lane] = both[256:]
                lap[c, rows, lane] = dot(lap_st[...], part)
            by_r = flat.reshape(8, 64, 256)
            for q in range(2):
                part = by_r[:, 32 * q : 32 * q + 32].reshape(256, 256).astype(BF16)
                both = dot(both_r[...], part).reshape(16, 32, 256)
                for r in range(8):
                    rows = pl.ds(64 * r + 32 * q, 32)
                    speed_grad[c, 0, rows, lane] = both[r]
                    lap[c, rows, lane] += both[8 + r]
            for n in range(32):
                for tile in range(2):
                    part = pl.ds(256 * block + 128 * tile, 128)
                    rows = pl.ds(16 * n, 16)
                    u = [u_ref[pl.ds(64 * k + 2 * n, 2), :, part].astype(F32).reshape(16, 128) for k in range(3)]
                    turn = (
                        u[0] * speed_grad[c, 0, rows, part]
                        + u[1] * speed_grad[c, 1, rows, part]
                        + u[2] * speed_grad[c, 2, rows, part]
                    )
                    new = ((u[c] + lap[c, rows, part]) - 0.01 * turn).astype(BF16).astype(F32)
                    new_ref[pl.ds(64 * c + 2 * n, 2), :, part] = new.reshape(2, 8, 128).astype(BF16)
                    square = new * new if c == 0 else ysum[rows, part] + new * new
                    if c < 2:
                        ysum[rows, part] = square
                    else:
                        cond[rows, part] = (1.0 + 0.5 * square).astype(BF16)

    for load in loads[5:10]:
        load.wait()
    fluid(0)

    lane8 = iota((8, 128), 1)
    has_left = slab > 0
    has_right = slab < n_slab - 1
    has_under = chan > 0
    has_over = chan < n_chan - 1
    has_next = {(1, 0): has_right, (-1, 0): has_left, (0, 1): has_over, (0, -1): has_under}

    def both_of(ds, dc):
        if ds == 0 or dc == 0:
            return has_next[ds, dc]
        return has_next[ds, 0] & has_next[0, dc]

    SIDES = ((0, 1, 0), (0, -1, 0), (0, 1, 1), (0, -1, 1))

    def halo_copies(i, want_edges, want_sides):
        turn = i % 2 if isinstance(i, int) else lax.rem(i, 2)

        def remote(src, dst, number, ds, dc):
            return pltpu.make_async_remote_copy(
                src_ref=src,
                dst_ref=dst,
                send_sem=halo_send.at[turn, number],
                recv_sem=halo_recv.at[turn, number],
                device_id=near(ds, dc),
                device_id_type=MESH,
            )

        edges = [
            (ds, dc, remote(edge_out.at[turn, 0 if ds == 1 else 1], edge_in.at[turn, d], d, ds, dc))
            for d, (ds, dc) in enumerate(EDGES)
            if want_edges
        ]
        sides = []
        for d, (ds, dc, m) in enumerate(SIDES):
            if m not in want_sides:
                continue
            k = 0 if dc == 1 else 1
            sides.append((ds, dc, remote(side_out.at[turn, k, m], side_in.at[turn, k, m], 6 + d, ds, dc)))
        return turn, edges, sides

    def send(copies):
        for ds, dc, copy in copies:
            pl.when(both_of(ds, dc))(copy.start)

    def arrive(copies):
        for ds, dc, copy in copies:
            pl.when(both_of(ds, dc))(copy.wait_send)
            pl.when(both_of(-ds, -dc))(copy.wait_recv)

    def lanes(m, l):
        return pl.ds(256 * m + 128 * l, 128)

    def between(i, m, turn):
        side_out[turn, 0, m] = basis[i, :, 7, :, lanes(m, 1)]
        side_out[turn, 1, m] = basis[i, :, 0, :, lanes(m, 0)]
        both = basis[i, :, 7, :, lanes(m, 0)] + basis[i, :, 0, :, lanes(m, 1)]
        basis[i, :, 7, :, lanes(m, 0)] = both
        basis[i, :, 0, :, lanes(m, 1)] = both

    def start_ends(i):
        turn, edges, sides = halo_copies(i, True, (0,))
        between(i, 0, turn)
        up = jnp.zeros((8, 128), F32)
        down = jnp.zeros((8, 128), F32)
        for l in range(2):
            for s in range(8):
                to = s + 8 * l
                here = lane8 == to
                up = jnp.where(here, pltpu.roll(basis[i, 7, s, :, lanes(0, l)], (to - 127) % 128, 1), up)
                down = jnp.where(here, pltpu.roll(basis[i, 0, s, :, lanes(0, l)], to, 1), down)
        edge_out[turn, 0] = up
        edge_out[turn, 1] = down
        send(edges)
        send(sides)

    def start_middle(i):
        turn, edges, sides = halo_copies(i, False, (1,))
        between(i, 1, turn)
        send(sides)

    def local_axial(i):
        j = iota((64, 128), 1)
        for l in range(2):
            high = [basis[i, 7, :, :, lanes(m, l)].reshape(64, 128) for m in range(2)]
            low = [basis[i, 0, :, :, lanes(m, l)].reshape(64, 128) for m in range(2)]
            ahead = [pltpu.roll(x, 127, 1) for x in low]
            behind = [pltpu.roll(x, 1, 1) for x in high]
            for m in range(2):
                more = jnp.where(j == 63, ahead[1 - m], ahead[m])
                less = jnp.where(j == 64, behind[1 - m], behind[m])
                if m == 0:
                    more = jnp.where(j == 127, 0.0, more)
                    less = jnp.where(j == 0, 0.0, less)
                basis[i, 7, :, :, lanes(m, l)] = (high[m] + more).reshape(8, 8, 128)
                basis[i, 0, :, :, lanes(m, l)] = (low[m] + less).reshape(8, 8, 128)

    deriv = gll()[0]

    def finish(i):
        turn, edges, sides = halo_copies(i, True, (0, 1))
        arrive(sides)
        arrive(edges)
        first = lane8 == 0
        last = lane8 == 127

        def lines(at, slot_left, slot_right, has):
            left_ok = has_left if has is None else has_left & has
            right_ok = has_right if has is None else has_right & has
            return (
                jnp.where(first & left_ok, pltpu.roll(edge_in[turn, slot_left], (128 - at) % 128, 1), 0.0),
                jnp.where(last & right_ok, pltpu.roll(edge_in[turn, slot_right], (127 - at) % 128, 1), 0.0),
            )

        for k, (has, s, l, at, dc) in enumerate(((has_under, 0, 0, 15, 1), (has_over, 7, 1, 0, -1))):
            face = [[jnp.where(has, side_in[turn, k, m, r], 0.0) for r in range(8)] for m in range(2)]
            ahead = [pltpu.roll(face[m][0], 127, 1) for m in range(2)]
            behind = [pltpu.roll(face[m][7], 1, 1) for m in range(2)]
            low, high = lines(at, EDGES.index((1, dc)), EDGES.index((-1, dc)), has)
            for m in range(2):
                more = jnp.where(lane8 == 63, ahead[1 - m], ahead[m])
                less = jnp.where(lane8 == 64, behind[1 - m], behind[m])
                if m == 0:
                    more = jnp.where(last, high, more)
                    less = jnp.where(first, low, less)
                face[m][7] = face[m][7] + more
                face[m][0] = face[m][0] + less
            for m in range(2):
                swept = along(deriv, face[m])
                for r in range(8):
                    basis[i, r, s, :, lanes(m, l)] += face[m][r]
                    grad[0, pl.ds(64 * r + 8 * s, 8), lanes(m, l)] += swept[r]
                    for q in range(8):
                        grad[1, pl.ds(64 * r + 8 * q, 8), lanes(m, l)] += float(deriv[q, s]) * face[m][r]

        slope = [jnp.where(last, float(deriv[r, 7]), float(deriv[r, 0])) for r in range(8)]
        for l in range(2):
            starts, ends = [], []
            for s in range(8):
                low, high = lines(s + 8 * l, EDGES.index((1, 0)), EDGES.index((-1, 0)), None)
                starts.append(low)
                ends.append(high)
                basis[i, 0, s, :, lanes(0, l)] += low
                basis[i, 7, s, :, lanes(0, l)] += high
                both = low + high
                for r in range(8):
                    grad[0, pl.ds(64 * r + 8 * s, 8), lanes(0, l)] += slope[r] * both
            for r, line in ((0, along(deriv, starts)), (7, along(deriv, ends))):
                for s in range(8):
                    grad[1, pl.ds(64 * r + 8 * s, 8), lanes(0, l)] += line[s]

        pieces = [basis[i, r, :, :, 0:256].reshape(64, 256) for r in (0, 7)]
        pieces += [basis[i, :, 7 * l, :, lanes(m, l)].reshape(64, 128) for l in range(2) for m in range(2)]
        high, low = cut(jnp.concatenate(pieces, 1))
        main, rest = fwd_st[256:320, 0:64], fwd_st[256:320, 256:320]
        value = dot(main, high) + (dot(rest, high) + dot(main, low))
        grad[2, 0:64, 0:256] = value[:, 0:256]
        grad[2, 448:512, 0:256] = value[:, 256:512]
        for l in range(2):
            for m in range(2):
                start = 512 + 256 * l + 128 * m
                for r in range(8):
                    grad[2, pl.ds(64 * r + 56 * l, 8), lanes(m, l)] = value[8 * r : 8 * r + 8, start : start + 128]

    fluid(1)
    pl.semaphore_wait(barrier, len(greet))
    start_ends(0)
    start_middle(0)
    local_axial(0)

    def packed(start, count):
        chosen = (iota((count, 512), 0) + start == position).astype(F32).astype(BF16)
        return dot(cond[...], chosen, NT).astype(BF16)

    def device_at(step):
        number = lax.rem(device + step + devices, devices)
        return (number // n_chan, lax.rem(number, n_chan))

    moves = [
        pltpu.make_async_remote_copy(
            src_ref=put_pack.at[k],
            dst_ref=got_pack.at[k],
            send_sem=pack_send.at[k],
            recv_sem=pack_recv.at[k],
            device_id=device_at(step),
            device_id_type=MESH,
        )
        for k, step in enumerate((n_chan, 1, -1))
    ]
    late = packed(512, 128)
    put_pack[0] = late
    moves[0].start()
    soon = packed(256, 256)
    put_pack[1] = soon[:, :128]
    put_pack[2] = soon[:, 128:]
    moves[1].start()
    moves[2].start()
    own_pack[...] = packed(0, 256)

    def place(block):
        code = block[512:528].astype(F32)
        slot = ((code[0:1] - 1.0) * 32.0 + code[1:2]).astype(jnp.int32)
        lane = iota((512, block.shape[1]), 0)
        here = lane & 127
        axial = here + jnp.where((lane < 256) == (here < 64), 0, 128)
        chosen = (((lane >> 7) & 1) * 256 + axial == slot).astype(F32).astype(BF16)
        return dot(block[0:512], chosen, NT)

    kap[...] = place(own_pack[...])
    node = iota((512, 128), 0)
    at_r = node >> 6
    at_s = (node >> 3) & 7
    for m in range(2):
        for l in range(2):
            here = iota((512, 128), 1)
            axial = slab * 256 + here + jnp.where(here < 64, 128 * m, 128 - 128 * m)
            m_r = jnp.where(((at_r == 0) & (axial > 0)) | ((at_r == 7) & (axial < n_slab * 256 - 1)), 0.5, 1.0)
            lateral = chan * 2 + l
            m_s = jnp.where(((at_s == 0) & (lateral > 0)) | ((at_s == 7) & (lateral < n_chan * 2 - 1)), 0.5, 1.0)
            inv_mult[:, lanes(m, l)] = m_r * m_s


    spare = lax.div(slab, n_slab)

    def gradient(i, block):
        lane = pl.ds(256 * block, 256)
        pairs = [cut(basis[i, 4 * h : 4 * h + 4, :, :, lane].reshape(256, 256)) for h in range(2)]

        def turn(h):
            high, low = pairs[h]
            both = dot(fwd_st[...], jnp.concatenate([high, high, low], 0))
            grad[1, pl.ds(256 * h, 256), lane] = both[:256]
            grad[2, pl.ds(256 * h, 256), lane] = both[256:]
            return both

        basis[ITERS + spare, 0, 0, :, 0:128] = turn(0)[0:8, 0:128]
        for s in range(8):
            for tile in range(2):
                part = pl.ds(256 * block + 128 * tile, 128)
                out = along(deriv, [basis[i, r, s, :, part] for r in range(8)])
                for r in range(8):
                    grad[0, pl.ds(64 * r + 8 * s, 8), part] = out[r]
        turn(1)

    def fold(x):
        total = jnp.sum(x.reshape(x.shape[0] // 8, 8, 256), axis=0)
        return total[:, :128] + total[:, 128:]

    def norm(i):
        totals = [None] * 4
        for n in range(64):
            for tile in range(4):
                part = pl.ds(128 * tile, 128)
                v = basis[i, n // 8, n % 8, :, part]
                term = v * v * inv_mult[pl.ds(8 * n, 8), part]
                totals[tile] = term if n == 0 else totals[tile] + term
        acc[2 * i] = (totals[0] + totals[1]) + (totals[2] + totals[3])

    def power(i, block):
        lane = pl.ds(256 * block, 256)
        mix = mix_ref[0:1, lane]

        def stage(h):
            rows = pl.ds(256 * h, 256)
            k = kap[rows, lane]
            k1 = k * grad[0, rows, lane]
            k2 = k * grad[1, rows, lane]
            flux[0, rows] = k1 + mix * k2
            h2, l2 = cut(k2 + mix * k1)
            h3, l3 = cut(k * grad[2, rows, lane])
            return jnp.concatenate([h2, h3, h2, h3, l2, l3], 0)

        staged = [stage(h) for h in range(2)]
        for h in range(2):
            value = dot(bwd_st[...], staged[h])
            ysum[pl.ds(256 * h, 256), lane] = value
            if h == 0:
                flux[1 + spare, 0:8, 0:128] = value[0:8, 0:128]
                for s in range(8):
                    for tile in range(2):
                        part = pl.ds(128 * tile, 128)
                        out = along(deriv.T, [flux[0, pl.ds(64 * r + 8 * s, 8), part] for r in range(8)])
                        for r in range(8):
                            flux[0, pl.ds(64 * r + 8 * s, 8), part] = out[r]
        total = None
        for h in range(2):
            rows = pl.ds(256 * h, 256)
            field = basis[i, 4 * h : 4 * h + 4, :, :, lane].reshape(256, 256)
            v = volume_ref[rows] * (0.05 / SCALE)
            value = ysum[rows, lane] + flux[0, rows] + jnp.concatenate([v, v], 1) * field
            basis[i + 1, 4 * h : 4 * h + 4, :, :, lane] = value.reshape(4, 8, 8, 256)
            part = fold(value * field)
            total = part if total is None else total + part
        return total

    for load in loads[10:13]:
        load.wait()
    gradient(0, 1)
    gradient(0, 0)
    finish(0)
    moves[1].wait()
    moves[2].wait()
    kap[...] += place(jnp.concatenate([got_pack[1], got_pack[2]], 1))
    moves[0].wait()
    last_part = place(got_pack[0])
    for tile in range(4):
        lane = pl.ds(128 * tile, 128)
        kap[:, lane] = (
            volume_ref[...]
            * (kap[:, lane] + last_part[:, 128 * tile : 128 * tile + 128])
            * damping[tile]
        )

    def body(i, carry):
        ends = power(i, 0)
        start_ends(i + 1)
        acc[2 * i + 1] = ends + power(i, 1)
        start_middle(i + 1)
        local_axial(i + 1)
        norm(i)
        gradient(i + 1, 1)
        gradient(i + 1, 0)
        finish(i + 1)
        return carry

    lax.fori_loop(0, ITERS - 1, body, 0)

    final = ITERS - 1
    norm(final)
    totals = [None] * 4
    twice = [2.0 * mix_ref[:, pl.ds(128 * tile, 128)] for tile in range(4)]
    for n in range(64):
        eight = pl.ds(8 * n, 8)
        v5 = volume_ref[eight, :] * (0.05 / SCALE)
        for tile in range(4):
            part = pl.ds(128 * tile, 128)
            g1, g2, g3 = grad[0, eight, part], grad[1, eight, part], grad[2, eight, part]
            v = basis[final, n // 8, n % 8, :, part]
            term = kap[eight, part] * (g1 * (g1 + twice[tile] * g2) + (g2 * g2 + g3 * g3)) + v5 * (v * v)
            totals[tile] = term if n == 0 else totals[tile] + term
    acc[2 * final + 1] = (totals[0] + totals[1]) + (totals[2] + totals[3])

    rows = [jnp.sum(acc[k], axis=0, keepdims=True) for k in range(2 * ITERS)]
    rows = jnp.concatenate(rows + [jnp.zeros((6, 128), F32)], 0)
    mine = jnp.sum(rows, axis=1, keepdims=True)
    message = jnp.sum(jnp.where(iota((16, 128), 0) == iota((16, 128), 1), mine, 0.0), axis=0, keepdims=True)

    def everyone(message, sums, me, count, sends, recvs, peer):
        sums[me] = message
        copies = [
            pltpu.make_async_remote_copy(
                src_ref=sums.at[me],
                dst_ref=sums.at[me],
                send_sem=sends.at[j],
                recv_sem=recvs.at[j],
                device_id=peer(lax.rem(me + j, count)),
                device_id_type=MESH,
            )
            for j in range(1, count)
        ]
        for copy in copies:
            copy.start()
        for copy in copies:
            copy.wait()
        total = sums[0]
        for j in range(1, count):
            total = total + sums[j]
        return total

    message = everyone(message, chan_sum, chan, n_chan, chan_send, chan_recv, lambda c: (slab, c))
    message = everyone(message, slab_sum, slab, n_slab, slab_send, slab_recv, lambda s: (s, chan))
    lane1 = iota((1, 128), 1)
    moment = [
        jnp.sum(jnp.where(lane1 == k, message, 0.0), axis=1, keepdims=True) for k in range(2 * ITERS)
    ]
    weight = [w * (1.0 / SCALE) for w in krylov_weights(moment)]
    full = [jnp.broadcast_to(w, (8, 128)) for w in weight]
    for r in range(8):
        for s in range(8):
            for l in range(2):
                pieces = []
                for m in range(2):
                    total = full[0] * basis[0, r, s, :, lanes(m, l)]
                    for i in range(1, ITERS):
                        total = total + full[i] * basis[i, r, s, :, lanes(m, l)]
                    pieces.append(total)
                for h, total in enumerate(ends_middle(*pieces)):
                    out_ref[pl.ds(256 * r + 32 * s + 2 * h + l, 8, stride=4), :] = total


def flush_kernel(new_ref, out_ref, new_hbm, out_hbm, sem):
    first = pltpu.make_async_copy(new_ref, new_hbm, sem.at[0])
    second = pltpu.make_async_copy(out_ref, out_hbm, sem.at[1])
    first.start()
    second.start()
    first.wait()
    second.wait()


def step(u, index, prev, source, flags, plies, ops):
    n_slab, n_chan = lax.axis_size("slab"), lax.axis_size("chan")
    anywhere = pl.BlockSpec(memory_space=pl.ANY)
    vmem = pl.BlockSpec(memory_space=pltpu.VMEM)
    dma = pltpu.SemaphoreType.DMA
    new, warmth = pl.pallas_call(
        functools.partial(kernel, n_slab, n_chan),
        in_specs=[anywhere] * 11,
        out_specs=[vmem, vmem],
        out_shape=[
            pltpu.MemorySpace.VMEM((192, 8, 512), BF16),
            pltpu.MemorySpace.VMEM((2048, 128), F32),
        ],
        scratch_shapes=[
            pltpu.VMEM((192, 8, 512), BF16),
            pltpu.VMEM((1, 512), jnp.int32),
            pltpu.VMEM((2048, 128), F32),
            pltpu.VMEM((2048, 128), F32),
            pltpu.VMEM((2, 256), jnp.int32),
            pltpu.VMEM((2, 256), jnp.int32),
            pltpu.VMEM((512, 768), BF16),
            pltpu.VMEM((256, 1536), BF16),
            pltpu.VMEM((256, 256), BF16),
            pltpu.VMEM((512, 256), BF16),
            pltpu.VMEM((512, 128), F32),
            pltpu.VMEM((3, 3, 512, 512), F32),
            pltpu.VMEM((3, 512, 512), F32),
            pltpu.VMEM((528, 512), BF16),
            pltpu.VMEM((528, 256), BF16),
            pltpu.VMEM((3, 528, 128), BF16),
            pltpu.VMEM((3, 528, 128), BF16),
            pltpu.VMEM((ITERS + 1, 8, 8, 8, 512), F32),
            pltpu.VMEM((512, 512), F32),
            pltpu.VMEM((8, 512), F32),
            pltpu.VMEM((512, 512), F32),
            pltpu.VMEM((3, 512, 512), F32),
            pltpu.VMEM((512, 512), F32),
            pltpu.VMEM((2, 512, 256), F32),
            pltpu.VMEM((2 * ITERS, 8, 128), F32),
            pltpu.VMEM((2, 2, 8, 128), F32),
            pltpu.VMEM((2, 6, 8, 128), F32),
            pltpu.VMEM((2, 2, 2, 8, 8, 128), F32),
            pltpu.VMEM((2, 2, 2, 8, 8, 128), F32),
            pltpu.VMEM((n_chan, 1, 128), F32),
            pltpu.VMEM((n_slab, 1, 128), F32),
            dma((14,)),
            dma((3,)),
            dma((3,)),
            dma((2, 10)),
            dma((2, 10)),
            dma((n_chan,)),
            dma((n_chan,)),
            dma((n_slab,)),
            dma((n_slab,)),
        ],
        compiler_params=pltpu.CompilerParams(
            collective_id=0, has_side_effects=True
        ),
        name="step",
    )(
        u,
        index,
        prev,
        source,
        flags,
        plies,
        ops["forward"],
        ops["backward"],
        ops["lap_st"],
        ops["both_r"],
        ops["volume"],
    )
    new, warmth = pl.pallas_call(
        flush_kernel,
        in_specs=[vmem, vmem],
        out_specs=[anywhere, anywhere],
        out_shape=[
            jax.ShapeDtypeStruct((192, 8, 512), BF16),
            jax.ShapeDtypeStruct((2048, 128), F32),
        ],
        scratch_shapes=[dma((2,))],
        name="flush",
    )(
        pltpu.with_memory_space_constraint(new, pltpu.VMEM),
        pltpu.with_memory_space_constraint(warmth, pltpu.VMEM),
    )
    return new, warmth


def lanes_first(x):
    return x.reshape(512, 2, 2, 128).transpose(0, 2, 1, 3).reshape(2048, 128)


def on_device(u, index, prev, source, flags, plies):
    ops = operators()
    stepped, warmth = step(
        u.reshape(192, 8, 512),
        index.reshape(1, 512),
        lanes_first(prev),
        lanes_first(source),
        flags,
        plies,
        ops,
    )
    warmth = warmth.reshape(512, 2, 2, 128).transpose(0, 2, 1, 3).reshape(8, 8, 8, 2, 256)
    return stepped.reshape(3, 8, 8, 8, 512), warmth


def solution(mesh):
    in_specs = (
        P(None, None, None, None, ("slab", "chan")),
        P(("slab", "chan")),
        P(None, None, None, "chan", "slab"),
        P(None, None, None, "chan", "slab"),
        P("chan", "slab"),
        P("chan", "slab"),
    )
    out_specs = (P(None, None, None, None, ("slab", "chan")), P(None, None, None, "chan", "slab"))
    return jax.shard_map(
        on_device, mesh=mesh, in_specs=in_specs, out_specs=out_specs, check_vma=False
    )
```

```python
import functools

import jax
import jax.numpy as jnp
import numpy as np
from jax import lax
from jax.experimental import pallas as pl
from jax.experimental.pallas import tpu as pltpu
from jax.sharding import PartitionSpec as P

F32 = jnp.float32
BF16 = jnp.bfloat16
MESH = pl.DeviceIdType.MESH
ITERS = 5
SCALE = 64.0
NT = (((1,), (1,)), ((), ()))
NN = (((1,), (0,)), ((), ()))


def gll():
    points = np.array(
        [
            -1.0,
            -0.8717401485096066,
            -0.5917001814331423,
            -0.2092992179024789,
            0.2092992179024789,
            0.5917001814331423,
            0.8717401485096066,
            1.0,
        ]
    )
    weights = np.array(
        [
            1.0 / 28.0,
            0.2107042271435061,
            0.3411226924835044,
            0.4124587946587038,
            0.4124587946587038,
            0.3411226924835044,
            0.2107042271435061,
            1.0 / 28.0,
        ]
    )
    low = np.ones(8)
    high = points.copy()
    for degree in range(1, 7):
        low, high = high, ((2 * degree + 1) * points * high - degree * low) / (degree + 1)
    gaps = points[:, None] - points[None, :] + np.eye(8)
    deriv = high[:, None] / (high[None, :] * gaps)
    deriv = deriv * (1.0 - np.eye(8))
    deriv[0, 0] = -14.0
    deriv[7, 7] = 14.0
    return deriv, weights


def two(matrix):
    high = np.asarray(matrix, np.float32).astype(BF16).astype(np.float64)
    return high, matrix - high


def operators():
    deriv, weights = gll()
    second = deriv @ deriv
    eye = np.eye
    kron = np.kron
    along_s = kron(eye(4), kron(deriv, eye(8)))
    along_t = kron(eye(32), deriv)
    along_r = kron(deriv, eye(32))
    ds_hi, ds_lo = two(along_s)
    dt_hi, dt_lo = two(along_t)
    forward = np.block([[ds_hi, ds_lo], [dt_hi, dt_lo]])
    backward = np.block([[ds_hi.T, dt_hi.T, ds_lo.T, dt_lo.T]])
    lap_st = 0.0002 * (kron(eye(4), kron(second, eye(8))) + kron(eye(32), second))
    both_r = np.block([[along_r], [0.0002 * kron(second, eye(32))]])
    volume = (weights[:, None, None] * weights[None, :, None] * weights[None, None, :]).reshape(512, 1)
    cast = lambda m: jnp.asarray(np.asarray(m, np.float32).astype(BF16))
    return {
        "forward": cast(forward),
        "backward": cast(backward),
        "lap_st": cast(lap_st),
        "both_r": cast(both_r),
        "volume": jnp.asarray(np.broadcast_to(volume, (512, 128)), F32),
    }


def dot(a, b, dims=NN):
    return lax.dot_general(a, b, dims, preferred_element_type=F32)


def iota(shape, dim):
    return lax.broadcasted_iota(jnp.int32, shape, dim)


def krylov_weights(m):
    n = ITERS
    zero = jnp.zeros_like(m[0])
    older, newer = [zero] * (2 * n), list(m)
    diag = [newer[1] / newer[0]]
    off = [zero]
    for k in range(1, n):
        fresh = [zero] * (2 * n)
        for l in range(k, 2 * n - k):
            fresh[l] = newer[l + 1] - diag[k - 1] * newer[l] - off[k - 1] * older[l]
        diag.append(fresh[k + 1] / fresh[k] - newer[k] / newer[k - 1])
        off.append(fresh[k] / newer[k - 1])
        older, newer = newer, fresh
    alpha = [1.0 / diag[0]]
    beta = []
    for k in range(1, n):
        beta.append(off[k] * alpha[k - 1] * alpha[k - 1])
        alpha.append(1.0 / (diag[k] - beta[k - 1] / alpha[k - 1]))
    one = jnp.ones_like(zero)
    res, way, sol = [one], [one], [zero] * n
    for k in range(n):
        for i in range(k + 1):
            sol[i] = sol[i] + alpha[k] * way[i]
        if k < n - 1:
            res = res + [zero]
            for i in range(k + 1):
                res[i + 1] = res[i + 1] - alpha[k] * way[i]
            way = [res[i] + (beta[k] * way[i] if i <= k else 0.0) for i in range(k + 2)]
    return sol


EDGES = ((1, 0), (-1, 0), (1, 1), (1, -1), (-1, 1), (-1, -1))
HALO = EDGES + ((0, 1), (0, -1))


def along(matrix, v):
    even = [v[k] + v[7 - k] for k in range(4)]
    odd = [v[k] - v[7 - k] for k in range(4)]
    first, last = [], []
    for i in range(4):
        same = [0.5 * float(matrix[i, k] + matrix[i, 7 - k]) for k in range(4)]
        flip = [0.5 * float(matrix[i, k] - matrix[i, 7 - k]) for k in range(4)]
        p = (same[0] * even[0] + same[1] * even[1]) + (same[2] * even[2] + same[3] * even[3])
        q = (flip[0] * odd[0] + flip[1] * odd[1]) + (flip[2] * odd[2] + flip[3] * odd[3])
        first.append(p + q)
        last.append(q - p)
    return first + last[::-1]


def cut(x):
    high = x.astype(BF16)
    return high, (x - high.astype(F32)).astype(BF16)


def ends_middle(low, high):
    half = iota(low.shape, 1) < 64
    return jnp.where(half, low, high), jnp.where(half, high, low)


def kernel(
    n_slab,
    n_chan,
    u_hbm,
    index_hbm,
    prev_hbm,
    source_hbm,
    flag_hbm,
    ply_hbm,
    forward_hbm,
    backward_hbm,
    lap_hbm,
    both_hbm,
    volume_hbm,
    new_ref,
    out_ref,
    u_ref,
    index_ref,
    prev_ref,
    source_ref,
    flag_ref,
    ply_ref,
    fwd_st,
    bwd_st,
    lap_st,
    both_r,
    volume_ref,
    speed_grad,
    lap,
    cond,
    own_pack,
    put_pack,
    got_pack,
    basis,
    kap,
    mix_ref,
    inv_mult,
    grad,
    ysum,
    flux,
    acc,
    edge_out,
    edge_in,
    side_out,
    side_in,
    chan_sum,
    slab_sum,
    load_sem,
    pack_send,
    pack_recv,
    halo_send,
    halo_recv,
    chan_send,
    chan_recv,
    slab_send,
    slab_recv,
):
    slab = lax.axis_index("slab")
    chan = lax.axis_index("chan")
    device = slab * n_chan + chan
    devices = n_slab * n_chan

    def near(ds, dc):
        return (lax.rem(slab + ds + n_slab, n_slab), lax.rem(chan + dc + n_chan, n_chan))

    left, right = pl.ds(0, 256), pl.ds(256, 256)
    loads = [
        pltpu.make_async_copy(src, dst, load_sem.at[k])
        for k, (src, dst) in enumerate(
            (
                (prev_hbm, prev_ref),
                (source_hbm, source_ref),
                (volume_hbm, volume_ref),
                (flag_hbm, flag_ref),
                (ply_hbm, ply_ref),
                (u_hbm.at[:, :, left], u_ref.at[:, :, left]),
                (lap_hbm, lap_st),
                (both_hbm, both_r),
                (forward_hbm, fwd_st.at[:, pl.ds(0, 512)]),
                (u_hbm.at[:, :, right], u_ref.at[:, :, right]),
                (forward_hbm.at[:, pl.ds(0, 256)], fwd_st.at[:, pl.ds(512, 256)]),
                (backward_hbm, bwd_st.at[:, pl.ds(0, 1024)]),
                (backward_hbm.at[:, pl.ds(0, 512)], bwd_st.at[:, pl.ds(1024, 512)]),
                (index_hbm, index_ref),
            )
        )
    ]
    loads[13].start()
    for load in loads[5:10] + loads[:5] + loads[10:13]:
        load.start()

    barrier = pltpu.get_barrier_semaphore()
    greet = [near(*d) for d in HALO]
    greet += [(slab, lax.rem(chan + j, n_chan)) for j in range(2, n_chan - 1)]
    greet += [(lax.rem(slab + j, n_slab), chan) for j in range(2, n_slab - 1)]
    for peer in greet:
        pl.semaphore_signal(barrier, inc=1, device_id=peer, device_id_type=MESH)

    loads[13].wait()
    target = index_ref[...]
    slot = target & 511
    distance = ((target >> 9) - device) & (devices - 1)
    group = jnp.where(
        distance == 1,
        1,
        jnp.where(distance == devices - 1, 2, jnp.where(distance == n_chan, 3, 0)),
    )
    member = iota((8, 512), 0) == group
    before = (iota((512, 512), 0) < iota((512, 512), 1)).astype(F32).astype(BF16)
    rank = dot(member.astype(F32).astype(BF16), before)
    begin = jnp.where(iota((8, 512), 0) == 0, 0, 128 + 128 * iota((8, 512), 0)).astype(F32)
    position = jnp.sum(jnp.where(member, rank + begin, 0.0), axis=0, keepdims=True).astype(jnp.int32)
    code = jnp.where(
        iota((16, 512), 0) == 0,
        (slot >> 5) + 1,
        jnp.where(iota((16, 512), 0) == 1, slot & 31, 0),
    )
    cond[512:528] = code.astype(F32).astype(BF16)

    def fluid(block):
        lane = pl.ds(256 * block, 256)
        for c in range(3):
            flat = u_ref[pl.ds(64 * c, 64), :, lane].astype(F32).reshape(512, 256)
            low = flat.astype(BF16)
            for h in range(2):
                rows = pl.ds(256 * h, 256)
                part = low[256 * h : 256 * h + 256]
                both = dot(fwd_st[:, 0:256], part)
                speed_grad[c, 1, rows, lane] = both[:256]
                speed_grad[c, 2, rows, lane] = both[256:]
                lap[c, rows, lane] = dot(lap_st[...], part)
            by_r = flat.reshape(8, 64, 256)
            for q in range(2):
                part = by_r[:, 32 * q : 32 * q + 32].reshape(256, 256).astype(BF16)
                both = dot(both_r[...], part).reshape(16, 32, 256)
                for r in range(8):
                    rows = pl.ds(64 * r + 32 * q, 32)
                    speed_grad[c, 0, rows, lane] = both[r]
                    lap[c, rows, lane] += both[8 + r]
            for n in range(32):
                for tile in range(2):
                    part = pl.ds(256 * block + 128 * tile, 128)
                    rows = pl.ds(16 * n, 16)
                    u = [u_ref[pl.ds(64 * k + 2 * n, 2), :, part].astype(F32).reshape(16, 128) for k in range(3)]
                    turn = (
                        u[0] * speed_grad[c, 0, rows, part]
                        + u[1] * speed_grad[c, 1, rows, part]
                        + u[2] * speed_grad[c, 2, rows, part]
                    )
                    new = ((u[c] + lap[c, rows, part]) - 0.01 * turn).astype(BF16).astype(F32)
                    new_ref[pl.ds(64 * c + 2 * n, 2), :, part] = new.reshape(2, 8, 128).astype(BF16)
                    square = new * new if c == 0 else ysum[rows, part] + new * new
                    if c < 2:
                        ysum[rows, part] = square
                    else:
                        cond[rows, part] = (1.0 + 0.5 * square).astype(BF16)

    for load in loads[5:10]:
        load.wait()
    fluid(0)

    lane8 = iota((8, 128), 1)
    has_left = slab > 0
    has_right = slab < n_slab - 1
    has_under = chan > 0
    has_over = chan < n_chan - 1
    has_next = {(1, 0): has_right, (-1, 0): has_left, (0, 1): has_over, (0, -1): has_under}

    def both_of(ds, dc):
        if ds == 0 or dc == 0:
            return has_next[ds, dc]
        return has_next[ds, 0] & has_next[0, dc]

    SIDES = ((0, 1, 0), (0, -1, 0), (0, 1, 1), (0, -1, 1))

    def halo_copies(i, want_edges, want_sides):
        turn = i % 2 if isinstance(i, int) else lax.rem(i, 2)

        def remote(src, dst, number, ds, dc):
            return pltpu.make_async_remote_copy(
                src_ref=src,
                dst_ref=dst,
                send_sem=halo_send.at[turn, number],
                recv_sem=halo_recv.at[turn, number],
                device_id=near(ds, dc),
                device_id_type=MESH,
            )

        edges = [
            (ds, dc, remote(edge_out.at[turn, 0 if ds == 1 else 1], edge_in.at[turn, d], d, ds, dc))
            for d, (ds, dc) in enumerate(EDGES)
            if want_edges
        ]
        sides = []
        for d, (ds, dc, m) in enumerate(SIDES):
            if m not in want_sides:
                continue
            k = 0 if dc == 1 else 1
            sides.append((ds, dc, remote(side_out.at[turn, k, m], side_in.at[turn, k, m], 6 + d, ds, dc)))
        return turn, edges, sides

    def send(copies):
        for ds, dc, copy in copies:
            pl.when(both_of(ds, dc))(copy.start)

    def arrive(copies):
        for ds, dc, copy in copies:
            pl.when(both_of(ds, dc))(copy.wait_send)
            pl.when(both_of(-ds, -dc))(copy.wait_recv)

    def lanes(m, l):
        return pl.ds(256 * m + 128 * l, 128)

    def between(i, m, turn):
        side_out[turn, 0, m] = basis[i, :, 7, :, lanes(m, 1)]
        side_out[turn, 1, m] = basis[i, :, 0, :, lanes(m, 0)]
        both = basis[i, :, 7, :, lanes(m, 0)] + basis[i, :, 0, :, lanes(m, 1)]
        basis[i, :, 7, :, lanes(m, 0)] = both
        basis[i, :, 0, :, lanes(m, 1)] = both

    def start_ends(i):
        turn, edges, sides = halo_copies(i, True, (0,))
        between(i, 0, turn)
        up = jnp.zeros((8, 128), F32)
        down = jnp.zeros((8, 128), F32)
        for l in range(2):
            for s in range(8):
                to = s + 8 * l
                here = lane8 == to
                up = jnp.where(here, pltpu.roll(basis[i, 7, s, :, lanes(0, l)], (to - 127) % 128, 1), up)
                down = jnp.where(here, pltpu.roll(basis[i, 0, s, :, lanes(0, l)], to, 1), down)
        edge_out[turn, 0] = up
        edge_out[turn, 1] = down
        send(edges)
        send(sides)

    def start_middle(i):
        turn, edges, sides = halo_copies(i, False, (1,))
        between(i, 1, turn)
        send(sides)

    def local_axial(i):
        j = iota((64, 128), 1)
        for l in range(2):
            high = [basis[i, 7, :, :, lanes(m, l)].reshape(64, 128) for m in range(2)]
            low = [basis[i, 0, :, :, lanes(m, l)].reshape(64, 128) for m in range(2)]
            ahead = [pltpu.roll(x, 127, 1) for x in low]
            behind = [pltpu.roll(x, 1, 1) for x in high]
            for m in range(2):
                more = jnp.where(j == 63, ahead[1 - m], ahead[m])
                less = jnp.where(j == 64, behind[1 - m], behind[m])
                if m == 0:
                    more = jnp.where(j == 127, 0.0, more)
                    less = jnp.where(j == 0, 0.0, less)
                basis[i, 7, :, :, lanes(m, l)] = (high[m] + more).reshape(8, 8, 128)
                basis[i, 0, :, :, lanes(m, l)] = (low[m] + less).reshape(8, 8, 128)

    deriv = gll()[0]

    def finish(i):
        turn, edges, sides = halo_copies(i, True, (0, 1))
        arrive(sides)
        arrive(edges)
        first = lane8 == 0
        last = lane8 == 127

        def lines(at, slot_left, slot_right, has):
            left_ok = has_left if has is None else has_left & has
            right_ok = has_right if has is None else has_right & has
            return (
                jnp.where(first & left_ok, pltpu.roll(edge_in[turn, slot_left], (128 - at) % 128, 1), 0.0),
                jnp.where(last & right_ok, pltpu.roll(edge_in[turn, slot_right], (127 - at) % 128, 1), 0.0),
            )

        for k, (has, s, l, at, dc) in enumerate(((has_under, 0, 0, 15, 1), (has_over, 7, 1, 0, -1))):
            face = [[jnp.where(has, side_in[turn, k, m, r], 0.0) for r in range(8)] for m in range(2)]
            ahead = [pltpu.roll(face[m][0], 127, 1) for m in range(2)]
            behind = [pltpu.roll(face[m][7], 1, 1) for m in range(2)]
            low, high = lines(at, EDGES.index((1, dc)), EDGES.index((-1, dc)), has)
            for m in range(2):
                more = jnp.where(lane8 == 63, ahead[1 - m], ahead[m])
                less = jnp.where(lane8 == 64, behind[1 - m], behind[m])
                if m == 0:
                    more = jnp.where(last, high, more)
                    less = jnp.where(first, low, less)
                face[m][7] = face[m][7] + more
                face[m][0] = face[m][0] + less
            for m in range(2):
                swept = along(deriv, face[m])
                for r in range(8):
                    basis[i, r, s, :, lanes(m, l)] += face[m][r]
                    grad[0, pl.ds(64 * r + 8 * s, 8), lanes(m, l)] += swept[r]
                    for q in range(8):
                        grad[1, pl.ds(64 * r + 8 * q, 8), lanes(m, l)] += float(deriv[q, s]) * face[m][r]

        slope = [jnp.where(last, float(deriv[r, 7]), float(deriv[r, 0])) for r in range(8)]
        for l in range(2):
            starts, ends = [], []
            for s in range(8):
                low, high = lines(s + 8 * l, EDGES.index((1, 0)), EDGES.index((-1, 0)), None)
                starts.append(low)
                ends.append(high)
                basis[i, 0, s, :, lanes(0, l)] += low
                basis[i, 7, s, :, lanes(0, l)] += high
                both = low + high
                for r in range(8):
                    grad[0, pl.ds(64 * r + 8 * s, 8), lanes(0, l)] += slope[r] * both
            for r, line in ((0, along(deriv, starts)), (7, along(deriv, ends))):
                for s in range(8):
                    grad[1, pl.ds(64 * r + 8 * s, 8), lanes(0, l)] += line[s]

        pieces = [basis[i, r, :, :, 0:256].reshape(64, 256) for r in (0, 7)]
        pieces += [basis[i, :, 7 * l, :, lanes(m, l)].reshape(64, 128) for l in range(2) for m in range(2)]
        high, low = cut(jnp.concatenate(pieces, 1))
        main, rest = fwd_st[256:320, 0:64], fwd_st[256:320, 256:320]
        value = dot(main, high) + (dot(rest, high) + dot(main, low))
        grad[2, 0:64, 0:256] = value[:, 0:256]
        grad[2, 448:512, 0:256] = value[:, 256:512]
        for l in range(2):
            for m in range(2):
                start = 512 + 256 * l + 128 * m
                for r in range(8):
                    grad[2, pl.ds(64 * r + 56 * l, 8), lanes(m, l)] = value[8 * r : 8 * r + 8, start : start + 128]

    fluid(1)

    for load in loads[:5]:
        load.wait()
    for l in range(2):
        halves = []
        for h in range(2):
            rows = pl.ds(2 * h + l, 512, stride=4)
            halves.append(volume_ref[...] * (0.05 * prev_ref[rows, :] + source_ref[rows, :]))
        for m, value in enumerate(ends_middle(*halves)):
            basis[0, :, :, :, pl.ds(256 * m + 128 * l, 128)] = value.reshape(8, 8, 8, 128)
    damping = []
    mixing = []
    for l in range(2):
        flag = flag_ref[pl.ds(l, 1)]
        ply = ply_ref[pl.ds(l, 1)].astype(F32)
        damp = jnp.where(flag == 1, 1.0 / (1.0 + 0.25 * ply), 1.0) * (1.0 / SCALE)
        mix = 0.4 * flag.astype(F32) * ply / (ply + 1.0)
        wide = [jnp.broadcast_to(x, (8, 256)) for x in (damp, mix)]
        damping.append(ends_middle(wide[0][:, :128], wide[0][:, 128:]))
        mixing.append(ends_middle(wide[1][:, :128], wide[1][:, 128:]))
    damping = [damping[l][m][0:1] for m in range(2) for l in range(2)]
    mixing = [mixing[l][m] for m in range(2) for l in range(2)]
    for tile in range(4):
        mix_ref[:, pl.ds(128 * tile, 128)] = mixing[tile]

    pl.semaphore_wait(barrier, len(greet))
    start_ends(0)
    start_middle(0)
    local_axial(0)

    def packed(start, count):
        chosen = (iota((count, 512), 0) + start == position).astype(F32).astype(BF16)
        return dot(cond[...], chosen, NT).astype(BF16)

    def device_at(step):
        number = lax.rem(device + step + devices, devices)
        return (number // n_chan, lax.rem(number, n_chan))

    moves = [
        pltpu.make_async_remote_copy(
            src_ref=put_pack.at[k],
            dst_ref=got_pack.at[k],
            send_sem=pack_send.at[k],
            recv_sem=pack_recv.at[k],
            device_id=device_at(step),
            device_id_type=MESH,
        )
        for k, step in enumerate((n_chan, 1, -1))
    ]
    late = packed(512, 128)
    put_pack[0] = late
    moves[0].start()
    soon = packed(256, 256)
    put_pack[1] = soon[:, :128]
    put_pack[2] = soon[:, 128:]
    moves[1].start()
    moves[2].start()
    own_pack[...] = packed(0, 256)

    def place(block):
        code = block[512:528].astype(F32)
        slot = ((code[0:1] - 1.0) * 32.0 + code[1:2]).astype(jnp.int32)
        lane = iota((512, block.shape[1]), 0)
        here = lane & 127
        axial = here + jnp.where((lane < 256) == (here < 64), 0, 128)
        chosen = (((lane >> 7) & 1) * 256 + axial == slot).astype(F32).astype(BF16)
        return dot(block[0:512], chosen, NT)

    kap[...] = place(own_pack[...])
    node = iota((512, 128), 0)
    at_r = node >> 6
    at_s = (node >> 3) & 7
    for m in range(2):
        for l in range(2):
            here = iota((512, 128), 1)
            axial = slab * 256 + here + jnp.where(here < 64, 128 * m, 128 - 128 * m)
            m_r = jnp.where(((at_r == 0) & (axial > 0)) | ((at_r == 7) & (axial < n_slab * 256 - 1)), 0.5, 1.0)
            lateral = chan * 2 + l
            m_s = jnp.where(((at_s == 0) & (lateral > 0)) | ((at_s == 7) & (lateral < n_chan * 2 - 1)), 0.5, 1.0)
            inv_mult[:, lanes(m, l)] = m_r * m_s


    spare = lax.div(slab, n_slab)

    def gradient(i, block):
        lane = pl.ds(256 * block, 256)
        pairs = [cut(basis[i, 4 * h : 4 * h + 4, :, :, lane].reshape(256, 256)) for h in range(2)]

        def turn(h):
            high, low = pairs[h]
            both = dot(fwd_st[...], jnp.concatenate([high, high, low], 0))
            grad[1, pl.ds(256 * h, 256), lane] = both[:256]
            grad[2, pl.ds(256 * h, 256), lane] = both[256:]
            return both

        basis[ITERS + spare, 0, 0, :, 0:128] = turn(0)[0:8, 0:128]
        for s in range(8):
            for tile in range(2):
                part = pl.ds(256 * block + 128 * tile, 128)
                out = along(deriv, [basis[i, r, s, :, part] for r in range(8)])
                for r in range(8):
                    grad[0, pl.ds(64 * r + 8 * s, 8), part] = out[r]
        turn(1)

    def fold(x):
        total = jnp.sum(x.reshape(x.shape[0] // 8, 8, 256), axis=0)
        return total[:, :128] + total[:, 128:]

    def norm(i):
        totals = [None] * 4
        for n in range(64):
            for tile in range(4):
                part = pl.ds(128 * tile, 128)
                v = basis[i, n // 8, n % 8, :, part]
                term = v * v * inv_mult[pl.ds(8 * n, 8), part]
                totals[tile] = term if n == 0 else totals[tile] + term
        acc[2 * i] = (totals[0] + totals[1]) + (totals[2] + totals[3])

    def power(i, block):
        lane = pl.ds(256 * block, 256)
        mix = mix_ref[0:1, lane]

        def stage(h):
            rows = pl.ds(256 * h, 256)
            k = kap[rows, lane]
            k1 = k * grad[0, rows, lane]
            k2 = k * grad[1, rows, lane]
            flux[0, rows] = k1 + mix * k2
            h2, l2 = cut(k2 + mix * k1)
            h3, l3 = cut(k * grad[2, rows, lane])
            return jnp.concatenate([h2, h3, h2, h3, l2, l3], 0)

        staged = [stage(h) for h in range(2)]
        for h in range(2):
            value = dot(bwd_st[...], staged[h])
            ysum[pl.ds(256 * h, 256), lane] = value
            if h == 0:
                flux[1 + spare, 0:8, 0:128] = value[0:8, 0:128]
                for s in range(8):
                    for tile in range(2):
                        part = pl.ds(128 * tile, 128)
                        out = along(deriv.T, [flux[0, pl.ds(64 * r + 8 * s, 8), part] for r in range(8)])
                        for r in range(8):
                            flux[0, pl.ds(64 * r + 8 * s, 8), part] = out[r]
        total = None
        for h in range(2):
            rows = pl.ds(256 * h, 256)
            field = basis[i, 4 * h : 4 * h + 4, :, :, lane].reshape(256, 256)
            v = volume_ref[rows] * (0.05 / SCALE)
            value = ysum[rows, lane] + flux[0, rows] + jnp.concatenate([v, v], 1) * field
            basis[i + 1, 4 * h : 4 * h + 4, :, :, lane] = value.reshape(4, 8, 8, 256)
            part = fold(value * field)
            total = part if total is None else total + part
        return total

    for load in loads[10:13]:
        load.wait()
    gradient(0, 1)
    gradient(0, 0)
    finish(0)
    moves[1].wait()
    moves[2].wait()
    kap[...] += place(jnp.concatenate([got_pack[1], got_pack[2]], 1))
    moves[0].wait()
    last_part = place(got_pack[0])
    for tile in range(4):
        lane = pl.ds(128 * tile, 128)
        kap[:, lane] = (
            volume_ref[...]
            * (kap[:, lane] + last_part[:, 128 * tile : 128 * tile + 128])
            * damping[tile]
        )

    def body(i, carry):
        ends = power(i, 0)
        start_ends(i + 1)
        acc[2 * i + 1] = ends + power(i, 1)
        start_middle(i + 1)
        local_axial(i + 1)
        norm(i)
        gradient(i + 1, 1)
        gradient(i + 1, 0)
        finish(i + 1)
        return carry

    lax.fori_loop(0, ITERS - 1, body, 0)

    final = ITERS - 1
    norm(final)
    totals = [None] * 4
    twice = [2.0 * mix_ref[:, pl.ds(128 * tile, 128)] for tile in range(4)]
    for n in range(64):
        eight = pl.ds(8 * n, 8)
        v5 = volume_ref[eight, :] * (0.05 / SCALE)
        for tile in range(4):
            part = pl.ds(128 * tile, 128)
            g1, g2, g3 = grad[0, eight, part], grad[1, eight, part], grad[2, eight, part]
            v = basis[final, n // 8, n % 8, :, part]
            term = kap[eight, part] * (g1 * (g1 + twice[tile] * g2) + (g2 * g2 + g3 * g3)) + v5 * (v * v)
            totals[tile] = term if n == 0 else totals[tile] + term
    acc[2 * final + 1] = (totals[0] + totals[1]) + (totals[2] + totals[3])

    rows = [jnp.sum(acc[k], axis=0, keepdims=True) for k in range(2 * ITERS)]
    rows = jnp.concatenate(rows + [jnp.zeros((6, 128), F32)], 0)
    mine = jnp.sum(rows, axis=1, keepdims=True)
    message = jnp.sum(jnp.where(iota((16, 128), 0) == iota((16, 128), 1), mine, 0.0), axis=0, keepdims=True)

    def everyone(message, sums, me, count, sends, recvs, peer):
        sums[me] = message
        copies = [
            pltpu.make_async_remote_copy(
                src_ref=sums.at[me],
                dst_ref=sums.at[me],
                send_sem=sends.at[j],
                recv_sem=recvs.at[j],
                device_id=peer(lax.rem(me + j, count)),
                device_id_type=MESH,
            )
            for j in range(1, count)
        ]
        for copy in copies:
            copy.start()
        for copy in copies:
            copy.wait()
        total = sums[0]
        for j in range(1, count):
            total = total + sums[j]
        return total

    message = everyone(message, chan_sum, chan, n_chan, chan_send, chan_recv, lambda c: (slab, c))
    message = everyone(message, slab_sum, slab, n_slab, slab_send, slab_recv, lambda s: (s, chan))
    lane1 = iota((1, 128), 1)
    moment = [
        jnp.sum(jnp.where(lane1 == k, message, 0.0), axis=1, keepdims=True) for k in range(2 * ITERS)
    ]
    weight = [w * (1.0 / SCALE) for w in krylov_weights(moment)]
    full = [jnp.broadcast_to(w, (8, 128)) for w in weight]
    for r in range(8):
        for s in range(8):
            for l in range(2):
                pieces = []
                for m in range(2):
                    total = full[0] * basis[0, r, s, :, lanes(m, l)]
                    for i in range(1, ITERS):
                        total = total + full[i] * basis[i, r, s, :, lanes(m, l)]
                    pieces.append(total)
                for h, total in enumerate(ends_middle(*pieces)):
                    out_ref[pl.ds(256 * r + 32 * s + 2 * h + l, 8, stride=4), :] = total


def flush_kernel(new_ref, out_ref, new_hbm, out_hbm, sem):
    first = pltpu.make_async_copy(new_ref, new_hbm, sem.at[0])
    second = pltpu.make_async_copy(out_ref, out_hbm, sem.at[1])
    first.start()
    second.start()
    first.wait()
    second.wait()


def step(u, index, prev, source, flags, plies, ops):
    n_slab, n_chan = lax.axis_size("slab"), lax.axis_size("chan")
    anywhere = pl.BlockSpec(memory_space=pl.ANY)
    vmem = pl.BlockSpec(memory_space=pltpu.VMEM)
    dma = pltpu.SemaphoreType.DMA
    new, warmth = pl.pallas_call(
        functools.partial(kernel, n_slab, n_chan),
        in_specs=[anywhere] * 11,
        out_specs=[vmem, vmem],
        out_shape=[
            pltpu.MemorySpace.VMEM((192, 8, 512), BF16),
            pltpu.MemorySpace.VMEM((2048, 128), F32),
        ],
        scratch_shapes=[
            pltpu.VMEM((192, 8, 512), BF16),
            pltpu.VMEM((1, 512), jnp.int32),
            pltpu.VMEM((2048, 128), F32),
            pltpu.VMEM((2048, 128), F32),
            pltpu.VMEM((2, 256), jnp.int32),
            pltpu.VMEM((2, 256), jnp.int32),
            pltpu.VMEM((512, 768), BF16),
            pltpu.VMEM((256, 1536), BF16),
            pltpu.VMEM((256, 256), BF16),
            pltpu.VMEM((512, 256), BF16),
            pltpu.VMEM((512, 128), F32),
            pltpu.VMEM((3, 3, 512, 512), F32),
            pltpu.VMEM((3, 512, 512), F32),
            pltpu.VMEM((528, 512), BF16),
            pltpu.VMEM((528, 256), BF16),
            pltpu.VMEM((3, 528, 128), BF16),
            pltpu.VMEM((3, 528, 128), BF16),
            pltpu.VMEM((ITERS + 1, 8, 8, 8, 512), F32),
            pltpu.VMEM((512, 512), F32),
            pltpu.VMEM((8, 512), F32),
            pltpu.VMEM((512, 512), F32),
            pltpu.VMEM((3, 512, 512), F32),
            pltpu.VMEM((512, 512), F32),
            pltpu.VMEM((2, 512, 256), F32),
            pltpu.VMEM((2 * ITERS, 8, 128), F32),
            pltpu.VMEM((2, 2, 8, 128), F32),
            pltpu.VMEM((2, 6, 8, 128), F32),
            pltpu.VMEM((2, 2, 2, 8, 8, 128), F32),
            pltpu.VMEM((2, 2, 2, 8, 8, 128), F32),
            pltpu.VMEM((n_chan, 1, 128), F32),
            pltpu.VMEM((n_slab, 1, 128), F32),
            dma((14,)),
            dma((3,)),
            dma((3,)),
            dma((2, 10)),
            dma((2, 10)),
            dma((n_chan,)),
            dma((n_chan,)),
            dma((n_slab,)),
            dma((n_slab,)),
        ],
        compiler_params=pltpu.CompilerParams(
            collective_id=0, has_side_effects=True
        ),
        name="step",
    )(
        u,
        index,
        prev,
        source,
        flags,
        plies,
        ops["forward"],
        ops["backward"],
        ops["lap_st"],
        ops["both_r"],
        ops["volume"],
    )
    new, warmth = pl.pallas_call(
        flush_kernel,
        in_specs=[vmem, vmem],
        out_specs=[anywhere, anywhere],
        out_shape=[
            jax.ShapeDtypeStruct((192, 8, 512), BF16),
            jax.ShapeDtypeStruct((2048, 128), F32),
        ],
        scratch_shapes=[dma((2,))],
        name="flush",
    )(
        pltpu.with_memory_space_constraint(new, pltpu.VMEM),
        pltpu.with_memory_space_constraint(warmth, pltpu.VMEM),
    )
    return new, warmth


def lanes_first(x):
    return x.reshape(512, 2, 2, 128).transpose(0, 2, 1, 3).reshape(2048, 128)


def on_device(u, index, prev, source, flags, plies):
    ops = operators()
    stepped, warmth = step(
        u.reshape(192, 8, 512),
        index.reshape(1, 512),
        lanes_first(prev),
        lanes_first(source),
        flags,
        plies,
        ops,
    )
    warmth = warmth.reshape(512, 2, 2, 128).transpose(0, 2, 1, 3).reshape(8, 8, 8, 2, 256)
    return stepped.reshape(3, 8, 8, 8, 512), warmth


def solution(mesh):
    in_specs = (
        P(None, None, None, None, ("slab", "chan")),
        P(("slab", "chan")),
        P(None, None, None, "chan", "slab"),
        P(None, None, None, "chan", "slab"),
        P("chan", "slab"),
        P("chan", "slab"),
    )
    out_specs = (P(None, None, None, None, ("slab", "chan")), P(None, None, None, "chan", "slab"))
    return jax.shard_map(
        on_device, mesh=mesh, in_specs=in_specs, out_specs=out_specs, check_vma=False
    )
```
